32 devices in a mesh: sector: 4 (over y, x), bin: 8 (over z, core).
Axes of the slice: x: 2, y: 2, z: 4, core: 2. Of those that a mesh axis runs over, the one named last changes fastest.
Arguments:
- sph_state: float32 [7, 32768], P(None, ('sector', 'bin')), as said below
- sph_dest: int32 [32768, 1], P(('sector', 'bin')), may hold values from 0 to 31; in each aligned block of 1024 rows (0 to 1023, 1024 to 2047, ...) at most 64 rows name the same one
- body_list: int32 [32, 2], P(('sector', 'bin')), may hold values from 0 to 3, all different within a row
- tile_codes: int32 [32, 2, 32], P(('sector', 'bin')), may hold values from 0 to 511, as said below
- triangles: float32 [9, 4, 32768], P(None, 'sector', 'bin'), as said below
Outputs:
- new_state: float32 [7, 65536], P(None, ('sector', 'bin'))
- body_kick: float32 [4, 6], P('sector')
The draws below stay inside these ranges and needn't reach their ends.
Inputs may be any that keep to these rules, and one draw needn't show every extreme that they name: `sph_dest`: within the spheres of one source bin no destination is named by more than 64 spheres, a bound that some block reaches. `body_list`: the 2 bodies of one bin are different. `tile_codes`: the 32 codes of one bin and intersection entry are different. `sph_state`: every radius (row 6) lies between 0.3 and 0.7. `triangles`: for every triangle, |e1 x e2|^2 is at least 0.2.
All inputs are finite; a program needn't handle non-finite values.
Results may differ from the reference program's by a relative error of at most 0.0003.
Values sent between devices are 32-bit elements; how exact they have to be, the bound alone decides.
No kernel may reach another device: no remote copies, remote signals or barrier semaphores. Data moves between devices by JAX's collectives and lax.ppermute only.
A program may use at most 64 MiB of HBM per device.

```python
import math
import jax
import jax.numpy as jnp
import numpy as np
from jax import lax

SPH_DEV = 1024
TBLK = 4096
NPO = 32
OVL = 2
BODIES = 4
DEVROWS = 32
CAP = 64
SPHERES = 32768
SLOTS = 65536
NBTRI = 32768
STILES = 16
TTILES = 32
N_SECTOR = 4
N_BIN = 8


def draw_sph_state(key, part):
    key = jax.random.fold_in(key, 101)
    key_position, key_velocity, key_radius = jax.random.split(key, 3)
    extent = 9.0
    position = jax.random.uniform(key_position, (3, SPHERES), jnp.float32, 0.0, extent)
    velocity = jnp.clip(jax.random.normal(key_velocity, (3, SPHERES), jnp.float32), -6.0, 6.0)
    radius = jax.random.uniform(key_radius, (1, SPHERES), jnp.float32, 0.3, 0.7)
    return jnp.concatenate([position, velocity, radius], 0).astype(jnp.float32)


def draw_triangles(key, part):
    key = jax.random.fold_in(key, 202)
    key_corner, key_first, key_second = jax.random.split(key, 3)
    extent = 9.0
    grid_shape = (3, BODIES, NBTRI)
    corner = jax.random.uniform(key_corner, grid_shape, jnp.float32, 0.0, extent)
    long_low, long_high, side_span = (0.8, 1.6, 0.4)
    first_unit = jax.random.uniform(key_first, grid_shape, jnp.float32, 0.0, 1.0)
    second_unit = jax.random.uniform(key_second, grid_shape, jnp.float32, 0.0, 1.0)
    first_low = jnp.array([long_low, -side_span, -side_span], jnp.float32)[:, None, None]
    first_high = jnp.array([long_high, side_span, side_span], jnp.float32)[:, None, None]
    second_low = jnp.array([-side_span, long_low, -side_span], jnp.float32)[:, None, None]
    second_high = jnp.array([side_span, long_high, side_span], jnp.float32)[:, None, None]
    edge_one = first_low + (first_high - first_low) * first_unit
    edge_two = second_low + (second_high - second_low) * second_unit
    return jnp.concatenate([corner, corner + edge_one, corner + edge_two], 0).astype(jnp.float32)


def draw_tile_codes(key, part):
    key = jax.random.fold_in(key, 303)
    key_list = jax.random.split(key, DEVROWS * OVL)
    choices_all = jax.vmap(lambda single: jax.random.permutation(single, STILES * TTILES)[:NPO])(key_list)
    return choices_all.reshape(DEVROWS, OVL, NPO).astype(jnp.int32)


def choose_distinct(rng, rows, number_of, top, lift):
    order = jax.random.permutation(jax.random.fold_in(rng, 1), number_of)
    favour = order
    for power in range(3):
        favour = favour * favour // number_of
    favour = favour * lift // number_of
    chance = jax.random.randint(jax.random.fold_in(rng, 2), (rows, number_of), 0, 4096) + favour
    holders = jax.random.permutation(jax.random.fold_in(rng, 3), rows)[jnp.arange(number_of) % rows]
    chance = jnp.where(jnp.arange(rows)[:, None] == holders[None, :], 1 << 14, chance)
    score = chance * number_of + jnp.arange(number_of)
    return lax.top_k(score.astype(jnp.int32), top)[1].astype(jnp.int32)


def assign_block(own_key, own, number, rows, number_of, top, limit, lean):
    sequence = jax.random.permutation(own_key, number_of)
    heavy_load, common = load_shares(number_of, rows * top, limit, lean, True), load_shares(number_of, rows * top, limit, lean, False)
    places = jnp.arange(number_of)

    def named(tallies, offset_by):
        used = int((tallies > 0).sum())
        fixed = max(1, used // 4)
        passed = fixed + (places - fixed + offset_by * (used - fixed)) % max(1, number_of - fixed)
        return jnp.zeros((number_of,), jnp.int32).at[sequence[jnp.where(places < fixed, places, passed)]].set(jnp.asarray(tallies, jnp.int32))

    tallies = jnp.where(number % 4 == 0, named(heavy_load, number // 4), named(common, number - number // 4 - 1))
    mixed = jax.random.permutation(jax.random.fold_in(own, 3), number_of)
    source_of, receiver = mixed[0:number_of // 2 * 2:2], mixed[1:number_of // 2 * 2:2]
    margin = jnp.minimum(tallies[source_of] - 1, limit - tallies[receiver]) // 2
    margin = jnp.where((source_of == sequence[0]) | (receiver == sequence[0]) | (tallies[receiver] == 0), 0, jnp.maximum(margin, 0))
    passed = jax.random.randint(jax.random.fold_in(own, 4), (number_of // 2,), 0, 1 << 20) % (margin + 1)
    tallies = tallies.at[source_of].add(-passed).at[receiver].add(passed)
    members = jnp.searchsorted(jnp.cumsum(tallies), jnp.arange(rows * top), side="right").astype(jnp.int32)
    listing = members.reshape(top, rows).T
    listing = listing[jax.random.permutation(jax.random.fold_in(own, 1), rows)]
    offset_by = jax.random.randint(jax.random.fold_in(own, 2), (rows, 1), 0, top)
    return jnp.take_along_axis(listing, (jnp.arange(top)[None, :] + offset_by) % top, axis=1)


def load_shares(number_of, total, most, lean, full):
    weights = [(1 << 20) // math.isqrt(rank ** lean) + 1 for rank in range(1, number_of + 1)]
    largest = most if full else min(most, max(-(-total // number_of), total * weights[0] // sum(weights)))
    least = 1 if total - largest >= number_of - 1 else 0
    holding, rest = [largest] + [least] * (number_of - 1), total - largest - least * (number_of - 1)
    while rest > 0:
        free = [i for i in range(1, number_of) if holding[i] < largest] or [i for i in range(1, number_of) if holding[i] < most]
        pool, remaining = sum([weights[i] for i in free]), rest
        for i in free:
            more = min(most - holding[i], max(1, remaining * weights[i] // pool), rest)
            holding[i] = holding[i] + more
            rest = rest - more
    return np.array(holding)


def setup_inputs(seed: int = 0) -> dict:
    key_of = jax.random.split(jax.random.key(seed), 6)
    sph_state = draw_sph_state(jax.random.fold_in(key_of[5], 71), 0)
    sph_dest_keys = jax.random.split(jax.random.fold_in(key_of[1], 1), SPHERES // SPH_DEV)
    sph_dest_turns = jax.random.permutation(jax.random.fold_in(key_of[1], 3), SPHERES // SPH_DEV)
    sph_dest = jax.vmap(lambda own, number: assign_block(jax.random.fold_in(key_of[1], 2), own, number, SPH_DEV, DEVROWS, 1, CAP, 1))(sph_dest_keys, sph_dest_turns).reshape((SPHERES, 1))
    body_list = choose_distinct(key_of[2], DEVROWS, BODIES, OVL, 8192)
    tile_codes = draw_tile_codes(jax.random.fold_in(key_of[5], 71), 0)
    triangles = draw_triangles(jax.random.fold_in(key_of[5], 71), 0)
    return dict(sph_state=sph_state, sph_dest=sph_dest, body_list=body_list, tile_codes=tile_codes, triangles=triangles)


stiff_pair = 50.0
damp_pair = 2.0
stiff_wall = 50.0
time_step = 0.01
gravity = 9.81
body_mass = 4.0
body_inertia = 40.0


def contact(spheres, facets):
    centre = spheres[0:3]
    radius = spheres[3]
    corner = facets[0:3]
    edge_one = facets[3:6] - corner
    edge_two = facets[6:9] - corner
    square_one = jnp.sum(edge_one * edge_one, 0)
    square_two = jnp.sum(edge_two * edge_two, 0)
    cross_term = jnp.sum(edge_one * edge_two, 0)
    inverse = 1.0 / (square_one * square_two - cross_term * cross_term)
    relative = centre[:, :, None] - corner[:, None, :]
    along_one = jnp.sum(relative * edge_one[:, None, :], 0)
    along_two = jnp.sum(relative * edge_two[:, None, :], 0)
    weight_b = (square_two * along_one - cross_term * along_two) * inverse
    weight_c = (square_one * along_two - cross_term * along_one) * inverse
    weight_a = jnp.maximum(1.0 - weight_b - weight_c, 0.0)
    weight_b = jnp.maximum(weight_b, 0.0)
    weight_c = jnp.maximum(weight_c, 0.0)
    totals = weight_a + weight_b + weight_c
    weight_b = weight_b / totals
    weight_c = weight_c / totals
    nearest = corner[:, None, :] + weight_b[None] * edge_one[:, None, :] + weight_c[None] * edge_two[:, None, :]
    offset = centre[:, :, None] - nearest
    squared = jnp.sum(offset * offset, 0)
    strength = stiff_wall * jnp.maximum(radius[:, None] * radius[:, None] - squared, 0.0)
    forces = strength[None] * offset
    on_spheres = jnp.sum(forces, 2)
    on_body = -jnp.sum(forces, (1, 2))
    torque = -jnp.sum(jnp.cross(nearest, forces, axis=0), (1, 2))
    return on_spheres, jnp.concatenate([on_body, torque])


def tile_forces(spheres, facets, tile_list):
    tiles_tri = facets.shape[1] // 128

    def advance_tile(carried, tile_code):
        forces, wrench = carried
        sphere_tile = tile_code // tiles_tri
        facet_tile = tile_code % tiles_tri
        sphere_part = lax.dynamic_slice_in_dim(spheres, sphere_tile * 128, 128, 1)
        facet_part = lax.dynamic_slice_in_dim(facets, facet_tile * 128, 128, 1)
        on_spheres, on_body = contact(sphere_part, facet_part)
        current = lax.dynamic_slice_in_dim(forces, sphere_tile * 128, 128, 1)
        forces = lax.dynamic_update_slice_in_dim(forces, current + on_spheres, sphere_tile * 128, 1)
        return (forces, wrench + on_body), None

    initial = (jnp.zeros((3, spheres.shape[1]), jnp.float32), jnp.zeros((6,), jnp.float32))
    (forces, wrench), unused = lax.scan(advance_tile, initial, tile_list)
    return forces, wrench


def sphere_forces(sphere_block):
    position = sphere_block[0:3]
    velocity = sphere_block[3:6]
    radius = sphere_block[6]
    occupied = (radius > 0).astype(jnp.float32)
    coords = jnp.concatenate([position, radius[None]], 0)
    baseline = radius * radius - jnp.sum(position * position, 0)
    inner_products = lax.dot_general(coords, coords, (((0,), (0,)), ((), ())), precision=lax.Precision.HIGHEST)
    intersection = jnp.maximum(baseline[:, None] + baseline[None, :] + 2.0 * inner_products, 0.0)
    intersection = intersection * occupied[:, None] * occupied[None, :]
    stacked = jnp.concatenate([position, velocity, jnp.ones((1, position.shape[1]), jnp.float32)], 0)
    weighted = lax.dot_general(stacked, intersection, (((1,), (1,)), ((), ())), precision=lax.Precision.HIGHEST)
    totals = weighted[6]
    return stiff_pair * (totals * position - weighted[0:3]) - damp_pair * (totals * velocity - weighted[3:6])


def advance(sphere_block, forces):
    position = sphere_block[0:3]
    velocity = sphere_block[3:6]
    radius = sphere_block[6]
    occupied = radius > 0
    masses = jnp.where(occupied, radius * radius * radius, 1.0)
    falling = jnp.array([0.0, 0.0, gravity], jnp.float32)
    acceleration = forces / masses[None] - falling[:, None]
    velocity_new = velocity + time_step * acceleration
    position_new = position + time_step * velocity_new
    result = jnp.concatenate([position_new, velocity_new, radius[None]], 0)
    return jnp.where(occupied[None], result, 0.0)


def migrate(sph_state, sph_dest):
    ndevices = N_SECTOR * N_BIN
    targets = sph_dest[:, 0].reshape(ndevices, SPH_DEV)

    def ranking(target_row):
        onehot = (target_row[:, None] == jnp.arange(ndevices, dtype=jnp.int32)[None, :]).astype(jnp.int32)
        return jnp.sum((jnp.cumsum(onehot, 0) - 1) * onehot, 1).astype(jnp.int32)

    ranks = lax.map(ranking, targets)
    sources = jnp.arange(ndevices, dtype=jnp.int32)[:, None]
    columns = (targets * (ndevices * CAP) + sources * CAP + ranks).reshape(-1)
    return jnp.zeros((7, SLOTS), jnp.float32).at[:, columns].set(sph_state)


def reference(sph_state, sph_dest, body_list, tile_codes, triangles):
    ndevices = N_SECTOR * N_BIN
    slots = migrate(sph_state, sph_dest)
    blocks = jnp.transpose(slots.reshape(7, ndevices, 2 * SPH_DEV), (1, 0, 2))
    device_ids = jnp.arange(ndevices, dtype=jnp.int32)

    def one_device(operands):
        sphere_block, bodies, tile_rows, device_id = operands
        bin_index = (device_id % N_BIN).astype(jnp.int32)
        forces = sphere_forces(sphere_block)
        coords = jnp.concatenate([sphere_block[0:3], sphere_block[6:7]], 0)
        wall_total = jnp.zeros_like(forces)
        wrench_rows = []
        for slot_index in range(OVL):
            facets = lax.dynamic_slice(triangles, (jnp.int32(0), bodies[slot_index].astype(jnp.int32), bin_index * TBLK), (9, 1, TBLK))[:, 0, :]
            on_spheres, on_body = tile_forces(coords, facets, tile_rows[slot_index])
            wall_total = wall_total + on_spheres
            wrench_rows.append(on_body)
        return advance(sphere_block, forces + wall_total), jnp.stack(wrench_rows)

    new_blocks, wrench_parts = lax.map(one_device, (blocks, body_list, tile_codes, device_ids))
    new_state = jnp.transpose(new_blocks, (1, 0, 2)).reshape(7, SLOTS)
    wrench = jnp.zeros((BODIES, 6), jnp.float32).at[body_list.reshape(-1)].add(wrench_parts.reshape(-1, 6))
    scaling = jnp.array([time_step / body_mass] * 3 + [time_step / body_inertia] * 3, jnp.float32)
    return new_state, wrench * scaling[None, :]
```

```python
import functools

import jax
import jax.numpy as jnp
from jax import lax
from jax.experimental import pallas as pl
from jax.experimental.pallas import tpu as pltpu
from jax.sharding import PartitionSpec as P

stiff_pair = 50.0
damp_pair = 2.0
stiff_wall = 50.0
time_step = 0.01
gravity = 9.81
body_mass = 4.0
body_inertia = 40.0

LANES = 128
PAYLOAD = ((0, 3), (1, 4), (2, 5), (6, None))
ROWS_STEP = 32
PAIR_BLOCK = 256


def iota(shape, dim):
    return lax.broadcasted_iota(jnp.int32, shape, dim)


def split3(x):
    hi = x.astype(jnp.bfloat16).astype(jnp.float32)
    rest = x - hi
    mid = rest.astype(jnp.bfloat16).astype(jnp.float32)
    return hi, mid, rest - mid


def dot(a, b, contract=((1,), (0,))):
    return lax.dot_general(a, b, (contract, ((), ())), preferred_element_type=jnp.float32)


def pack_kernel(dest_ref, state_ref, out_ref):
    blocks = dest_ref.shape[0]
    ndevices = out_ref.shape[0] * LANES // (8 * 64)
    capacity = 64
    dest = dest_ref[...]
    wide = blocks * ndevices
    expand = (iota((blocks, wide), 1) // ndevices == iota((blocks, wide), 0)).astype(jnp.bfloat16)
    dest_cols = jnp.transpose(dest.astype(jnp.float32)).astype(jnp.bfloat16)
    named = dot(dest_cols, expand)
    onehot = (named == (iota((LANES, wide), 1) % ndevices).astype(jnp.float32)).astype(jnp.float32)
    lower = (iota((LANES, LANES), 0) >= iota((LANES, LANES), 1)).astype(jnp.bfloat16)
    counted = dot(lower, onehot.astype(jnp.bfloat16))
    total = jnp.broadcast_to(counted[LANES - 1 :], (8, wide))
    before = jnp.zeros((8, wide), jnp.float32)
    for step in range(1, blocks):
        moved = pltpu.roll(total, step * ndevices, 1)
        before = before + jnp.where(iota((8, wide), 1) >= step * ndevices, moved, 0.0)
    place = (onehot * (counted - 1.0 + before[0:1])).astype(jnp.bfloat16)
    ranks = dot(expand, place, ((1,), (1,)))
    rank_row = jnp.concatenate([ranks[b : b + 1] for b in range(blocks)], 1)
    dest_row = jnp.concatenate([dest[b : b + 1] for b in range(blocks)], 1)
    leaving = blocks * LANES
    chosen = rank_row == iota((capacity, leaving), 0).astype(jnp.float32)
    to_dest = (dest_row == iota((ndevices, leaving), 0)).astype(jnp.float32).astype(jnp.bfloat16)
    out = None
    for part in split3(state_ref[...]):
        rows = []
        for pair in PAYLOAD:
            for source in pair:
                if source is None:
                    rows.append(jnp.zeros((capacity, leaving), jnp.bfloat16))
                else:
                    rows.append(jnp.where(chosen, part[source : source + 1], 0.0).astype(jnp.bfloat16))
        piece = dot(to_dest, jnp.concatenate(rows, 0), ((1,), (1,)))
        out = piece if out is None else out + piece
    groups = len(PAYLOAD)
    for k in range(groups):
        out_ref[pl.ds(k, ndevices, stride=groups), :] = out[:, k * LANES : (k + 1) * LANES]


def lane_sum(x):
    return jnp.sum(jnp.sum(x, 0, keepdims=True), 1, keepdims=True)


def wall_kernel(sectors, bins, *refs):
    tri_refs = refs[2 : 2 + sectors]
    bodies_ref, codes_ref = refs[0:2]
    arrived_ref = refs[2 + sectors]
    wrench_ref, packed_ref, force_ref, meta_ref = refs[3 + sectors : 7 + sectors]
    (raw, facet, px, py, pz, rr, acc, meta_smem, tri_sem, meta_sem) = refs[7 + sectors :]
    entries = bodies_ref.shape[1]
    codes = codes_ref.shape[2]
    tiles_tri = raw.shape[2]
    tiles = packed_slots(arrived_ref) // LANES
    me = lax.axis_index("sector")

    def fetch(entry, source):
        return pltpu.make_async_copy(tri_refs[source], raw.at[entry], tri_sem.at[entry])

    for entry in range(entries):
        relative = bodies_ref[0, entry] ^ me
        for source in range(sectors):

            @pl.when(relative == source)
            def _():
                fetch(entry, source).start()

    turned = jnp.transpose(arrived_ref[...])
    alive = jnp.sum((turned[0:64] > 0.0).astype(jnp.float32), 0, keepdims=True)
    alive = jnp.broadcast_to(alive, (8, LANES)).astype(jnp.bfloat16)
    row, col = iota((LANES, LANES), 0), iota((LANES, LANES), 1)
    of_tile = dot(alive, ((row // 8 == col) & (row % 4 == 3)).astype(jnp.bfloat16))
    of_first = dot(alive, (row == 8 * col + 3).astype(jnp.bfloat16))
    padded = jnp.floor((of_tile + 7.0) / 8.0) * 8.0
    base = dot(padded.astype(jnp.bfloat16), (row < col).astype(jnp.bfloat16))
    pick = iota((8, LANES), 0)
    meta = jnp.where(pick == 0, base, jnp.where(pick == 1, base + of_first, padded))
    meta_ref[...] = meta.astype(jnp.int32)
    copy = pltpu.make_async_copy(meta_ref, meta_smem, meta_sem)
    copy.start()
    copy.wait()

    lane = iota((64, LANES), 1)
    for tile in range(tiles):
        for half in range(2):
            q = 2 * tile + half
            even = pltpu.roll(turned[0:64], (LANES - 4 * q) % LANES, 1)
            odd = pltpu.roll(turned[64:128], (LANES + 4 - 4 * q) % LANES, 1)
            chunk = jnp.where(lane < 4, even, jnp.where(lane < 8, odd, 0.0))
            start = meta_smem[half, tile]
            packed_ref[pl.ds(start, 64), :] = chunk
            if half:
                packed_ref[pl.ds(start + 64, 8), :] = jnp.zeros((8, LANES), jnp.float32)
    rows_used = meta_smem[0, tiles]
    packed_ref[pl.ds(pl.multiple_of(rows_used, 8), PAIR_BLOCK), :] = jnp.zeros((PAIR_BLOCK, LANES), jnp.float32)

    steps = (rows_used + ROWS_STEP - 1) // ROWS_STEP

    def spread(step, carry):
        at = pl.ds(pl.multiple_of(step * ROWS_STEP, ROWS_STEP), ROWS_STEP)
        block = packed_ref[at, :]
        shape = (ROWS_STEP, LANES)
        px[at, :] = jnp.broadcast_to(block[:, 0:1], shape)
        py[at, :] = jnp.broadcast_to(block[:, 1:2], shape)
        pz[at, :] = jnp.broadcast_to(block[:, 2:3], shape)
        radius = jnp.broadcast_to(block[:, 3:4], shape)
        rr[at, :] = radius * radius
        for which in range(3 * entries):
            acc[which, at, :] = jnp.zeros(shape, jnp.float32)
        return carry

    lax.fori_loop(0, steps + 1, spread, 0)

    for entry in range(entries):
        fetch(entry, 0).wait()
        corner = [raw[entry, i] for i in range(3)]
        one = [raw[entry, 3 + i] - corner[i] for i in range(3)]
        two = [raw[entry, 6 + i] - corner[i] for i in range(3)]
        d11 = one[0] * one[0] + one[1] * one[1] + one[2] * one[2]
        d12 = one[0] * two[0] + one[1] * two[1] + one[2] * two[2]
        d22 = two[0] * two[0] + two[1] * two[1] + two[2] * two[2]
        inverse = 1.0 / (d11 * d22 - d12 * d12)
        for i in range(3):
            facet[entry, i] = corner[i]
            facet[entry, 3 + i] = one[i]
            facet[entry, 6 + i] = two[i]
            facet[entry, 9 + i] = (d22 * one[i] - d12 * two[i]) * inverse
            facet[entry, 12 + i] = (d11 * two[i] - d12 * one[i]) * inverse

        def one_tile(number, carry):
            code = codes_ref[0, entry, number]
            sphere_tile = code // tiles_tri
            facet_tile = code % tiles_tri
            f = [facet[entry, i, pl.ds(facet_tile, 1), :] for i in range(15)]
            first = meta_smem[0, sphere_tile]
            count = meta_smem[2, sphere_tile]

            def rows(step, inner):
                start = first + step * ROWS_STEP
                at = pl.ds(pl.multiple_of(start, 8), ROWS_STEP)
                inside = iota((ROWS_STEP, LANES), 0) < count - step * ROWS_STEP
                dx, dy, dz = px[at, :] - f[0], py[at, :] - f[1], pz[at, :] - f[2]
                beta = dx * f[9] + dy * f[10] + dz * f[11]
                gamma = dx * f[12] + dy * f[13] + dz * f[14]
                alpha = jnp.maximum(1.0 - beta - gamma, 0.0)
                beta = jnp.maximum(beta, 0.0)
                gamma = jnp.maximum(gamma, 0.0)
                scale = 1.0 / (alpha + beta + gamma)
                beta = beta * scale
                gamma = gamma * scale
                ox = dx - beta * f[3] - gamma * f[6]
                oy = dy - beta * f[4] - gamma * f[7]
                oz = dz - beta * f[5] - gamma * f[8]
                deep = jnp.maximum(rr[at, :] - (ox * ox + oy * oy + oz * oz), 0.0)
                deep = jnp.where(inside, deep, 0.0)
                acc[3 * entry, at, :] += deep * ox
                acc[3 * entry + 1, at, :] += deep * oy
                acc[3 * entry + 2, at, :] += deep * oz
                return inner

            lax.fori_loop(0, (count + ROWS_STEP - 1) // ROWS_STEP, rows, 0)
            return carry

        lax.fori_loop(0, codes, one_tile, 0)

    lane8 = iota((ROWS_STEP, LANES), 1)

    def gather(step, carry):
        at = pl.ds(pl.multiple_of(step * ROWS_STEP, ROWS_STEP), ROWS_STEP)
        x, y, z = px[at, :], py[at, :], pz[at, :]
        sums = []
        for entry in range(entries):
            fx, fy, fz = acc[3 * entry, at, :], acc[3 * entry + 1, at, :], acc[3 * entry + 2, at, :]
            new = [fx, fy, fz, y * fz - z * fy, z * fx - x * fz, x * fy - y * fx]
            sums += [carry[6 * entry + i] + jnp.sum(new[i].reshape(-1, 8, LANES), 0) for i in range(6)]
        whole = []
        for i in range(3):
            both = acc[i, at, :]
            for entry in range(1, entries):
                both = both + acc[3 * entry + i, at, :]
            whole.append(jnp.sum(both, 1, keepdims=True) * stiff_wall)
        force_ref[at, :] = jnp.where(
            lane8 == 0, whole[0], jnp.where(lane8 == 1, whole[1], jnp.where(lane8 == 2, whole[2], 0.0))
        )
        return tuple(sums)

    zero = jnp.zeros((8, LANES), jnp.float32)
    sums = lax.fori_loop(0, steps, gather, (zero,) * (6 * entries))
    out_lane = iota((sectors * bins, LANES), 1)
    owner = iota((sectors * bins, LANES), 0) // bins
    out = jnp.zeros((sectors * bins, LANES), jnp.float32)
    for entry in range(entries):
        mine = jnp.zeros((1, LANES), jnp.float32)
        for i in range(6):
            mine = jnp.where(iota((1, LANES), 1) == i, lane_sum(sums[6 * entry + i]), mine)
        out = out + jnp.where(owner == bodies_ref[0, entry], mine * (-stiff_wall), 0.0)
    wrench_ref[...] = out


def packed_slots(arrived_ref):
    return arrived_ref.shape[0] * LANES // 8


def pair_kernel(meta_ref, arrived_ref, packed_ref, force_ref, out_ref, left, right, moved, summed, slot):
    tiles = packed_slots(arrived_ref) // LANES
    rows_used = meta_ref[0, tiles]
    blocks = (rows_used + PAIR_BLOCK - 1) // PAIR_BLOCK
    row8 = iota((8, LANES), 0)

    def prepare(tile, carry):
        at = pl.ds(pl.multiple_of(tile * LANES, LANES), LANES)
        columns = packed_ref[at, :]
        rows = jnp.transpose(columns)[0:8]
        x, y, z, r = rows[0:1], rows[1:2], rows[2:3], rows[3:4]
        level = r * r - (x * x + y * y + z * z)
        other = jnp.where(r > 0.0, level, -3.0e38)
        i_side = jnp.where(row8 < 4, 2.0 * rows, jnp.where(row8 == 4, level, jnp.where(row8 == 5, 1.0, 0.0)))
        j_side = jnp.where(row8 < 4, rows, jnp.where(row8 == 4, 1.0, jnp.where(row8 == 5, other, 0.0)))
        ih, im, il = split3(i_side)
        jh, jm, jl = split3(j_side)
        rest = jnp.zeros((LANES - 48, LANES), jnp.float32)
        left[at, :] = jnp.transpose(jnp.concatenate([ih, ih, im, ih, il, im, rest], 0)).astype(jnp.bfloat16)
        right[:, at] = jnp.concatenate([jh, jm, jh, jl, jh, jm, rest], 0).astype(jnp.bfloat16)
        lane = iota((LANES, LANES), 1)
        value = jnp.where(lane == 3, 1.0, columns)
        vh, vm, vl = split3(value)
        moved[at, :] = (vh + pltpu.roll(vm, 8, 1) + pltpu.roll(vl, 16, 1)).astype(jnp.bfloat16)
        return carry

    lax.fori_loop(0, blocks * (PAIR_BLOCK // LANES), prepare, 0)

    def row_block(ib, carry):
        at = pl.ds(pl.multiple_of(ib * PAIR_BLOCK, PAIR_BLOCK), PAIR_BLOCK)
        mine = left[at, :]

        def column_block(jb, total):
            other = pl.ds(pl.multiple_of(jb * PAIR_BLOCK, PAIR_BLOCK), PAIR_BLOCK)
            weight = jnp.maximum(dot(mine, right[:, other]), 0.0)
            high = weight.astype(jnp.bfloat16)
            low = (weight - high.astype(jnp.float32)).astype(jnp.bfloat16)
            values = moved[other, :]
            return total + (dot(high, values) + dot(low, values))

        total = lax.fori_loop(0, blocks, column_block, jnp.zeros((PAIR_BLOCK, LANES), jnp.float32))
        total = total + pltpu.roll(total, LANES - 8, 1) + pltpu.roll(total, LANES - 16, 1)
        weights = jnp.broadcast_to(total[:, 3:4], (PAIR_BLOCK, LANES))
        differ = weights * packed_ref[at, :] - total
        summed[at, :] = stiff_pair * differ - damp_pair * pltpu.roll(differ, LANES - 4, 1) + force_ref[at, :]
        return carry

    lax.fori_loop(0, blocks, row_block, 0)

    lane = iota((8, LANES), 1)
    for tile in range(tiles):
        for half in range(2):
            slot[tile, half * 64 : half * 64 + 64, :] = summed[pl.ds(meta_ref[half, tile], 64), :]
        force = jnp.transpose(slot[tile])[0:8]
        words = arrived_ref[8 * tile : 8 * tile + 8, :]
        swapped = pltpu.roll(pltpu.roll(words, 64, 1), 4, 0)
        state = jnp.where((row8 < 4) == (lane < 64), words, swapped)
        radius = jnp.broadcast_to(state[3:4], (8, LANES))
        live = radius > 0.0
        mass = jnp.where(live, radius * radius * radius, 1.0)
        falling = jnp.where(row8 == 6, gravity, 0.0)
        speed = state + time_step * (pltpu.roll(force, 4, 0) / mass - falling)
        place = state + time_step * pltpu.roll(speed, 4, 0)
        result = jnp.where(
            row8 < 3, place, jnp.where(row8 < 6, pltpu.roll(speed, 7, 0), pltpu.roll(state, 3, 0))
        )
        result = jnp.where(live, result, 0.0)
        out_ref[:, tile * LANES : (tile + 1) * LANES] = result[0:7]


def whole_vmem():
    return pl.BlockSpec(memory_space=pltpu.VMEM)


def whole_smem():
    return pl.BlockSpec(memory_space=pltpu.SMEM)


def fast(sph_state, sph_dest, body_list, tile_codes, triangles):
    sectors = lax.axis_size("sector")
    bins = lax.axis_size("bin")
    ndevices = sectors * bins
    leaving = sph_state.shape[1]
    slots = 2 * leaving
    words = 8 * slots // LANES
    block = triangles.reshape(triangles.shape[0], -1, LANES)
    blocks = [block] + [
        lax.ppermute(block, "sector", [(i, i ^ step) for i in range(sectors)]) for step in range(1, sectors)
    ]
    outgoing = pl.pallas_call(
        pack_kernel,
        out_shape=jax.ShapeDtypeStruct((words, LANES), jnp.float32),
        in_specs=[whole_vmem(), whole_vmem()],
        out_specs=whole_vmem(),
        name="pack",
    )(sph_dest.reshape(-1, LANES), sph_state)
    outgoing = outgoing.reshape(ndevices, 1, words * LANES // ndevices)
    arrived = lax.all_to_all(outgoing, ("sector", "bin"), split_axis=0, concat_axis=0, tiled=True)
    arrived = arrived.reshape(words, LANES)
    room = slots + PAIR_BLOCK + 2 * ROWS_STEP
    entries = body_list.shape[1]
    column = pltpu.VMEM((room, LANES), jnp.float32)
    wrench, packed, force, meta = pl.pallas_call(
        functools.partial(wall_kernel, sectors, bins),
        out_shape=[
            jax.ShapeDtypeStruct((ndevices, LANES), jnp.float32),
            jax.ShapeDtypeStruct((room, LANES), jnp.float32),
            jax.ShapeDtypeStruct((room, LANES), jnp.float32),
            jax.ShapeDtypeStruct((8, LANES), jnp.int32),
        ],
        in_specs=[whole_smem(), whole_smem()] + [pl.BlockSpec(memory_space=pl.ANY)] * sectors + [whole_vmem()],
        out_specs=[whole_vmem()] * 4,
        scratch_shapes=[
            pltpu.VMEM((entries,) + block.shape, jnp.float32),
            pltpu.VMEM((entries, 15) + block.shape[1:], jnp.float32),
            column,
            column,
            column,
            column,
            pltpu.VMEM((3 * entries, room, LANES), jnp.float32),
            pltpu.SMEM((8, LANES), jnp.int32),
            pltpu.SemaphoreType.DMA((entries,)),
            pltpu.SemaphoreType.DMA(()),
        ],
        name="wall",
    )(body_list, tile_codes, *blocks, arrived)
    shared = lax.all_to_all(
        wrench.reshape(ndevices, 1, LANES), ("sector", "bin"), split_axis=0, concat_axis=0, tiled=True
    )
    half_words = jnp.bfloat16
    new_block = pl.pallas_call(
        pair_kernel,
        out_shape=jax.ShapeDtypeStruct((7, slots), jnp.float32),
        in_specs=[whole_smem(), whole_vmem(), whole_vmem(), whole_vmem()],
        out_specs=whole_vmem(),
        scratch_shapes=[
            pltpu.VMEM((room, LANES), half_words),
            pltpu.VMEM((LANES, slots + PAIR_BLOCK), half_words),
            pltpu.VMEM((room, LANES), half_words),
            pltpu.VMEM((room, LANES), jnp.float32),
            pltpu.VMEM((slots // LANES, LANES, LANES), jnp.float32),
        ],
        name="pair",
    )(meta, arrived, packed, force)
    scaling = jnp.array([time_step / body_mass] * 3 + [time_step / body_inertia] * 3, jnp.float32)
    kick = jnp.sum(shared[:, 0, :6], 0, keepdims=True) * scaling[None, :]
    return new_block, kick


def contact(spheres, facets):
    centre = spheres[0:3]
    radius = spheres[3]
    corner = facets[0:3]
    edge_one = facets[3:6] - corner
    edge_two = facets[6:9] - corner
    square_one = jnp.sum(edge_one * edge_one, 0)
    square_two = jnp.sum(edge_two * edge_two, 0)
    cross_term = jnp.sum(edge_one * edge_two, 0)
    inverse = 1.0 / (square_one * square_two - cross_term * cross_term)
    relative = centre[:, :, None] - corner[:, None, :]
    along_one = jnp.sum(relative * edge_one[:, None, :], 0)
    along_two = jnp.sum(relative * edge_two[:, None, :], 0)
    weight_b = (square_two * along_one - cross_term * along_two) * inverse
    weight_c = (square_one * along_two - cross_term * along_one) * inverse
    weight_a = jnp.maximum(1.0 - weight_b - weight_c, 0.0)
    weight_b = jnp.maximum(weight_b, 0.0)
    weight_c = jnp.maximum(weight_c, 0.0)
    totals = weight_a + weight_b + weight_c
    weight_b = weight_b / totals
    weight_c = weight_c / totals
    nearest = (
        corner[:, None, :]
        + weight_b[None] * edge_one[:, None, :]
        + weight_c[None] * edge_two[:, None, :]
    )
    offset = centre[:, :, None] - nearest
    squared = jnp.sum(offset * offset, 0)
    strength = stiff_wall * jnp.maximum(radius[:, None] * radius[:, None] - squared, 0.0)
    forces = strength[None] * offset
    on_spheres = jnp.sum(forces, 2)
    on_body = -jnp.sum(forces, (1, 2))
    torque = -jnp.sum(jnp.cross(nearest, forces, axis=0), (1, 2))
    return (on_spheres, jnp.concatenate([on_body, torque]))


def tile_forces(spheres, facets, tile_list):
    tiles_tri = facets.shape[1] // 128

    def advance_tile(carried, tile_code):
        forces, wrench = carried
        sphere_tile = tile_code // tiles_tri
        facet_tile = tile_code % tiles_tri
        sphere_part = lax.dynamic_slice_in_dim(spheres, sphere_tile * 128, 128, 1)
        facet_part = lax.dynamic_slice_in_dim(facets, facet_tile * 128, 128, 1)
        on_spheres, on_body = contact(sphere_part, facet_part)
        current = lax.dynamic_slice_in_dim(forces, sphere_tile * 128, 128, 1)
        forces = lax.dynamic_update_slice_in_dim(forces, current + on_spheres, sphere_tile * 128, 1)
        return ((forces, wrench + on_body), None)

    initial = (jnp.zeros((3, spheres.shape[1]), jnp.float32), jnp.zeros((6,), jnp.float32))
    (forces, wrench), unused = lax.scan(advance_tile, initial, tile_list)
    return (forces, wrench)


def sphere_forces(sphere_block):
    position = sphere_block[0:3]
    velocity = sphere_block[3:6]
    radius = sphere_block[6]
    width_all = sphere_block.shape[1]
    occupied = (radius > 0).astype(jnp.float32)
    coords = jnp.concatenate([position, radius[None]], 0)
    baseline = radius * radius - jnp.sum(position * position, 0)
    stacked = jnp.concatenate([position, velocity, jnp.ones((1, width_all), jnp.float32)], 0)
    row_block = 512

    def row_group(row_start):
        coords_rows = lax.dynamic_slice_in_dim(coords, row_start, row_block, 1)
        base_rows = lax.dynamic_slice_in_dim(baseline, row_start, row_block, 0)
        live_rows = lax.dynamic_slice_in_dim(occupied, row_start, row_block, 0)
        inner_products = lax.dot_general(
            coords_rows, coords, (((0,), (0,)), ((), ())), precision=lax.Precision.HIGHEST
        )
        intersection = jnp.maximum(
            base_rows[:, None] + baseline[None, :] + 2.0 * inner_products, 0.0
        )
        intersection = intersection * live_rows[:, None] * occupied[None, :]
        return lax.dot_general(
            stacked, intersection, (((1,), (1,)), ((), ())), precision=lax.Precision.HIGHEST
        )

    starts = jnp.arange(width_all // row_block, dtype=jnp.int32) * row_block
    grouped = lax.map(row_group, starts)
    weighted = jnp.transpose(grouped, (1, 0, 2)).reshape(7, width_all)
    totals = weighted[6]
    return stiff_pair * (totals * position - weighted[0:3]) - damp_pair * (
        totals * velocity - weighted[3:6]
    )


def advance(sphere_block, forces):
    position = sphere_block[0:3]
    velocity = sphere_block[3:6]
    radius = sphere_block[6]
    occupied = radius > 0
    masses = jnp.where(occupied, radius * radius * radius, 1.0)
    falling = jnp.array([0.0, 0.0, gravity], jnp.float32)
    acceleration = forces / masses[None] - falling[:, None]
    velocity_new = velocity + time_step * acceleration
    position_new = position + time_step * velocity_new
    result = jnp.concatenate([position_new, velocity_new, radius[None]], 0)
    return jnp.where(occupied[None], result, 0.0)


def bin_total(partial_row):
    return lax.psum(partial_row, "bin")


def general(sph_state, sph_dest, body_list, tile_codes, triangles):
    sectors = lax.axis_size("sector")
    bins = lax.axis_size("bin")
    ndevices = sectors * bins
    leaving = sph_state.shape[1]
    capacity = 2 * leaving // ndevices
    targets = sph_dest[:, 0]
    onehot = (targets[:, None] == jnp.arange(ndevices, dtype=jnp.int32)[None, :]).astype(jnp.int32)
    ranks = jnp.sum((jnp.cumsum(onehot, 0) - 1) * onehot, 1)
    columns = targets * capacity + ranks
    outgoing = jnp.zeros((7, ndevices * capacity), jnp.float32).at[:, columns].set(sph_state)
    outgoing = outgoing.reshape(7, sectors, bins, capacity)
    arrived = lax.all_to_all(
        lax.all_to_all(outgoing, "sector", split_axis=1, concat_axis=1, tiled=True),
        "bin",
        split_axis=2,
        concat_axis=2,
        tiled=True,
    )
    sphere_block = arrived.reshape(7, ndevices * capacity)
    width_all = sphere_block.shape[1]
    coords = jnp.concatenate([sphere_block[0:3], sphere_block[6:7]], 0)
    pair_total = sphere_forces(sphere_block)
    everyone = lax.all_gather(triangles, "sector", axis=1, tiled=True)
    wall_total = jnp.zeros((3, width_all), jnp.float32)
    partial_value = jnp.zeros((sectors, 6), jnp.float32)
    for slot_index in range(body_list.shape[1]):
        owner_body = body_list[0, slot_index]
        facets = lax.dynamic_index_in_dim(everyone, owner_body, 1, keepdims=False)
        on_spheres, on_body = tile_forces(coords, facets, tile_codes[0, slot_index])
        wall_total = wall_total + on_spheres
        selector = (jnp.arange(sectors, dtype=jnp.int32) == owner_body).astype(jnp.float32)
        partial_value = partial_value + selector[:, None] * on_body[None, :]
    own_row = lax.psum_scatter(partial_value, "sector", scatter_dimension=0, tiled=True)
    own_row = bin_total(own_row)
    new_block = advance(sphere_block, pair_total + wall_total)
    scaling = jnp.array([time_step / body_mass] * 3 + [time_step / body_inertia] * 3, jnp.float32)
    return (new_block, own_row * scaling[None, :])


def local(sph_state, sph_dest, body_list, tile_codes, triangles):
    sectors = lax.axis_size("sector")
    ndevices = sectors * lax.axis_size("bin")
    leaving = sph_state.shape[1]
    fits = 2 * leaving == 64 * ndevices and 16 * leaving == LANES * LANES and sectors & (sectors - 1) == 0
    chosen = fast if fits else general
    return chosen(sph_state, sph_dest, body_list, tile_codes, triangles)


def solution(mesh):
    return jax.shard_map(
        local,
        mesh=mesh,
        in_specs=(
            P(None, ("sector", "bin")),
            P(("sector", "bin"), None),
            P(("sector", "bin"), None),
            P(("sector", "bin"), None, None),
            P(None, "sector", "bin"),
        ),
        out_specs=(P(None, ("sector", "bin")), P("sector", None)),
        check_vma=False,
    )
```

```python
import functools

import jax
import jax.numpy as jnp
from jax import lax
from jax.experimental import pallas as pl
from jax.experimental.pallas import tpu as pltpu
from jax.sharding import PartitionSpec as P

stiff_pair = 50.0
damp_pair = 2.0
stiff_wall = 50.0
time_step = 0.01
gravity = 9.81
body_mass = 4.0
body_inertia = 40.0

LANES = 128
PAYLOAD = ((0, 3), (1, 4), (2, 5), (6, None))
PAIR_BLOCK = 256
WALL_ROWS = 128


def iota(shape, dim):
    return lax.broadcasted_iota(jnp.int32, shape, dim)


def split3(x):
    hi = x.astype(jnp.bfloat16).astype(jnp.float32)
    rest = x - hi
    mid = rest.astype(jnp.bfloat16).astype(jnp.float32)
    return hi, mid, rest - mid


def dot(a, b, contract=((1,), (0,))):
    return lax.dot_general(a, b, (contract, ((), ())), preferred_element_type=jnp.float32)


def pack_kernel(dest_ref, state_ref, out_ref):
    blocks = dest_ref.shape[0]
    ndevices = out_ref.shape[0] * LANES // (8 * 64)
    capacity = 64
    dest = dest_ref[...]
    wide = blocks * ndevices
    expand = (iota((blocks, wide), 1) // ndevices == iota((blocks, wide), 0)).astype(jnp.bfloat16)
    dest_cols = jnp.transpose(dest.astype(jnp.float32)).astype(jnp.bfloat16)
    named = dot(dest_cols, expand)
    onehot = (named == (iota((LANES, wide), 1) % ndevices).astype(jnp.float32)).astype(jnp.float32)
    lower = (iota((LANES, LANES), 0) >= iota((LANES, LANES), 1)).astype(jnp.bfloat16)
    counted = dot(lower, onehot.astype(jnp.bfloat16))
    total = jnp.broadcast_to(counted[LANES - 1 :], (8, wide))
    before = jnp.zeros((8, wide), jnp.float32)
    for step in range(1, blocks):
        moved = pltpu.roll(total, step * ndevices, 1)
        before = before + jnp.where(iota((8, wide), 1) >= step * ndevices, moved, 0.0)
    place = (onehot * (counted - 1.0 + before[0:1])).astype(jnp.bfloat16)
    ranks = dot(expand, place, ((1,), (1,)))
    rank_row = jnp.concatenate([ranks[b : b + 1] for b in range(blocks)], 1)
    dest_row = jnp.concatenate([dest[b : b + 1] for b in range(blocks)], 1)
    leaving = blocks * LANES
    chosen = rank_row == iota((capacity, leaving), 0).astype(jnp.float32)
    to_dest = (dest_row == iota((ndevices, leaving), 0)).astype(jnp.float32).astype(jnp.bfloat16)
    out = None
    for part in split3(state_ref[...]):
        rows = []
        for pair in PAYLOAD:
            for source in pair:
                if source is None:
                    rows.append(jnp.zeros((capacity, leaving), jnp.bfloat16))
                else:
                    rows.append(jnp.where(chosen, part[source : source + 1], 0.0).astype(jnp.bfloat16))
        piece = dot(to_dest, jnp.concatenate(rows, 0), ((1,), (1,)))
        out = piece if out is None else out + piece
    groups = len(PAYLOAD)
    for k in range(groups):
        out_ref[pl.ds(k, ndevices, stride=groups), :] = out[:, k * LANES : (k + 1) * LANES]


def total_of(x):
    return jnp.sum(jnp.sum(x, 0, keepdims=True), 1, keepdims=True)


def state_tile(arrived_ref, tile):
    words = arrived_ref[8 * tile : 8 * tile + 8, :]
    swapped = pltpu.roll(pltpu.roll(words, 64, 1), 4, 0)
    same = (iota((8, LANES), 0) < 4) == (iota((8, LANES), 1) < 64)
    return jnp.where(same, words, swapped)


def wall_kernel(sectors, bins, *refs):
    tri_refs = refs[2 : 2 + sectors]
    bodies_ref, codes_ref = refs[0:2]
    entries = bodies_ref.shape[1]
    arrived_ref = refs[2 + sectors]
    wrench_ref, force_ref = refs[3 + sectors : 5 + sectors]
    raw, facet, px, py, pz, rr, place, gathered, tri_sem = refs[5 + sectors : 14 + sectors]
    accs = refs[14 + sectors :]
    codes = codes_ref.shape[2]
    tiles_tri = raw.shape[2]
    tiles = arrived_ref.shape[0] // 8
    me = lax.axis_index("sector")

    def fetch(entry, source):
        return pltpu.make_async_copy(tri_refs[source], raw.at[entry], tri_sem.at[entry])

    for entry in range(entries):
        relative = bodies_ref[0, entry] ^ me
        for source in range(sectors):

            @pl.when(relative == source)
            def _():
                fetch(entry, source).start()

    turned = jnp.transpose(arrived_ref[...])[0:64]
    squared = turned * turned
    for q in range(2 * tiles):
        at = slice(64 * q, 64 * q + 64)
        for ref, source, i in ((px, turned, 0), (py, turned, 1), (pz, turned, 2), (rr, squared, 3)):
            lane = 4 * q + i
            ref[at, :] = jnp.broadcast_to(source[:, lane : lane + 1], (64, LANES))
    for tile in range(tiles):
        state = state_tile(arrived_ref, tile)
        for i in range(3):
            place[i, tile : tile + 1, :] = state[i : i + 1]

    for acc in accs:
        acc[...] = jnp.zeros_like(acc)

    for entry in range(entries):
        fetch(entry, 0).wait()
        corner = [raw[entry, i] for i in range(3)]
        one = [raw[entry, 3 + i] - corner[i] for i in range(3)]
        two = [raw[entry, 6 + i] - corner[i] for i in range(3)]
        d11 = one[0] * one[0] + one[1] * one[1] + one[2] * one[2]
        d12 = one[0] * two[0] + one[1] * two[1] + one[2] * two[2]
        d22 = two[0] * two[0] + two[1] * two[1] + two[2] * two[2]
        inverse = 1.0 / (d11 * d22 - d12 * d12)
        for i in range(3):
            facet[entry, i] = corner[i]
            facet[entry, 3 + i] = one[i]
            facet[entry, 6 + i] = two[i]
            facet[entry, 9 + i] = (d22 * one[i] - d12 * two[i]) * inverse
            facet[entry, 12 + i] = (d11 * two[i] - d12 * one[i]) * inverse

    def one_tile(entry, number):
        code = codes_ref[0, entry, number]
        first = pl.multiple_of(code // tiles_tri * LANES, LANES)
        facet_tile = code % tiles_tri
        f = [facet[entry, i, pl.ds(facet_tile, 1), :] for i in range(15)]
        for part in range(LANES // WALL_ROWS):
            at = pl.ds(pl.multiple_of(first + part * WALL_ROWS, WALL_ROWS), WALL_ROWS)
            dx, dy, dz = px[at, :] - f[0], py[at, :] - f[1], pz[at, :] - f[2]
            beta = dx * f[9] + dy * f[10] + dz * f[11]
            gamma = dx * f[12] + dy * f[13] + dz * f[14]
            alpha = jnp.maximum(1.0 - beta - gamma, 0.0)
            beta = jnp.maximum(beta, 0.0)
            gamma = jnp.maximum(gamma, 0.0)
            scale = 1.0 / (alpha + beta + gamma)
            beta = beta * scale
            gamma = gamma * scale
            ox = dx - beta * f[3] - gamma * f[6]
            oy = dy - beta * f[4] - gamma * f[7]
            oz = dz - beta * f[5] - gamma * f[8]
            deep = jnp.maximum(rr[at, :] - (ox * ox + oy * oy + oz * oz), 0.0)
            accs[3 * entry][at, :] += deep * ox
            accs[3 * entry + 1][at, :] += deep * oy
            accs[3 * entry + 2][at, :] += deep * oz

    def step(number, carry):
        for entry in range(entries):
            one_tile(entry, number)
        return carry

    lax.fori_loop(0, codes, step, 0)

    def gather(tile, carry):
        at = pl.ds(pl.multiple_of(tile * LANES, LANES), LANES)
        for which in range(3 * entries):
            row = jnp.sum(jnp.transpose(accs[which][at, :]), 0, keepdims=True)
            gathered[which, pl.ds(tile, 1), :] = row
        return carry

    lax.fori_loop(0, tiles, gather, 0)
    x, y, z = place[0], place[1], place[2]
    owner = iota((sectors * bins, LANES), 0) // bins
    lane = iota((1, LANES), 1)
    out = jnp.zeros((sectors * bins, LANES), jnp.float32)
    whole = [0.0, 0.0, 0.0]
    for entry in range(entries):
        fx, fy, fz = (gathered[3 * entry + i] for i in range(3))
        parts = (fx, fy, fz, y * fz - z * fy, z * fx - x * fz, x * fy - y * fx)
        mine = jnp.zeros((1, LANES), jnp.float32)
        for i, part in enumerate(parts):
            mine = jnp.where(lane == i, total_of(part), mine)
        out = out + jnp.where(owner == bodies_ref[0, entry], mine * (-stiff_wall), 0.0)
        whole = [whole[0] + fx, whole[1] + fy, whole[2] + fz]
    wrench_ref[...] = out
    for i in range(3):
        force_ref[i] = stiff_wall * whole[i]


def pair_kernel(arrived_ref, force_ref, out_ref, left, right, moved):
    tiles = arrived_ref.shape[0] // 8
    blocks = tiles * LANES // PAIR_BLOCK
    row8 = iota((8, LANES), 0)
    for tile in range(tiles):
        at = slice(tile * LANES, (tile + 1) * LANES)
        state = state_tile(arrived_ref, tile)
        square = state * state
        level = square[3:4] - (square[0:1] + square[1:2] + square[2:3])
        other = jnp.where(state[3:4] > 0.0, level, -3.0e38)
        i_side = jnp.where(row8 < 4, 2.0 * state, jnp.where(row8 == 4, level, jnp.where(row8 == 5, 1.0, 0.0)))
        j_side = jnp.where(row8 < 4, state, jnp.where(row8 == 4, 1.0, jnp.where(row8 == 5, other, 0.0)))
        ih, im, il = split3(i_side)
        jh, jm, jl = split3(j_side)
        right[:, at] = jnp.concatenate([ih, ih, im, ih, il, im], 0).astype(jnp.bfloat16)
        left[at, 0:48] = jnp.transpose(jnp.concatenate([jh, jm, jh, jl, jh, jm], 0)).astype(jnp.bfloat16)
        value = jnp.where(row8 == 3, 1.0, state)
        moved[:, at] = jnp.concatenate(list(split3(value)) + [jnp.zeros((8, LANES), jnp.float32)], 0).astype(
            jnp.bfloat16
        )

    def block_of(ib, carry):
        columns = pl.ds(pl.multiple_of(ib * PAIR_BLOCK, PAIR_BLOCK), PAIR_BLOCK)
        mine = right[:, columns]
        total = jnp.zeros((32, PAIR_BLOCK), jnp.float32)
        for jb in range(blocks):
            rows = slice(jb * PAIR_BLOCK, (jb + 1) * PAIR_BLOCK)
            weight = jnp.maximum(dot(left[rows, 0:48], mine), 0.0)
            high = weight.astype(jnp.bfloat16)
            low = (weight - high.astype(jnp.float32)).astype(jnp.bfloat16)
            values = moved[:, rows]
            total = total + (dot(values, high) + dot(values, low))
        total = total[0:8] + total[8:16] + total[16:24]
        for part in range(PAIR_BLOCK // LANES):
            tile = ib * (PAIR_BLOCK // LANES) + part
            words = arrived_ref[pl.ds(pl.multiple_of(8 * tile, 8), 8), :]
            swapped = pltpu.roll(pltpu.roll(words, 64, 1), 4, 0)
            state = jnp.where((row8 < 4) == (iota((8, LANES), 1) < 64), words, swapped)
            moment = total[:, part * LANES : (part + 1) * LANES]
            differ = moment[3:4] * state - moment
            force = stiff_pair * differ - damp_pair * pltpu.roll(differ, 4, 0)
            for i in range(3):
                force = force + jnp.where(row8 == i, force_ref[i, pl.ds(tile, 1), :], 0.0)
            radius = jnp.broadcast_to(state[3:4], (8, LANES))
            live = radius > 0.0
            mass = jnp.where(live, radius * radius * radius, 1.0)
            falling = jnp.where(row8 == 6, gravity, 0.0)
            speed = state + time_step * (pltpu.roll(force, 4, 0) / mass - falling)
            place = state + time_step * pltpu.roll(speed, 4, 0)
            result = jnp.where(
                row8 < 3, place, jnp.where(row8 < 6, pltpu.roll(speed, 7, 0), pltpu.roll(state, 3, 0))
            )
            result = jnp.where(live, result, 0.0)
            out_ref[:, pl.ds(pl.multiple_of(tile * LANES, LANES), LANES)] = result[0:7]
        return carry

    lax.fori_loop(0, blocks, block_of, 0)


def whole_vmem():
    return pl.BlockSpec(memory_space=pltpu.VMEM)


def whole_smem():
    return pl.BlockSpec(memory_space=pltpu.SMEM)


def fast(sph_state, sph_dest, body_list, tile_codes, triangles):
    sectors = lax.axis_size("sector")
    bins = lax.axis_size("bin")
    ndevices = sectors * bins
    leaving = sph_state.shape[1]
    slots = 2 * leaving
    words = 8 * slots // LANES
    block = triangles.reshape(triangles.shape[0], -1, LANES)
    blocks = [block] + [
        lax.ppermute(block, "sector", [(i, i ^ step) for i in range(sectors)]) for step in range(1, sectors)
    ]
    outgoing = pl.pallas_call(
        pack_kernel,
        out_shape=jax.ShapeDtypeStruct((words, LANES), jnp.float32),
        in_specs=[whole_vmem(), whole_vmem()],
        out_specs=whole_vmem(),
        name="pack",
    )(sph_dest.reshape(-1, LANES), sph_state)
    outgoing = outgoing.reshape(ndevices, 1, words * LANES // ndevices)
    arrived = lax.all_to_all(outgoing, ("sector", "bin"), split_axis=0, concat_axis=0, tiled=True)
    arrived = arrived.reshape(words, LANES)
    entries = body_list.shape[1]
    column = pltpu.VMEM((slots, LANES), jnp.float32)
    tiles = slots // LANES
    wrench, force = pl.pallas_call(
        functools.partial(wall_kernel, sectors, bins),
        out_shape=[
            jax.ShapeDtypeStruct((ndevices, LANES), jnp.float32),
            jax.ShapeDtypeStruct((3, tiles, LANES), jnp.float32),
        ],
        in_specs=[whole_smem(), whole_smem()] + [pl.BlockSpec(memory_space=pl.ANY)] * sectors + [whole_vmem()],
        out_specs=[whole_vmem()] * 2,
        scratch_shapes=[
            pltpu.VMEM((entries,) + block.shape, jnp.float32),
            pltpu.VMEM((entries, 15) + block.shape[1:], jnp.float32),
            column,
            column,
            column,
            column,
            pltpu.VMEM((3, tiles, LANES), jnp.float32),
            pltpu.VMEM((3 * entries, tiles, LANES), jnp.float32),
            pltpu.SemaphoreType.DMA((entries,)),
        ]
        + [column] * (3 * entries),
        name="wall",
    )(body_list, tile_codes, *blocks, arrived)
    shared = lax.all_to_all(
        wrench.reshape(ndevices, 1, LANES), ("sector", "bin"), split_axis=0, concat_axis=0, tiled=True
    )
    new_block = pl.pallas_call(
        pair_kernel,
        out_shape=jax.ShapeDtypeStruct((7, slots), jnp.float32),
        in_specs=[whole_vmem(), whole_vmem()],
        out_specs=whole_vmem(),
        scratch_shapes=[
            pltpu.VMEM((slots, LANES), jnp.bfloat16),
            pltpu.VMEM((48, slots), jnp.bfloat16),
            pltpu.VMEM((32, slots), jnp.bfloat16),
        ],
        name="pair",
    )(arrived, force)
    scaling = jnp.array([time_step / body_mass] * 3 + [time_step / body_inertia] * 3, jnp.float32)
    kick = jnp.sum(shared[:, 0, :6], 0, keepdims=True) * scaling[None, :]
    return new_block, kick


def contact(spheres, facets):
    centre = spheres[0:3]
    radius = spheres[3]
    corner = facets[0:3]
    edge_one = facets[3:6] - corner
    edge_two = facets[6:9] - corner
    square_one = jnp.sum(edge_one * edge_one, 0)
    square_two = jnp.sum(edge_two * edge_two, 0)
    cross_term = jnp.sum(edge_one * edge_two, 0)
    inverse = 1.0 / (square_one * square_two - cross_term * cross_term)
    relative = centre[:, :, None] - corner[:, None, :]
    along_one = jnp.sum(relative * edge_one[:, None, :], 0)
    along_two = jnp.sum(relative * edge_two[:, None, :], 0)
    weight_b = (square_two * along_one - cross_term * along_two) * inverse
    weight_c = (square_one * along_two - cross_term * along_one) * inverse
    weight_a = jnp.maximum(1.0 - weight_b - weight_c, 0.0)
    weight_b = jnp.maximum(weight_b, 0.0)
    weight_c = jnp.maximum(weight_c, 0.0)
    totals = weight_a + weight_b + weight_c
    weight_b = weight_b / totals
    weight_c = weight_c / totals
    nearest = (
        corner[:, None, :]
        + weight_b[None] * edge_one[:, None, :]
        + weight_c[None] * edge_two[:, None, :]
    )
    offset = centre[:, :, None] - nearest
    squared = jnp.sum(offset * offset, 0)
    strength = stiff_wall * jnp.maximum(radius[:, None] * radius[:, None] - squared, 0.0)
    forces = strength[None] * offset
    on_spheres = jnp.sum(forces, 2)
    on_body = -jnp.sum(forces, (1, 2))
    torque = -jnp.sum(jnp.cross(nearest, forces, axis=0), (1, 2))
    return (on_spheres, jnp.concatenate([on_body, torque]))


def tile_forces(spheres, facets, tile_list):
    tiles_tri = facets.shape[1] // 128

    def advance_tile(carried, tile_code):
        forces, wrench = carried
        sphere_tile = tile_code // tiles_tri
        facet_tile = tile_code % tiles_tri
        sphere_part = lax.dynamic_slice_in_dim(spheres, sphere_tile * 128, 128, 1)
        facet_part = lax.dynamic_slice_in_dim(facets, facet_tile * 128, 128, 1)
        on_spheres, on_body = contact(sphere_part, facet_part)
        current = lax.dynamic_slice_in_dim(forces, sphere_tile * 128, 128, 1)
        forces = lax.dynamic_update_slice_in_dim(forces, current + on_spheres, sphere_tile * 128, 1)
        return ((forces, wrench + on_body), None)

    initial = (jnp.zeros((3, spheres.shape[1]), jnp.float32), jnp.zeros((6,), jnp.float32))
    (forces, wrench), unused = lax.scan(advance_tile, initial, tile_list)
    return (forces, wrench)


def sphere_forces(sphere_block):
    position = sphere_block[0:3]
    velocity = sphere_block[3:6]
    radius = sphere_block[6]
    width_all = sphere_block.shape[1]
    occupied = (radius > 0).astype(jnp.float32)
    coords = jnp.concatenate([position, radius[None]], 0)
    baseline = radius * radius - jnp.sum(position * position, 0)
    stacked = jnp.concatenate([position, velocity, jnp.ones((1, width_all), jnp.float32)], 0)
    row_block = 512

    def row_group(row_start):
        coords_rows = lax.dynamic_slice_in_dim(coords, row_start, row_block, 1)
        base_rows = lax.dynamic_slice_in_dim(baseline, row_start, row_block, 0)
        live_rows = lax.dynamic_slice_in_dim(occupied, row_start, row_block, 0)
        inner_products = lax.dot_general(
            coords_rows, coords, (((0,), (0,)), ((), ())), precision=lax.Precision.HIGHEST
        )
        intersection = jnp.maximum(
            base_rows[:, None] + baseline[None, :] + 2.0 * inner_products, 0.0
        )
        intersection = intersection * live_rows[:, None] * occupied[None, :]
        return lax.dot_general(
            stacked, intersection, (((1,), (1,)), ((), ())), precision=lax.Precision.HIGHEST
        )

    starts = jnp.arange(width_all // row_block, dtype=jnp.int32) * row_block
    grouped = lax.map(row_group, starts)
    weighted = jnp.transpose(grouped, (1, 0, 2)).reshape(7, width_all)
    totals = weighted[6]
    return stiff_pair * (totals * position - weighted[0:3]) - damp_pair * (
        totals * velocity - weighted[3:6]
    )


def advance(sphere_block, forces):
    position = sphere_block[0:3]
    velocity = sphere_block[3:6]
    radius = sphere_block[6]
    occupied = radius > 0
    masses = jnp.where(occupied, radius * radius * radius, 1.0)
    falling = jnp.array([0.0, 0.0, gravity], jnp.float32)
    acceleration = forces / masses[None] - falling[:, None]
    velocity_new = velocity + time_step * acceleration
    position_new = position + time_step * velocity_new
    result = jnp.concatenate([position_new, velocity_new, radius[None]], 0)
    return jnp.where(occupied[None], result, 0.0)


def bin_total(partial_row):
    return lax.psum(partial_row, "bin")


def general(sph_state, sph_dest, body_list, tile_codes, triangles):
    sectors = lax.axis_size("sector")
    bins = lax.axis_size("bin")
    ndevices = sectors * bins
    leaving = sph_state.shape[1]
    capacity = 2 * leaving // ndevices
    targets = sph_dest[:, 0]
    onehot = (targets[:, None] == jnp.arange(ndevices, dtype=jnp.int32)[None, :]).astype(jnp.int32)
    ranks = jnp.sum((jnp.cumsum(onehot, 0) - 1) * onehot, 1)
    columns = targets * capacity + ranks
    outgoing = jnp.zeros((7, ndevices * capacity), jnp.float32).at[:, columns].set(sph_state)
    outgoing = outgoing.reshape(7, sectors, bins, capacity)
    arrived = lax.all_to_all(
        lax.all_to_all(outgoing, "sector", split_axis=1, concat_axis=1, tiled=True),
        "bin",
        split_axis=2,
        concat_axis=2,
        tiled=True,
    )
    sphere_block = arrived.reshape(7, ndevices * capacity)
    width_all = sphere_block.shape[1]
    coords = jnp.concatenate([sphere_block[0:3], sphere_block[6:7]], 0)
    pair_total = sphere_forces(sphere_block)
    everyone = lax.all_gather(triangles, "sector", axis=1, tiled=True)
    wall_total = jnp.zeros((3, width_all), jnp.float32)
    partial_value = jnp.zeros((sectors, 6), jnp.float32)
    for slot_index in range(body_list.shape[1]):
        owner_body = body_list[0, slot_index]
        facets = lax.dynamic_index_in_dim(everyone, owner_body, 1, keepdims=False)
        on_spheres, on_body = tile_forces(coords, facets, tile_codes[0, slot_index])
        wall_total = wall_total + on_spheres
        selector = (jnp.arange(sectors, dtype=jnp.int32) == owner_body).astype(jnp.float32)
        partial_value = partial_value + selector[:, None] * on_body[None, :]
    own_row = lax.psum_scatter(partial_value, "sector", scatter_dimension=0, tiled=True)
    own_row = bin_total(own_row)
    new_block = advance(sphere_block, pair_total + wall_total)
    scaling = jnp.array([time_step / body_mass] * 3 + [time_step / body_inertia] * 3, jnp.float32)
    return (new_block, own_row * scaling[None, :])


def local(sph_state, sph_dest, body_list, tile_codes, triangles):
    sectors = lax.axis_size("sector")
    ndevices = sectors * lax.axis_size("bin")
    leaving = sph_state.shape[1]
    fits = 2 * leaving == 64 * ndevices and 16 * leaving == LANES * LANES and sectors & (sectors - 1) == 0
    chosen = fast if fits else general
    return chosen(sph_state, sph_dest, body_list, tile_codes, triangles)


def solution(mesh):
    return jax.shard_map(
        local,
        mesh=mesh,
        in_specs=(
            P(None, ("sector", "bin")),
            P(("sector", "bin"), None),
            P(("sector", "bin"), None),
            P(("sector", "bin"), None, None),
            P(None, "sector", "bin"),
        ),
        out_specs=(P(None, ("sector", "bin")), P("sector", None)),
        check_vma=False,
    )
```

```python
import functools

import jax
import jax.numpy as jnp
from jax import lax
from jax.experimental import pallas as pl
from jax.experimental.pallas import tpu as pltpu
from jax.sharding import PartitionSpec as P

stiff_pair = 50.0
damp_pair = 2.0
stiff_wall = 50.0
time_step = 0.01
gravity = 9.81
body_mass = 4.0
body_inertia = 40.0

LANES = 128
PAYLOAD = ((0, 3), (1, 4), (2, 5), (6, None))
PAIR_BLOCK = 256
WALL_ROWS = 128


def iota(shape, dim):
    return lax.broadcasted_iota(jnp.int32, shape, dim)


def split3(x):
    hi = x.astype(jnp.bfloat16).astype(jnp.float32)
    rest = x - hi
    mid = rest.astype(jnp.bfloat16).astype(jnp.float32)
    return hi, mid, rest - mid


def dot(a, b, contract=((1,), (0,))):
    return lax.dot_general(a, b, (contract, ((), ())), preferred_element_type=jnp.float32)


def pack_kernel(dest_ref, state_ref, out_ref):
    blocks = dest_ref.shape[0]
    ndevices = out_ref.shape[0] * LANES // (8 * 64)
    capacity = 64
    dest = dest_ref[...]
    wide = blocks * ndevices
    expand = (iota((blocks, wide), 1) // ndevices == iota((blocks, wide), 0)).astype(jnp.bfloat16)
    dest_cols = jnp.transpose(dest.astype(jnp.float32)).astype(jnp.bfloat16)
    named = dot(dest_cols, expand)
    onehot = (named == (iota((LANES, wide), 1) % ndevices).astype(jnp.float32)).astype(jnp.float32)
    lower = (iota((LANES, LANES), 0) >= iota((LANES, LANES), 1)).astype(jnp.bfloat16)
    counted = dot(lower, onehot.astype(jnp.bfloat16))
    total = jnp.broadcast_to(counted[LANES - 1 :], (8, wide))
    before = jnp.zeros((8, wide), jnp.float32)
    for step in range(1, blocks):
        moved = pltpu.roll(total, step * ndevices, 1)
        before = before + jnp.where(iota((8, wide), 1) >= step * ndevices, moved, 0.0)
    place = (onehot * (counted - 1.0 + before[0:1])).astype(jnp.bfloat16)
    ranks = dot(expand, place, ((1,), (1,)))
    rank_row = jnp.concatenate([ranks[b : b + 1] for b in range(blocks)], 1)
    dest_row = jnp.concatenate([dest[b : b + 1] for b in range(blocks)], 1)
    leaving = blocks * LANES
    chosen = rank_row == iota((capacity, leaving), 0).astype(jnp.float32)
    to_dest = (dest_row == iota((ndevices, leaving), 0)).astype(jnp.float32).astype(jnp.bfloat16)
    out = None
    for part in split3(state_ref[...]):
        rows = []
        for pair in PAYLOAD:
            for source in pair:
                if source is None:
                    rows.append(jnp.zeros((capacity, leaving), jnp.bfloat16))
                else:
                    rows.append(jnp.where(chosen, part[source : source + 1], 0.0).astype(jnp.bfloat16))
        piece = dot(to_dest, jnp.concatenate(rows, 0), ((1,), (1,)))
        out = piece if out is None else out + piece
    groups = len(PAYLOAD)
    for k in range(groups):
        out_ref[pl.ds(k, ndevices, stride=groups), :] = out[:, k * LANES : (k + 1) * LANES]


def total_of(x):
    return jnp.sum(jnp.sum(x, 0, keepdims=True), 1, keepdims=True)


def state_tile(arrived_ref, tile):
    words = arrived_ref[8 * tile : 8 * tile + 8, :]
    swapped = pltpu.roll(pltpu.roll(words, 64, 1), 4, 0)
    same = (iota((8, LANES), 0) < 4) == (iota((8, LANES), 1) < 64)
    return jnp.where(same, words, swapped)


def facet_kernel(sectors, *refs):
    bodies_ref = refs[0]
    tri_refs = refs[1 : 1 + sectors]
    facet, raw, tri_sem = refs[1 + sectors :]
    entries = bodies_ref.shape[1]
    me = lax.axis_index("sector")

    def fetch(entry, source):
        return pltpu.make_async_copy(tri_refs[source], raw.at[entry], tri_sem.at[entry])

    for entry in range(entries):
        relative = bodies_ref[0, entry] ^ me
        for source in range(sectors):

            @pl.when(relative == source)
            def _():
                fetch(entry, source).start()

    for entry in range(entries):
        fetch(entry, 0).wait()
        corner = [raw[entry, i] for i in range(3)]
        one = [raw[entry, 3 + i] - corner[i] for i in range(3)]
        two = [raw[entry, 6 + i] - corner[i] for i in range(3)]
        d11 = one[0] * one[0] + one[1] * one[1] + one[2] * one[2]
        d12 = one[0] * two[0] + one[1] * two[1] + one[2] * two[2]
        d22 = two[0] * two[0] + two[1] * two[1] + two[2] * two[2]
        inverse = 1.0 / (d11 * d22 - d12 * d12)
        for i in range(3):
            facet[entry, i] = corner[i]
            facet[entry, 3 + i] = one[i]
            facet[entry, 6 + i] = two[i]
            facet[entry, 9 + i] = (d22 * one[i] - d12 * two[i]) * inverse
            facet[entry, 12 + i] = (d11 * two[i] - d12 * one[i]) * inverse


def wall_kernel(sectors, bins, *refs):
    bodies_ref, codes_ref, facet, arrived_ref, wrench_ref, force_ref, px, py, pz, rr, place, gathered = refs[:12]
    accs = refs[12:]
    entries = bodies_ref.shape[1]
    codes = codes_ref.shape[2]
    tiles_tri = facet.shape[2]
    tiles = arrived_ref.shape[0] // 8

    turned = jnp.transpose(arrived_ref[...])[0:64]
    squared = turned * turned
    for q in range(2 * tiles):
        at = slice(64 * q, 64 * q + 64)
        for ref, source, i in ((px, turned, 0), (py, turned, 1), (pz, turned, 2), (rr, squared, 3)):
            lane = 4 * q + i
            ref[at, :] = jnp.broadcast_to(source[:, lane : lane + 1], (64, LANES))
    for tile in range(tiles):
        state = state_tile(arrived_ref, tile)
        for i in range(3):
            place[i, tile : tile + 1, :] = state[i : i + 1]

    for acc in accs:
        acc[...] = jnp.zeros_like(acc)

    def one_tile(entry, number):
        code = codes_ref[0, entry, number]
        first = pl.multiple_of(code // tiles_tri * LANES, LANES)
        facet_tile = code % tiles_tri
        f = [facet[entry, i, pl.ds(facet_tile, 1), :] for i in range(15)]
        for part in range(LANES // WALL_ROWS):
            at = pl.ds(pl.multiple_of(first + part * WALL_ROWS, WALL_ROWS), WALL_ROWS)
            dx, dy, dz = px[at, :] - f[0], py[at, :] - f[1], pz[at, :] - f[2]
            beta = dx * f[9] + dy * f[10] + dz * f[11]
            gamma = dx * f[12] + dy * f[13] + dz * f[14]
            alpha = jnp.maximum(1.0 - beta - gamma, 0.0)
            beta = jnp.maximum(beta, 0.0)
            gamma = jnp.maximum(gamma, 0.0)
            scale = 1.0 / (alpha + beta + gamma)
            beta = beta * scale
            gamma = gamma * scale
            ox = dx - beta * f[3] - gamma * f[6]
            oy = dy - beta * f[4] - gamma * f[7]
            oz = dz - beta * f[5] - gamma * f[8]
            deep = jnp.maximum(rr[at, :] - (ox * ox + oy * oy + oz * oz), 0.0)
            accs[3 * entry][at, :] += deep * ox
            accs[3 * entry + 1][at, :] += deep * oy
            accs[3 * entry + 2][at, :] += deep * oz

    def step(number, carry):
        for entry in range(entries):
            one_tile(entry, number)
        return carry

    lax.fori_loop(0, codes, step, 0)

    def gather(tile, carry):
        at = pl.ds(pl.multiple_of(tile * LANES, LANES), LANES)
        for which in range(3 * entries):
            row = jnp.sum(jnp.transpose(accs[which][at, :]), 0, keepdims=True)
            gathered[which, pl.ds(tile, 1), :] = row
        return carry

    lax.fori_loop(0, tiles, gather, 0)
    x, y, z = place[0], place[1], place[2]
    owner = iota((sectors * bins, LANES), 0) // bins
    lane = iota((1, LANES), 1)
    out = jnp.zeros((sectors * bins, LANES), jnp.float32)
    whole = [0.0, 0.0, 0.0]
    for entry in range(entries):
        fx, fy, fz = (gathered[3 * entry + i] for i in range(3))
        parts = (fx, fy, fz, y * fz - z * fy, z * fx - x * fz, x * fy - y * fx)
        mine = jnp.zeros((1, LANES), jnp.float32)
        for i, part in enumerate(parts):
            scale = time_step / (body_mass if i < 3 else body_inertia)
            mine = jnp.where(lane == i, total_of(part) * scale, mine)
        out = out + jnp.where(owner == bodies_ref[0, entry], mine * (-stiff_wall), 0.0)
        whole = [whole[0] + fx, whole[1] + fy, whole[2] + fz]
    wrench_ref[...] = out
    for i in range(3):
        force_ref[i] = stiff_wall * whole[i]


def pair_kernel(arrived_ref, force_ref, out_hbm, left, right, moved, out_ref, out_sem):
    tiles = arrived_ref.shape[0] // 8
    blocks = tiles * LANES // PAIR_BLOCK
    row8 = iota((8, LANES), 0)
    for tile in range(tiles):
        at = slice(tile * LANES, (tile + 1) * LANES)
        state = state_tile(arrived_ref, tile)
        square = state * state
        level = square[3:4] - (square[0:1] + square[1:2] + square[2:3])
        other = jnp.where(state[3:4] > 0.0, level, -3.0e38)
        i_side = jnp.where(row8 < 4, 2.0 * state, jnp.where(row8 == 4, level, jnp.where(row8 == 5, 1.0, 0.0)))
        j_side = jnp.where(row8 < 4, state, jnp.where(row8 == 4, 1.0, jnp.where(row8 == 5, other, 0.0)))
        ih, im, il = split3(i_side)
        jh, jm, jl = split3(j_side)
        right[:, at] = jnp.concatenate([ih, ih, im, ih, il, im], 0).astype(jnp.bfloat16)
        left[at, 0:48] = jnp.transpose(jnp.concatenate([jh, jm, jh, jl, jh, jm], 0)).astype(jnp.bfloat16)
        value = jnp.where(row8 == 3, 1.0, state)
        moved[:, at] = jnp.concatenate(list(split3(value)) + [jnp.zeros((8, LANES), jnp.float32)], 0).astype(
            jnp.bfloat16
        )

    def block_of(ib, carry):
        columns = pl.ds(pl.multiple_of(ib * PAIR_BLOCK, PAIR_BLOCK), PAIR_BLOCK)
        mine = right[:, columns]
        total = jnp.zeros((32, PAIR_BLOCK), jnp.float32)
        for jb in range(blocks):
            rows = slice(jb * PAIR_BLOCK, (jb + 1) * PAIR_BLOCK)
            weight = jnp.maximum(dot(left[rows, 0:48], mine), 0.0)
            high = weight.astype(jnp.bfloat16)
            low = (weight - high.astype(jnp.float32)).astype(jnp.bfloat16)
            values = moved[:, rows]
            total = total + (dot(values, high) + dot(values, low))
        total = total[0:8] + total[8:16] + total[16:24]
        for part in range(PAIR_BLOCK // LANES):
            tile = ib * (PAIR_BLOCK // LANES) + part
            words = arrived_ref[pl.ds(pl.multiple_of(8 * tile, 8), 8), :]
            swapped = pltpu.roll(pltpu.roll(words, 64, 1), 4, 0)
            state = jnp.where((row8 < 4) == (iota((8, LANES), 1) < 64), words, swapped)
            moment = total[:, part * LANES : (part + 1) * LANES]
            differ = moment[3:4] * state - moment
            force = stiff_pair * differ - damp_pair * pltpu.roll(differ, 4, 0)
            for i in range(3):
                force = force + jnp.where(row8 == i, force_ref[i, pl.ds(tile, 1), :], 0.0)
            radius = jnp.broadcast_to(state[3:4], (8, LANES))
            live = radius > 0.0
            mass = jnp.where(live, radius * radius * radius, 1.0)
            falling = jnp.where(row8 == 6, gravity, 0.0)
            speed = state + time_step * (pltpu.roll(force, 4, 0) / mass - falling)
            place = state + time_step * pltpu.roll(speed, 4, 0)
            result = jnp.where(
                row8 < 3, place, jnp.where(row8 < 6, pltpu.roll(speed, 7, 0), pltpu.roll(state, 3, 0))
            )
            result = jnp.where(live, result, 0.0)
            out_ref[:, pl.ds(pl.multiple_of(tile * LANES, LANES), LANES)] = result[0:7]
        leave(ib).start()
        return carry

    def leave(ib):
        columns = pl.ds(pl.multiple_of(ib * PAIR_BLOCK, PAIR_BLOCK), PAIR_BLOCK)
        return pltpu.make_async_copy(out_ref.at[:, columns], out_hbm.at[:, columns], out_sem.at[ib])

    lax.fori_loop(0, blocks, block_of, 0)
    for ib in range(blocks):
        leave(ib).wait()


def whole_vmem():
    return pl.BlockSpec(memory_space=pltpu.VMEM)


def whole_smem():
    return pl.BlockSpec(memory_space=pltpu.SMEM)


def near(x):
    return pltpu.with_memory_space_constraint(x, pltpu.VMEM)


def fast(sph_state, sph_dest, body_list, tile_codes, triangles):
    sectors = lax.axis_size("sector")
    bins = lax.axis_size("bin")
    ndevices = sectors * bins
    leaving = sph_state.shape[1]
    slots = 2 * leaving
    words = 8 * slots // LANES
    block = triangles.reshape(triangles.shape[0], -1, LANES)
    blocks = [block] + [
        lax.ppermute(block, "sector", [(i, i ^ step) for i in range(sectors)]) for step in range(1, sectors)
    ]
    outgoing = pl.pallas_call(
        pack_kernel,
        out_shape=pltpu.VMEM((words, LANES), jnp.float32),
        in_specs=[whole_vmem(), whole_vmem()],
        out_specs=whole_vmem(),
        name="pack",
    )(sph_dest.reshape(-1, LANES), sph_state)
    outgoing = outgoing.reshape(ndevices, 1, words * LANES // ndevices)
    arrived = lax.all_to_all(outgoing, ("sector", "bin"), split_axis=0, concat_axis=0, tiled=True)
    arrived = arrived.reshape(words, LANES)
    entries = body_list.shape[1]
    column = pltpu.VMEM((slots, LANES), jnp.float32)
    tiles = slots // LANES
    facets = pl.pallas_call(
        functools.partial(facet_kernel, sectors),
        out_shape=pltpu.VMEM((entries, 15) + block.shape[1:], jnp.float32),
        in_specs=[whole_smem(), pl.BlockSpec(memory_space=pltpu.HBM)] + [whole_vmem()] * (sectors - 1),
        out_specs=whole_vmem(),
        scratch_shapes=[pltpu.VMEM((entries,) + block.shape, jnp.float32), pltpu.SemaphoreType.DMA((entries,))],
        name="facet",
    )(body_list, blocks[0], *[near(other) for other in blocks[1:]])
    wrench, force = pl.pallas_call(
        functools.partial(wall_kernel, sectors, bins),
        out_shape=[
            pltpu.VMEM((ndevices, LANES), jnp.float32),
            pltpu.VMEM((3, tiles, LANES), jnp.float32),
        ],
        in_specs=[whole_smem(), whole_smem(), whole_vmem(), whole_vmem()],
        out_specs=[whole_vmem()] * 2,
        scratch_shapes=[
            column,
            column,
            column,
            column,
            pltpu.VMEM((3, tiles, LANES), jnp.float32),
            pltpu.VMEM((3 * entries, tiles, LANES), jnp.float32),
        ]
        + [column] * (3 * entries),
        name="wall",
    )(body_list, tile_codes, near(facets), near(arrived))
    shared = lax.all_to_all(
        wrench.reshape(ndevices, 1, LANES), ("sector", "bin"), split_axis=0, concat_axis=0, tiled=True
    )
    new_block = pl.pallas_call(
        pair_kernel,
        out_shape=jax.ShapeDtypeStruct((7, slots), jnp.float32),
        in_specs=[whole_vmem(), whole_vmem()],
        out_specs=pl.BlockSpec(memory_space=pltpu.HBM),
        scratch_shapes=[
            pltpu.VMEM((slots, LANES), jnp.bfloat16),
            pltpu.VMEM((48, slots), jnp.bfloat16),
            pltpu.VMEM((32, slots), jnp.bfloat16),
            pltpu.VMEM((7, slots), jnp.float32),
            pltpu.SemaphoreType.DMA((slots // PAIR_BLOCK,)),
        ],
        name="pair",
    )(near(arrived), near(force))
    kick = jnp.sum(shared[:, 0, :6], 0, keepdims=True)
    return new_block, kick


def contact(spheres, facets):
    centre = spheres[0:3]
    radius = spheres[3]
    corner = facets[0:3]
    edge_one = facets[3:6] - corner
    edge_two = facets[6:9] - corner
    square_one = jnp.sum(edge_one * edge_one, 0)
    square_two = jnp.sum(edge_two * edge_two, 0)
    cross_term = jnp.sum(edge_one * edge_two, 0)
    inverse = 1.0 / (square_one * square_two - cross_term * cross_term)
    relative = centre[:, :, None] - corner[:, None, :]
    along_one = jnp.sum(relative * edge_one[:, None, :], 0)
    along_two = jnp.sum(relative * edge_two[:, None, :], 0)
    weight_b = (square_two * along_one - cross_term * along_two) * inverse
    weight_c = (square_one * along_two - cross_term * along_one) * inverse
    weight_a = jnp.maximum(1.0 - weight_b - weight_c, 0.0)
    weight_b = jnp.maximum(weight_b, 0.0)
    weight_c = jnp.maximum(weight_c, 0.0)
    totals = weight_a + weight_b + weight_c
    weight_b = weight_b / totals
    weight_c = weight_c / totals
    nearest = (
        corner[:, None, :]
        + weight_b[None] * edge_one[:, None, :]
        + weight_c[None] * edge_two[:, None, :]
    )
    offset = centre[:, :, None] - nearest
    squared = jnp.sum(offset * offset, 0)
    strength = stiff_wall * jnp.maximum(radius[:, None] * radius[:, None] - squared, 0.0)
    forces = strength[None] * offset
    on_spheres = jnp.sum(forces, 2)
    on_body = -jnp.sum(forces, (1, 2))
    torque = -jnp.sum(jnp.cross(nearest, forces, axis=0), (1, 2))
    return (on_spheres, jnp.concatenate([on_body, torque]))


def tile_forces(spheres, facets, tile_list):
    tiles_tri = facets.shape[1] // 128

    def advance_tile(carried, tile_code):
        forces, wrench = carried
        sphere_tile = tile_code // tiles_tri
        facet_tile = tile_code % tiles_tri
        sphere_part = lax.dynamic_slice_in_dim(spheres, sphere_tile * 128, 128, 1)
        facet_part = lax.dynamic_slice_in_dim(facets, facet_tile * 128, 128, 1)
        on_spheres, on_body = contact(sphere_part, facet_part)
        current = lax.dynamic_slice_in_dim(forces, sphere_tile * 128, 128, 1)
        forces = lax.dynamic_update_slice_in_dim(forces, current + on_spheres, sphere_tile * 128, 1)
        return ((forces, wrench + on_body), None)

    initial = (jnp.zeros((3, spheres.shape[1]), jnp.float32), jnp.zeros((6,), jnp.float32))
    (forces, wrench), unused = lax.scan(advance_tile, initial, tile_list)
    return (forces, wrench)


def sphere_forces(sphere_block):
    position = sphere_block[0:3]
    velocity = sphere_block[3:6]
    radius = sphere_block[6]
    width_all = sphere_block.shape[1]
    occupied = (radius > 0).astype(jnp.float32)
    coords = jnp.concatenate([position, radius[None]], 0)
    baseline = radius * radius - jnp.sum(position * position, 0)
    stacked = jnp.concatenate([position, velocity, jnp.ones((1, width_all), jnp.float32)], 0)
    row_block = 512

    def row_group(row_start):
        coords_rows = lax.dynamic_slice_in_dim(coords, row_start, row_block, 1)
        base_rows = lax.dynamic_slice_in_dim(baseline, row_start, row_block, 0)
        live_rows = lax.dynamic_slice_in_dim(occupied, row_start, row_block, 0)
        inner_products = lax.dot_general(
            coords_rows, coords, (((0,), (0,)), ((), ())), precision=lax.Precision.HIGHEST
        )
        intersection = jnp.maximum(
            base_rows[:, None] + baseline[None, :] + 2.0 * inner_products, 0.0
        )
        intersection = intersection * live_rows[:, None] * occupied[None, :]
        return lax.dot_general(
            stacked, intersection, (((1,), (1,)), ((), ())), precision=lax.Precision.HIGHEST
        )

    starts = jnp.arange(width_all // row_block, dtype=jnp.int32) * row_block
    grouped = lax.map(row_group, starts)
    weighted = jnp.transpose(grouped, (1, 0, 2)).reshape(7, width_all)
    totals = weighted[6]
    return stiff_pair * (totals * position - weighted[0:3]) - damp_pair * (
        totals * velocity - weighted[3:6]
    )


def advance(sphere_block, forces):
    position = sphere_block[0:3]
    velocity = sphere_block[3:6]
    radius = sphere_block[6]
    occupied = radius > 0
    masses = jnp.where(occupied, radius * radius * radius, 1.0)
    falling = jnp.array([0.0, 0.0, gravity], jnp.float32)
    acceleration = forces / masses[None] - falling[:, None]
    velocity_new = velocity + time_step * acceleration
    position_new = position + time_step * velocity_new
    result = jnp.concatenate([position_new, velocity_new, radius[None]], 0)
    return jnp.where(occupied[None], result, 0.0)


def bin_total(partial_row):
    return lax.psum(partial_row, "bin")


def general(sph_state, sph_dest, body_list, tile_codes, triangles):
    sectors = lax.axis_size("sector")
    bins = lax.axis_size("bin")
    ndevices = sectors * bins
    leaving = sph_state.shape[1]
    capacity = 2 * leaving // ndevices
    targets = sph_dest[:, 0]
    onehot = (targets[:, None] == jnp.arange(ndevices, dtype=jnp.int32)[None, :]).astype(jnp.int32)
    ranks = jnp.sum((jnp.cumsum(onehot, 0) - 1) * onehot, 1)
    columns = targets * capacity + ranks
    outgoing = jnp.zeros((7, ndevices * capacity), jnp.float32).at[:, columns].set(sph_state)
    outgoing = outgoing.reshape(7, sectors, bins, capacity)
    arrived = lax.all_to_all(
        lax.all_to_all(outgoing, "sector", split_axis=1, concat_axis=1, tiled=True),
        "bin",
        split_axis=2,
        concat_axis=2,
        tiled=True,
    )
    sphere_block = arrived.reshape(7, ndevices * capacity)
    width_all = sphere_block.shape[1]
    coords = jnp.concatenate([sphere_block[0:3], sphere_block[6:7]], 0)
    pair_total = sphere_forces(sphere_block)
    everyone = lax.all_gather(triangles, "sector", axis=1, tiled=True)
    wall_total = jnp.zeros((3, width_all), jnp.float32)
    partial_value = jnp.zeros((sectors, 6), jnp.float32)
    for slot_index in range(body_list.shape[1]):
        owner_body = body_list[0, slot_index]
        facets = lax.dynamic_index_in_dim(everyone, owner_body, 1, keepdims=False)
        on_spheres, on_body = tile_forces(coords, facets, tile_codes[0, slot_index])
        wall_total = wall_total + on_spheres
        selector = (jnp.arange(sectors, dtype=jnp.int32) == owner_body).astype(jnp.float32)
        partial_value = partial_value + selector[:, None] * on_body[None, :]
    own_row = lax.psum_scatter(partial_value, "sector", scatter_dimension=0, tiled=True)
    own_row = bin_total(own_row)
    new_block = advance(sphere_block, pair_total + wall_total)
    scaling = jnp.array([time_step / body_mass] * 3 + [time_step / body_inertia] * 3, jnp.float32)
    return (new_block, own_row * scaling[None, :])


def local(sph_state, sph_dest, body_list, tile_codes, triangles):
    sectors = lax.axis_size("sector")
    ndevices = sectors * lax.axis_size("bin")
    leaving = sph_state.shape[1]
    fits = 2 * leaving == 64 * ndevices and 16 * leaving == LANES * LANES and sectors & (sectors - 1) == 0
    chosen = fast if fits else general
    return chosen(sph_state, sph_dest, body_list, tile_codes, triangles)


def solution(mesh):
    return jax.shard_map(
        local,
        mesh=mesh,
        in_specs=(
            P(None, ("sector", "bin")),
            P(("sector", "bin"), None),
            P(("sector", "bin"), None),
            P(("sector", "bin"), None, None),
            P(None, "sector", "bin"),
        ),
        out_specs=(P(None, ("sector", "bin")), P("sector", None)),
        check_vma=False,
    )
```

```python
import functools

import jax
import jax.numpy as jnp
from jax import lax
from jax.experimental import pallas as pl
from jax.experimental.pallas import tpu as pltpu
from jax.sharding import PartitionSpec as P

stiff_pair = 50.0
damp_pair = 2.0
stiff_wall = 50.0
time_step = 0.01
gravity = 9.81
body_mass = 4.0
body_inertia = 40.0

LANES = 128
PAYLOAD = ((0, 3), (1, 4), (2, 5), (6, None))
PAIR_BLOCK = 256
SPREAD = 4


def iota(shape, dim):
    return lax.broadcasted_iota(jnp.int32, shape, dim)


def split3(x):
    hi = x.astype(jnp.bfloat16).astype(jnp.float32)
    rest = x - hi
    mid = rest.astype(jnp.bfloat16).astype(jnp.float32)
    return hi, mid, rest - mid


def dot(a, b, contract=((1,), (0,))):
    return lax.dot_general(a, b, (contract, ((), ())), preferred_element_type=jnp.float32)


def pack_kernel(dest_ref, state_ref, out_ref):
    blocks = dest_ref.shape[0]
    ndevices = out_ref.shape[0] * LANES // (8 * 64)
    capacity = 64
    dest = dest_ref[...]
    wide = blocks * ndevices
    expand = (iota((blocks, wide), 1) // ndevices == iota((blocks, wide), 0)).astype(jnp.bfloat16)
    dest_cols = jnp.transpose(dest.astype(jnp.float32)).astype(jnp.bfloat16)
    named = dot(dest_cols, expand)
    onehot = (named == (iota((LANES, wide), 1) % ndevices).astype(jnp.float32)).astype(jnp.float32)
    lower = (iota((LANES, LANES), 0) >= iota((LANES, LANES), 1)).astype(jnp.bfloat16)
    counted = dot(lower, onehot.astype(jnp.bfloat16))
    total = jnp.broadcast_to(counted[LANES - 1 :], (8, wide))
    before = jnp.zeros((8, wide), jnp.float32)
    for step in range(1, blocks):
        moved = pltpu.roll(total, step * ndevices, 1)
        before = before + jnp.where(iota((8, wide), 1) >= step * ndevices, moved, 0.0)
    place = (onehot * (counted - 1.0 + before[0:1])).astype(jnp.bfloat16)
    ranks = dot(expand, place, ((1,), (1,)))
    rank_row = jnp.concatenate([ranks[b : b + 1] for b in range(blocks)], 1)
    dest_row = jnp.concatenate([dest[b : b + 1] for b in range(blocks)], 1)
    leaving = blocks * LANES
    chosen = rank_row == iota((capacity, leaving), 0).astype(jnp.float32)
    to_dest = (dest_row == iota((ndevices, leaving), 0)).astype(jnp.float32).astype(jnp.bfloat16)
    out = None
    for part in split3(state_ref[...]):
        rows = []
        for pair in PAYLOAD:
            for source in pair:
                if source is None:
                    rows.append(jnp.zeros((capacity, leaving), jnp.bfloat16))
                else:
                    rows.append(jnp.where(chosen, part[source : source + 1], 0.0).astype(jnp.bfloat16))
        piece = dot(to_dest, jnp.concatenate(rows, 0), ((1,), (1,)))
        out = piece if out is None else out + piece
    groups = len(PAYLOAD)
    for k in range(groups):
        out_ref[pl.ds(k, ndevices, stride=groups), :] = out[:, k * LANES : (k + 1) * LANES]


def quotient(code, size):
    power = size & (size - 1) == 0
    return lax.shift_right_logical(code, size.bit_length() - 1) if power else lax.div(code, size)


def remainder(code, size):
    return code & (size - 1) if size & (size - 1) == 0 else lax.rem(code, size)


def total_of(x):
    return jnp.sum(jnp.sum(x, 0, keepdims=True), 1, keepdims=True)


def state_tile(arrived_ref, tile):
    words = arrived_ref[8 * tile : 8 * tile + 8, :]
    swapped = pltpu.roll(pltpu.roll(words, 64, 1), 4, 0)
    same = (iota((8, LANES), 0) < 4) == (iota((8, LANES), 1) < 64)
    return jnp.where(same, words, swapped)


def facet_kernel(sectors, *refs):
    bodies_ref = refs[0]
    tri_refs = refs[1 : 1 + sectors]
    facet, raw, tri_sem = refs[1 + sectors :]
    entries = bodies_ref.shape[1]
    me = lax.axis_index("sector")

    def fetch(entry, source):
        return pltpu.make_async_copy(tri_refs[source], raw.at[entry], tri_sem.at[entry])

    for entry in range(entries):
        relative = bodies_ref[0, entry] ^ me
        for source in range(sectors):

            @pl.when(relative == source)
            def _():
                fetch(entry, source).start()

    for entry in range(entries):
        fetch(entry, 0).wait()
        corner = [raw[entry, i] for i in range(3)]
        one = [raw[entry, 3 + i] - corner[i] for i in range(3)]
        two = [raw[entry, 6 + i] - corner[i] for i in range(3)]
        d11 = one[0] * one[0] + one[1] * one[1] + one[2] * one[2]
        d12 = one[0] * two[0] + one[1] * two[1] + one[2] * two[2]
        d22 = two[0] * two[0] + two[1] * two[1] + two[2] * two[2]
        inverse = 1.0 / (d11 * d22 - d12 * d12)
        for i in range(3):
            facet[entry, i] = corner[i]
            facet[entry, 3 + i] = one[i]
            facet[entry, 6 + i] = two[i]
            facet[entry, 9 + i] = (d22 * one[i] - d12 * two[i]) * inverse
            facet[entry, 12 + i] = (d11 * two[i] - d12 * one[i]) * inverse


def sphere_side(state, row8):
    square = state * state
    level = square[3:4] - (square[0:1] + square[1:2] + square[2:3])
    other = jnp.where(state[3:4] > 0.0, level, -3.0e38)
    return level, jnp.where(
        row8 < 4, state, jnp.where(row8 == 4, 1.0, jnp.where(row8 == 5, other, jnp.where(row8 == 6, square[3:4], 0.0)))
    )


def wall_kernel(sectors, bins, *refs):
    bodies_ref, codes_ref, facet, arrived_ref, wrench_ref, force_ref, left = refs[:7]
    spread, place, gathered = refs[7:10]
    accs = refs[10:]
    entries = bodies_ref.shape[1]
    codes = codes_ref.shape[2]
    tiles_tri = facet.shape[2]
    tiles = arrived_ref.shape[0] // 8
    row8 = iota((8, LANES), 0)

    wanted = iota((48, 4 * LANES), 1) // LANES
    wanted = jnp.where(wanted == 3, 6, wanted)
    row = iota((48, 4 * LANES), 0)
    select = (row % 8 == wanted) & ((row // 8 == 0) | (row // 8 == 1) | (row // 8 == 3))
    select = select.astype(jnp.float32).astype(jnp.bfloat16)
    for tile in range(tiles):
        at = slice(tile * LANES, (tile + 1) * LANES)
        state = state_tile(arrived_ref, tile)
        jh, jm, jl = split3(sphere_side(state, row8)[1])
        left[at, 0:48] = jnp.transpose(jnp.concatenate([jh, jm, jh, jl, jh, jm], 0)).astype(jnp.bfloat16)
        for i in range(3):
            place[i, tile : tile + 1, :] = state[i : i + 1]
    for group in range(tiles // SPREAD):
        at = slice(group * SPREAD * LANES, (group + 1) * SPREAD * LANES)
        wide = dot(left[at, 0:48], select)
        for i in range(4):
            spread[i, at, :] = wide[:, i * LANES : (i + 1) * LANES]
    for acc in accs:
        acc[...] = jnp.zeros_like(acc)

    def one_tile(entry, number):
        code = codes_ref[0, entry, number]
        first = pl.multiple_of(quotient(code, tiles_tri) * LANES, LANES)
        facet_tile = remainder(code, tiles_tri)
        f = [facet[entry, i, pl.ds(facet_tile, 1), :] for i in range(15)]
        at = pl.ds(first, LANES)
        dx, dy, dz = spread[0, at, :] - f[0], spread[1, at, :] - f[1], spread[2, at, :] - f[2]
        beta = dx * f[9] + dy * f[10] + dz * f[11]
        gamma = dx * f[12] + dy * f[13] + dz * f[14]
        alpha = jnp.maximum(1.0 - beta - gamma, 0.0)
        beta = jnp.maximum(beta, 0.0)
        gamma = jnp.maximum(gamma, 0.0)
        scale = 1.0 / (alpha + beta + gamma)
        beta = beta * scale
        gamma = gamma * scale
        ox = dx - beta * f[3] - gamma * f[6]
        oy = dy - beta * f[4] - gamma * f[7]
        oz = dz - beta * f[5] - gamma * f[8]
        deep = jnp.maximum(spread[3, at, :] - (ox * ox + oy * oy + oz * oz), 0.0)
        accs[3 * entry][at, :] += deep * ox
        accs[3 * entry + 1][at, :] += deep * oy
        accs[3 * entry + 2][at, :] += deep * oz

    def step(number, carry):
        for entry in range(entries):
            one_tile(entry, number)
        return carry

    lax.fori_loop(0, codes, step, 0)

    ones = jnp.ones((16, 2 * LANES), jnp.bfloat16)

    def gather(tile, carry):
        at = pl.ds(pl.multiple_of(tile * LANES, LANES), LANES)
        for which in range(3 * entries):
            value = accs[which][at, :]
            high = value.astype(jnp.bfloat16)
            low = (value - high.astype(jnp.float32)).astype(jnp.bfloat16)
            row = dot(ones, jnp.concatenate([high, low], 1), ((1,), (1,)))
            gathered[which, pl.ds(tile, 1), :] = row[0:1]
        return carry

    lax.fori_loop(0, tiles, gather, 0, unroll=2)
    x, y, z = place[0], place[1], place[2]
    owner = iota((sectors * bins, LANES), 0) // bins
    lane = iota((1, LANES), 1)
    out = jnp.zeros((sectors * bins, LANES), jnp.float32)
    whole = [0.0, 0.0, 0.0]
    for entry in range(entries):
        fx, fy, fz = (gathered[3 * entry + i] for i in range(3))
        parts = (fx, fy, fz, y * fz - z * fy, z * fx - x * fz, x * fy - y * fx)
        mine = jnp.zeros((1, LANES), jnp.float32)
        for i, part in enumerate(parts):
            scale = time_step / (body_mass if i < 3 else body_inertia)
            mine = jnp.where(lane == i, total_of(part) * scale, mine)
        out = out + jnp.where(owner == bodies_ref[0, entry], mine * (-stiff_wall), 0.0)
        whole = [whole[0] + fx, whole[1] + fy, whole[2] + fz]
    wrench_ref[...] = out
    for i in range(3):
        force_ref[i] = stiff_wall * whole[i]


def pair_kernel(arrived_ref, force_ref, left, out_hbm, right, moved, out_ref, out_sem):
    tiles = arrived_ref.shape[0] // 8
    blocks = tiles * LANES // PAIR_BLOCK
    row8 = iota((8, LANES), 0)
    for tile in range(tiles):
        at = slice(tile * LANES, (tile + 1) * LANES)
        state = state_tile(arrived_ref, tile)
        level = sphere_side(state, row8)[0]
        i_side = jnp.where(row8 < 4, 2.0 * state, jnp.where(row8 == 4, level, jnp.where(row8 == 5, 1.0, 0.0)))
        ih, im, il = split3(i_side)
        right[:, at] = jnp.concatenate([ih, ih, im, ih, il, im], 0).astype(jnp.bfloat16)
        value = jnp.where(row8 == 3, 1.0, state)
        moved[:, at] = jnp.concatenate(list(split3(value)) + [jnp.zeros((8, LANES), jnp.float32)], 0).astype(
            jnp.bfloat16
        )

    def block_of(ib, carry):
        columns = pl.ds(pl.multiple_of(ib * PAIR_BLOCK, PAIR_BLOCK), PAIR_BLOCK)
        mine = right[:, columns]
        total = jnp.zeros((32, PAIR_BLOCK), jnp.float32)
        for jb in range(blocks):
            rows = slice(jb * PAIR_BLOCK, (jb + 1) * PAIR_BLOCK)
            weight = jnp.maximum(dot(left[rows, 0:48], mine), 0.0)
            high = weight.astype(jnp.bfloat16)
            low = (weight - high.astype(jnp.float32)).astype(jnp.bfloat16)
            values = moved[:, rows]
            total = total + (dot(values, high) + dot(values, low))
        total = total[0:8] + total[8:16] + total[16:24]
        for part in range(PAIR_BLOCK // LANES):
            tile = ib * (PAIR_BLOCK // LANES) + part
            words = arrived_ref[pl.ds(pl.multiple_of(8 * tile, 8), 8), :]
            swapped = pltpu.roll(pltpu.roll(words, 64, 1), 4, 0)
            state = jnp.where((row8 < 4) == (iota((8, LANES), 1) < 64), words, swapped)
            moment = total[:, part * LANES : (part + 1) * LANES]
            differ = moment[3:4] * state - moment
            force = stiff_pair * differ - damp_pair * pltpu.roll(differ, 4, 0)
            for i in range(3):
                force = force + jnp.where(row8 == i, force_ref[i, pl.ds(tile, 1), :], 0.0)
            radius = jnp.broadcast_to(state[3:4], (8, LANES))
            live = radius > 0.0
            mass = jnp.where(live, radius * radius * radius, 1.0)
            falling = jnp.where(row8 == 6, gravity, 0.0)
            speed = state + time_step * (pltpu.roll(force, 4, 0) / mass - falling)
            place = state + time_step * pltpu.roll(speed, 4, 0)
            result = jnp.where(
                row8 < 3, place, jnp.where(row8 < 6, pltpu.roll(speed, 7, 0), pltpu.roll(state, 3, 0))
            )
            result = jnp.where(live, result, 0.0)
            out_ref[:, pl.ds(pl.multiple_of(tile * LANES, LANES), LANES)] = result[0:7]
        leave(ib).start()
        return carry

    def leave(ib):
        columns = pl.ds(pl.multiple_of(ib * PAIR_BLOCK, PAIR_BLOCK), PAIR_BLOCK)
        return pltpu.make_async_copy(out_ref.at[:, columns], out_hbm.at[:, columns], out_sem.at[ib])

    lax.fori_loop(0, blocks, block_of, 0)
    for ib in range(blocks):
        leave(ib).wait()


def whole_vmem():
    return pl.BlockSpec(memory_space=pltpu.VMEM)


def whole_smem():
    return pl.BlockSpec(memory_space=pltpu.SMEM)


def near(x):
    return pltpu.with_memory_space_constraint(x, pltpu.VMEM)


def fast(sph_state, sph_dest, body_list, tile_codes, triangles):
    sectors = lax.axis_size("sector")
    bins = lax.axis_size("bin")
    ndevices = sectors * bins
    leaving = sph_state.shape[1]
    slots = 2 * leaving
    words = 8 * slots // LANES
    block = triangles.reshape(triangles.shape[0], -1, LANES)
    blocks = [block] + [
        lax.ppermute(block, "sector", [(i, i ^ step) for i in range(sectors)]) for step in range(1, sectors)
    ]
    outgoing = pl.pallas_call(
        pack_kernel,
        out_shape=pltpu.VMEM((words, LANES), jnp.float32),
        in_specs=[whole_vmem(), whole_vmem()],
        out_specs=whole_vmem(),
        name="pack",
    )(sph_dest.reshape(-1, LANES), sph_state)
    outgoing = outgoing.reshape(ndevices, 1, words * LANES // ndevices)
    arrived = lax.all_to_all(outgoing, ("sector", "bin"), split_axis=0, concat_axis=0, tiled=True)
    arrived = arrived.reshape(words, LANES)
    entries = body_list.shape[1]
    column = pltpu.VMEM((slots, LANES), jnp.float32)
    tiles = slots // LANES
    facets = pl.pallas_call(
        functools.partial(facet_kernel, sectors),
        out_shape=pltpu.VMEM((entries, 15) + block.shape[1:], jnp.float32),
        in_specs=[whole_smem(), pl.BlockSpec(memory_space=pltpu.HBM)] + [whole_vmem()] * (sectors - 1),
        out_specs=whole_vmem(),
        scratch_shapes=[pltpu.VMEM((entries,) + block.shape, jnp.float32), pltpu.SemaphoreType.DMA((entries,))],
        name="facet",
    )(body_list, blocks[0], *[near(other) for other in blocks[1:]])
    wrench, force, left = pl.pallas_call(
        functools.partial(wall_kernel, sectors, bins),
        out_shape=[
            pltpu.VMEM((ndevices, LANES), jnp.float32),
            pltpu.VMEM((3, tiles, LANES), jnp.float32),
            pltpu.VMEM((slots, LANES), jnp.bfloat16),
        ],
        in_specs=[whole_smem(), whole_smem()] + [whole_vmem()] * 2,
        out_specs=[whole_vmem()] * 3,
        scratch_shapes=[
            pltpu.VMEM((4, slots, LANES), jnp.float32),
            pltpu.VMEM((3, tiles, LANES), jnp.float32),
            pltpu.VMEM((3 * entries, tiles, LANES), jnp.float32),
        ]
        + [column] * (3 * entries),
        name="wall",
    )(body_list, tile_codes, near(facets), near(arrived))
    shared = lax.all_to_all(
        wrench.reshape(ndevices, 1, LANES), ("sector", "bin"), split_axis=0, concat_axis=0, tiled=True
    )
    new_block = pl.pallas_call(
        pair_kernel,
        out_shape=jax.ShapeDtypeStruct((7, slots), jnp.float32),
        in_specs=[whole_vmem()] * 3,
        out_specs=pl.BlockSpec(memory_space=pltpu.HBM),
        scratch_shapes=[
            pltpu.VMEM((48, slots), jnp.bfloat16),
            pltpu.VMEM((32, slots), jnp.bfloat16),
            pltpu.VMEM((7, slots), jnp.float32),
            pltpu.SemaphoreType.DMA((slots // PAIR_BLOCK,)),
        ],
        name="pair",
    )(near(arrived), near(force), near(left))
    kick = jnp.sum(shared[:, 0, :6], 0, keepdims=True)
    return new_block, kick


def contact(spheres, facets):
    centre = spheres[0:3]
    radius = spheres[3]
    corner = facets[0:3]
    edge_one = facets[3:6] - corner
    edge_two = facets[6:9] - corner
    square_one = jnp.sum(edge_one * edge_one, 0)
    square_two = jnp.sum(edge_two * edge_two, 0)
    cross_term = jnp.sum(edge_one * edge_two, 0)
    inverse = 1.0 / (square_one * square_two - cross_term * cross_term)
    relative = centre[:, :, None] - corner[:, None, :]
    along_one = jnp.sum(relative * edge_one[:, None, :], 0)
    along_two = jnp.sum(relative * edge_two[:, None, :], 0)
    weight_b = (square_two * along_one - cross_term * along_two) * inverse
    weight_c = (square_one * along_two - cross_term * along_one) * inverse
    weight_a = jnp.maximum(1.0 - weight_b - weight_c, 0.0)
    weight_b = jnp.maximum(weight_b, 0.0)
    weight_c = jnp.maximum(weight_c, 0.0)
    totals = weight_a + weight_b + weight_c
    weight_b = weight_b / totals
    weight_c = weight_c / totals
    nearest = (
        corner[:, None, :]
        + weight_b[None] * edge_one[:, None, :]
        + weight_c[None] * edge_two[:, None, :]
    )
    offset = centre[:, :, None] - nearest
    squared = jnp.sum(offset * offset, 0)
    strength = stiff_wall * jnp.maximum(radius[:, None] * radius[:, None] - squared, 0.0)
    forces = strength[None] * offset
    on_spheres = jnp.sum(forces, 2)
    on_body = -jnp.sum(forces, (1, 2))
    torque = -jnp.sum(jnp.cross(nearest, forces, axis=0), (1, 2))
    return (on_spheres, jnp.concatenate([on_body, torque]))


def tile_forces(spheres, facets, tile_list):
    tiles_tri = facets.shape[1] // 128

    def advance_tile(carried, tile_code):
        forces, wrench = carried
        sphere_tile = tile_code // tiles_tri
        facet_tile = tile_code % tiles_tri
        sphere_part = lax.dynamic_slice_in_dim(spheres, sphere_tile * 128, 128, 1)
        facet_part = lax.dynamic_slice_in_dim(facets, facet_tile * 128, 128, 1)
        on_spheres, on_body = contact(sphere_part, facet_part)
        current = lax.dynamic_slice_in_dim(forces, sphere_tile * 128, 128, 1)
        forces = lax.dynamic_update_slice_in_dim(forces, current + on_spheres, sphere_tile * 128, 1)
        return ((forces, wrench + on_body), None)

    initial = (jnp.zeros((3, spheres.shape[1]), jnp.float32), jnp.zeros((6,), jnp.float32))
    (forces, wrench), unused = lax.scan(advance_tile, initial, tile_list)
    return (forces, wrench)


def sphere_forces(sphere_block):
    position = sphere_block[0:3]
    velocity = sphere_block[3:6]
    radius = sphere_block[6]
    width_all = sphere_block.shape[1]
    occupied = (radius > 0).astype(jnp.float32)
    coords = jnp.concatenate([position, radius[None]], 0)
    baseline = radius * radius - jnp.sum(position * position, 0)
    stacked = jnp.concatenate([position, velocity, jnp.ones((1, width_all), jnp.float32)], 0)
    row_block = 512

    def row_group(row_start):
        coords_rows = lax.dynamic_slice_in_dim(coords, row_start, row_block, 1)
        base_rows = lax.dynamic_slice_in_dim(baseline, row_start, row_block, 0)
        live_rows = lax.dynamic_slice_in_dim(occupied, row_start, row_block, 0)
        inner_products = lax.dot_general(
            coords_rows, coords, (((0,), (0,)), ((), ())), precision=lax.Precision.HIGHEST
        )
        intersection = jnp.maximum(
            base_rows[:, None] + baseline[None, :] + 2.0 * inner_products, 0.0
        )
        intersection = intersection * live_rows[:, None] * occupied[None, :]
        return lax.dot_general(
            stacked, intersection, (((1,), (1,)), ((), ())), precision=lax.Precision.HIGHEST
        )

    starts = jnp.arange(width_all // row_block, dtype=jnp.int32) * row_block
    grouped = lax.map(row_group, starts)
    weighted = jnp.transpose(grouped, (1, 0, 2)).reshape(7, width_all)
    totals = weighted[6]
    return stiff_pair * (totals * position - weighted[0:3]) - damp_pair * (
        totals * velocity - weighted[3:6]
    )


def advance(sphere_block, forces):
    position = sphere_block[0:3]
    velocity = sphere_block[3:6]
    radius = sphere_block[6]
    occupied = radius > 0
    masses = jnp.where(occupied, radius * radius * radius, 1.0)
    falling = jnp.array([0.0, 0.0, gravity], jnp.float32)
    acceleration = forces / masses[None] - falling[:, None]
    velocity_new = velocity + time_step * acceleration
    position_new = position + time_step * velocity_new
    result = jnp.concatenate([position_new, velocity_new, radius[None]], 0)
    return jnp.where(occupied[None], result, 0.0)


def bin_total(partial_row):
    return lax.psum(partial_row, "bin")


def general(sph_state, sph_dest, body_list, tile_codes, triangles):
    sectors = lax.axis_size("sector")
    bins = lax.axis_size("bin")
    ndevices = sectors * bins
    leaving = sph_state.shape[1]
    capacity = 2 * leaving // ndevices
    targets = sph_dest[:, 0]
    onehot = (targets[:, None] == jnp.arange(ndevices, dtype=jnp.int32)[None, :]).astype(jnp.int32)
    ranks = jnp.sum((jnp.cumsum(onehot, 0) - 1) * onehot, 1)
    columns = targets * capacity + ranks
    outgoing = jnp.zeros((7, ndevices * capacity), jnp.float32).at[:, columns].set(sph_state)
    outgoing = outgoing.reshape(7, sectors, bins, capacity)
    arrived = lax.all_to_all(
        lax.all_to_all(outgoing, "sector", split_axis=1, concat_axis=1, tiled=True),
        "bin",
        split_axis=2,
        concat_axis=2,
        tiled=True,
    )
    sphere_block = arrived.reshape(7, ndevices * capacity)
    width_all = sphere_block.shape[1]
    coords = jnp.concatenate([sphere_block[0:3], sphere_block[6:7]], 0)
    pair_total = sphere_forces(sphere_block)
    everyone = lax.all_gather(triangles, "sector", axis=1, tiled=True)
    wall_total = jnp.zeros((3, width_all), jnp.float32)
    partial_value = jnp.zeros((sectors, 6), jnp.float32)
    for slot_index in range(body_list.shape[1]):
        owner_body = body_list[0, slot_index]
        facets = lax.dynamic_index_in_dim(everyone, owner_body, 1, keepdims=False)
        on_spheres, on_body = tile_forces(coords, facets, tile_codes[0, slot_index])
        wall_total = wall_total + on_spheres
        selector = (jnp.arange(sectors, dtype=jnp.int32) == owner_body).astype(jnp.float32)
        partial_value = partial_value + selector[:, None] * on_body[None, :]
    own_row = lax.psum_scatter(partial_value, "sector", scatter_dimension=0, tiled=True)
    own_row = bin_total(own_row)
    new_block = advance(sphere_block, pair_total + wall_total)
    scaling = jnp.array([time_step / body_mass] * 3 + [time_step / body_inertia] * 3, jnp.float32)
    return (new_block, own_row * scaling[None, :])


def local(sph_state, sph_dest, body_list, tile_codes, triangles):
    sectors = lax.axis_size("sector")
    ndevices = sectors * lax.axis_size("bin")
    leaving = sph_state.shape[1]
    fits = 2 * leaving == 64 * ndevices and 16 * leaving == LANES * LANES and sectors & (sectors - 1) == 0
    chosen = fast if fits else general
    return chosen(sph_state, sph_dest, body_list, tile_codes, triangles)


def solution(mesh):
    return jax.shard_map(
        local,
        mesh=mesh,
        in_specs=(
            P(None, ("sector", "bin")),
            P(("sector", "bin"), None),
            P(("sector", "bin"), None),
            P(("sector", "bin"), None, None),
            P(None, "sector", "bin"),
        ),
        out_specs=(P(None, ("sector", "bin")), P("sector", None)),
        check_vma=False,
    )
```

```python
import functools

import jax
import jax.numpy as jnp
from jax import lax
from jax.experimental import pallas as pl
from jax.experimental.pallas import tpu as pltpu
from jax.sharding import PartitionSpec as P

stiff_pair = 50.0
damp_pair = 2.0
stiff_wall = 50.0
time_step = 0.01
gravity = 9.81
body_mass = 4.0
body_inertia = 40.0

LANES = 128
PAYLOAD = ((0, 3), (1, 4), (2, 5), (6, None))
PAIR_BLOCK = 256
SPREAD = 4


def iota(shape, dim):
    return lax.broadcasted_iota(jnp.int32, shape, dim)


def split3(x):
    hi = x.astype(jnp.bfloat16).astype(jnp.float32)
    rest = x - hi
    mid = rest.astype(jnp.bfloat16).astype(jnp.float32)
    return hi, mid, rest - mid


def dot(a, b, contract=((1,), (0,))):
    return lax.dot_general(a, b, (contract, ((), ())), preferred_element_type=jnp.float32)


def pack_kernel(dest_ref, state_ref, out_ref):
    blocks = dest_ref.shape[0]
    ndevices = out_ref.shape[0] * LANES // (8 * 64)
    capacity = 64
    dest = dest_ref[...]
    wide = blocks * ndevices
    expand = (iota((blocks, wide), 1) // ndevices == iota((blocks, wide), 0)).astype(jnp.bfloat16)
    dest_cols = jnp.transpose(dest.astype(jnp.float32)).astype(jnp.bfloat16)
    named = dot(dest_cols, expand)
    onehot = (named == (iota((LANES, wide), 1) % ndevices).astype(jnp.float32)).astype(jnp.float32)
    lower = (iota((LANES, LANES), 0) >= iota((LANES, LANES), 1)).astype(jnp.bfloat16)
    counted = dot(lower, onehot.astype(jnp.bfloat16))
    total = jnp.broadcast_to(counted[LANES - 1 :], (8, wide))
    before = jnp.zeros((8, wide), jnp.float32)
    for step in range(1, blocks):
        moved = pltpu.roll(total, step * ndevices, 1)
        before = before + jnp.where(iota((8, wide), 1) >= step * ndevices, moved, 0.0)
    place = (onehot * (counted - 1.0 + before[0:1])).astype(jnp.bfloat16)
    ranks = dot(expand, place, ((1,), (1,)))
    rank_row = jnp.concatenate([ranks[b : b + 1] for b in range(blocks)], 1)
    dest_row = jnp.concatenate([dest[b : b + 1] for b in range(blocks)], 1)
    leaving = blocks * LANES
    chosen = dest_row == iota((ndevices, leaving), 0)
    slot = (iota((LANES, leaving), 0) % capacity).astype(jnp.float32)
    at_rank = (rank_row == slot).astype(jnp.float32).astype(jnp.bfloat16)
    groups = len(PAYLOAD)
    sources = [pair[half] for half in range(2) for pair in PAYLOAD if pair[half] is not None]
    rows = [
        jnp.where(chosen, part[source : source + 1], 0.0).astype(jnp.bfloat16)
        for part in split3(state_ref[...])
        for source in sources
    ]
    pieces = dot(jnp.concatenate(rows, 0), at_rank, ((1,), (1,)))
    height = len(sources) * ndevices
    out = (pieces[:height] + pieces[height : 2 * height]) + pieces[2 * height :]
    low = iota((ndevices, LANES), 1) < capacity
    for k, pair in enumerate(PAYLOAD):
        halves = []
        for source in pair:
            if source is None:
                halves.append(jnp.zeros((ndevices, LANES), jnp.float32))
            else:
                place = sources.index(source) * ndevices
                halves.append(out[place : place + ndevices])
        out_ref[pl.ds(k, ndevices, stride=groups), :] = jnp.where(low, halves[0], halves[1])


def quotient(code, size):
    power = size & (size - 1) == 0
    return lax.shift_right_logical(code, size.bit_length() - 1) if power else lax.div(code, size)


def remainder(code, size):
    return code & (size - 1) if size & (size - 1) == 0 else lax.rem(code, size)


def total_of(x):
    return jnp.sum(jnp.sum(x, 0, keepdims=True), 1, keepdims=True)


def state_tile(arrived_ref, tile):
    words = arrived_ref[8 * tile : 8 * tile + 8, :]
    swapped = pltpu.roll(pltpu.roll(words, 64, 1), 4, 0)
    same = (iota((8, LANES), 0) < 4) == (iota((8, LANES), 1) < 64)
    return jnp.where(same, words, swapped)


def facet_kernel(sectors, *refs):
    bodies_ref = refs[0]
    tri_refs = refs[1 : 1 + sectors]
    facet, raw, tri_sem = refs[1 + sectors :]
    entries = bodies_ref.shape[1]
    me = lax.axis_index("sector")

    def fetch(entry, source):
        return pltpu.make_async_copy(tri_refs[source], raw.at[entry], tri_sem.at[entry])

    for entry in range(entries):
        relative = bodies_ref[0, entry] ^ me
        for source in range(sectors):

            @pl.when(relative == source)
            def _():
                fetch(entry, source).start()

    for entry in range(entries):
        fetch(entry, 0).wait()
        corner = [raw[entry, i] for i in range(3)]
        one = [raw[entry, 3 + i] - corner[i] for i in range(3)]
        two = [raw[entry, 6 + i] - corner[i] for i in range(3)]
        d11 = one[0] * one[0] + one[1] * one[1] + one[2] * one[2]
        d12 = one[0] * two[0] + one[1] * two[1] + one[2] * two[2]
        d22 = two[0] * two[0] + two[1] * two[1] + two[2] * two[2]
        inverse = 1.0 / (d11 * d22 - d12 * d12)
        for i in range(3):
            facet[entry, i] = corner[i]
            facet[entry, 3 + i] = one[i]
            facet[entry, 6 + i] = two[i]
            facet[entry, 9 + i] = (d22 * one[i] - d12 * two[i]) * inverse
            facet[entry, 12 + i] = (d11 * two[i] - d12 * one[i]) * inverse


def sphere_side(state, row8):
    square = state * state
    level = square[3:4] - (square[0:1] + square[1:2] + square[2:3])
    other = jnp.where(state[3:4] > 0.0, level, -3.0e38)
    return level, jnp.where(
        row8 < 4, state, jnp.where(row8 == 4, 1.0, jnp.where(row8 == 5, other, jnp.where(row8 == 6, square[3:4], 0.0)))
    )


def wall_kernel(sectors, bins, *refs):
    bodies_ref, codes_ref, facet, arrived_ref, wrench_ref, force_ref, left = refs[:7]
    spread, place, gathered = refs[7:10]
    accs = refs[10:]
    entries = bodies_ref.shape[1]
    codes = codes_ref.shape[2]
    tiles_tri = facet.shape[2]
    tiles = arrived_ref.shape[0] // 8
    row8 = iota((8, LANES), 0)

    wanted = iota((48, 4 * LANES), 1) // LANES
    wanted = jnp.where(wanted == 3, 6, wanted)
    row = iota((48, 4 * LANES), 0)
    select = (row % 8 == wanted) & ((row // 8 == 0) | (row // 8 == 1) | (row // 8 == 3))
    select = select.astype(jnp.float32).astype(jnp.bfloat16)
    for tile in range(tiles):
        at = slice(tile * LANES, (tile + 1) * LANES)
        state = state_tile(arrived_ref, tile)
        jh, jm, jl = split3(sphere_side(state, row8)[1])
        left[at, 0:48] = jnp.transpose(jnp.concatenate([jh, jm, jh, jl, jh, jm], 0)).astype(jnp.bfloat16)
        for i in range(3):
            place[i, tile : tile + 1, :] = state[i : i + 1]
    for group in range(tiles // SPREAD):
        at = slice(group * SPREAD * LANES, (group + 1) * SPREAD * LANES)
        wide = dot(left[at, 0:48], select)
        for i in range(4):
            spread[i, at, :] = wide[:, i * LANES : (i + 1) * LANES]
    for acc in accs:
        acc[...] = jnp.zeros_like(acc)

    def one_tile(entry, number):
        code = codes_ref[0, entry, number]
        first = pl.multiple_of(quotient(code, tiles_tri) * LANES, LANES)
        facet_tile = remainder(code, tiles_tri)
        f = [facet[entry, i, pl.ds(facet_tile, 1), :] for i in range(15)]
        at = pl.ds(first, LANES)
        dx, dy, dz = spread[0, at, :] - f[0], spread[1, at, :] - f[1], spread[2, at, :] - f[2]
        beta = dx * f[9] + dy * f[10] + dz * f[11]
        gamma = dx * f[12] + dy * f[13] + dz * f[14]
        alpha = jnp.maximum(1.0 - beta - gamma, 0.0)
        beta = jnp.maximum(beta, 0.0)
        gamma = jnp.maximum(gamma, 0.0)
        scale = 1.0 / (alpha + beta + gamma)
        beta = beta * scale
        gamma = gamma * scale
        ox = dx - beta * f[3] - gamma * f[6]
        oy = dy - beta * f[4] - gamma * f[7]
        oz = dz - beta * f[5] - gamma * f[8]
        deep = jnp.maximum(spread[3, at, :] - (ox * ox + oy * oy + oz * oz), 0.0)
        accs[3 * entry][at, :] += deep * ox
        accs[3 * entry + 1][at, :] += deep * oy
        accs[3 * entry + 2][at, :] += deep * oz

    def step(number, carry):
        for entry in range(entries):
            one_tile(entry, number)
        return carry

    lax.fori_loop(0, codes, step, 0)

    ones = jnp.ones((16, 2 * LANES), jnp.bfloat16)

    def gather(tile, carry):
        at = pl.ds(pl.multiple_of(tile * LANES, LANES), LANES)
        for which in range(3 * entries):
            value = accs[which][at, :]
            high = value.astype(jnp.bfloat16)
            low = (value - high.astype(jnp.float32)).astype(jnp.bfloat16)
            row = dot(ones, jnp.concatenate([high, low], 1), ((1,), (1,)))
            gathered[which, pl.ds(tile, 1), :] = row[0:1]
        return carry

    lax.fori_loop(0, tiles, gather, 0, unroll=2)
    x, y, z = place[0], place[1], place[2]
    owner = iota((sectors * bins, LANES), 0) // bins
    lane = iota((1, LANES), 1)
    out = jnp.zeros((sectors * bins, LANES), jnp.float32)
    whole = [0.0, 0.0, 0.0]
    for entry in range(entries):
        fx, fy, fz = (gathered[3 * entry + i] for i in range(3))
        parts = (fx, fy, fz, y * fz - z * fy, z * fx - x * fz, x * fy - y * fx)
        mine = jnp.zeros((1, LANES), jnp.float32)
        for i, part in enumerate(parts):
            scale = time_step / (body_mass if i < 3 else body_inertia)
            mine = jnp.where(lane == i, total_of(part) * scale, mine)
        out = out + jnp.where(owner == bodies_ref[0, entry], mine * (-stiff_wall), 0.0)
        whole = [whole[0] + fx, whole[1] + fy, whole[2] + fz]
    wrench_ref[...] = out
    for i in range(3):
        force_ref[i] = stiff_wall * whole[i]


def pair_kernel(arrived_ref, force_ref, left, out_hbm, right, moved, out_ref, out_sem):
    tiles = arrived_ref.shape[0] // 8
    blocks = tiles * LANES // PAIR_BLOCK
    row8 = iota((8, LANES), 0)
    for tile in range(tiles):
        at = slice(tile * LANES, (tile + 1) * LANES)
        state = state_tile(arrived_ref, tile)
        level = sphere_side(state, row8)[0]
        i_side = jnp.where(row8 < 4, 2.0 * state, jnp.where(row8 == 4, level, jnp.where(row8 == 5, 1.0, 0.0)))
        ih, im, il = split3(i_side)
        right[:, at] = jnp.concatenate([ih, ih, im, ih, il, im], 0).astype(jnp.bfloat16)
        value = jnp.where(row8 == 3, 1.0, state)
        moved[:, at] = jnp.concatenate(list(split3(value)) + [jnp.zeros((8, LANES), jnp.float32)], 0).astype(
            jnp.bfloat16
        )

    def block_of(ib, carry):
        columns = pl.ds(pl.multiple_of(ib * PAIR_BLOCK, PAIR_BLOCK), PAIR_BLOCK)
        mine = right[:, columns]
        total = jnp.zeros((32, PAIR_BLOCK), jnp.float32)
        for jb in range(blocks):
            rows = slice(jb * PAIR_BLOCK, (jb + 1) * PAIR_BLOCK)
            weight = jnp.maximum(dot(left[rows, 0:48], mine), 0.0)
            high = weight.astype(jnp.bfloat16)
            low = (weight - high.astype(jnp.float32)).astype(jnp.bfloat16)
            values = moved[:, rows]
            total = total + (dot(values, high) + dot(values, low))
        total = total[0:8] + total[8:16] + total[16:24]
        for part in range(PAIR_BLOCK // LANES):
            tile = ib * (PAIR_BLOCK // LANES) + part
            words = arrived_ref[pl.ds(pl.multiple_of(8 * tile, 8), 8), :]
            swapped = pltpu.roll(pltpu.roll(words, 64, 1), 4, 0)
            state = jnp.where((row8 < 4) == (iota((8, LANES), 1) < 64), words, swapped)
            moment = total[:, part * LANES : (part + 1) * LANES]
            differ = moment[3:4] * state - moment
            force = stiff_pair * differ - damp_pair * pltpu.roll(differ, 4, 0)
            for i in range(3):
                force = force + jnp.where(row8 == i, force_ref[i, pl.ds(tile, 1), :], 0.0)
            radius = jnp.broadcast_to(state[3:4], (8, LANES))
            live = radius > 0.0
            mass = jnp.where(live, radius * radius * radius, 1.0)
            falling = jnp.where(row8 == 6, gravity, 0.0)
            speed = state + time_step * (pltpu.roll(force, 4, 0) / mass - falling)
            place = state + time_step * pltpu.roll(speed, 4, 0)
            result = jnp.where(
                row8 < 3, place, jnp.where(row8 < 6, pltpu.roll(speed, 7, 0), pltpu.roll(state, 3, 0))
            )
            result = jnp.where(live, result, 0.0)
            out_ref[:, pl.ds(pl.multiple_of(tile * LANES, LANES), LANES)] = result[0:7]
        leave(ib).start()
        return carry

    def leave(ib):
        columns = pl.ds(pl.multiple_of(ib * PAIR_BLOCK, PAIR_BLOCK), PAIR_BLOCK)
        return pltpu.make_async_copy(out_ref.at[:, columns], out_hbm.at[:, columns], out_sem.at[ib])

    lax.fori_loop(0, blocks, block_of, 0)
    for ib in range(blocks):
        leave(ib).wait()


def whole_vmem():
    return pl.BlockSpec(memory_space=pltpu.VMEM)


def whole_smem():
    return pl.BlockSpec(memory_space=pltpu.SMEM)


def near(x):
    return pltpu.with_memory_space_constraint(x, pltpu.VMEM)


def fast(sph_state, sph_dest, body_list, tile_codes, triangles):
    sectors = lax.axis_size("sector")
    bins = lax.axis_size("bin")
    ndevices = sectors * bins
    leaving = sph_state.shape[1]
    slots = 2 * leaving
    words = 8 * slots // LANES
    block = triangles.reshape(triangles.shape[0], -1, LANES)
    outgoing = pl.pallas_call(
        pack_kernel,
        out_shape=pltpu.VMEM((words, LANES), jnp.float32),
        in_specs=[whole_vmem(), whole_vmem()],
        out_specs=whole_vmem(),
        name="pack",
    )(sph_dest.reshape(-1, LANES), sph_state)
    blocks = [block] + [
        lax.ppermute(block, "sector", [(i, i ^ step) for i in range(sectors)]) for step in range(1, sectors)
    ]
    outgoing = outgoing.reshape(ndevices, 1, words * LANES // ndevices)
    arrived = lax.all_to_all(outgoing, ("sector", "bin"), split_axis=0, concat_axis=0, tiled=True)
    arrived = arrived.reshape(words, LANES)
    entries = body_list.shape[1]
    column = pltpu.VMEM((slots, LANES), jnp.float32)
    tiles = slots // LANES
    facets = pl.pallas_call(
        functools.partial(facet_kernel, sectors),
        out_shape=pltpu.VMEM((entries, 15) + block.shape[1:], jnp.float32),
        in_specs=[whole_smem(), pl.BlockSpec(memory_space=pltpu.HBM)] + [whole_vmem()] * (sectors - 1),
        out_specs=whole_vmem(),
        scratch_shapes=[pltpu.VMEM((entries,) + block.shape, jnp.float32), pltpu.SemaphoreType.DMA((entries,))],
        name="facet",
    )(body_list, blocks[0], *[near(other) for other in blocks[1:]])
    wrench, force, left = pl.pallas_call(
        functools.partial(wall_kernel, sectors, bins),
        out_shape=[
            pltpu.VMEM((ndevices, LANES), jnp.float32),
            pltpu.VMEM((3, tiles, LANES), jnp.float32),
            pltpu.VMEM((slots, LANES), jnp.bfloat16),
        ],
        in_specs=[whole_smem(), whole_smem()] + [whole_vmem()] * 2,
        out_specs=[whole_vmem()] * 3,
        scratch_shapes=[
            pltpu.VMEM((4, slots, LANES), jnp.float32),
            pltpu.VMEM((3, tiles, LANES), jnp.float32),
            pltpu.VMEM((3 * entries, tiles, LANES), jnp.float32),
        ]
        + [column] * (3 * entries),
        name="wall",
    )(body_list, tile_codes, near(facets), near(arrived))
    shared = lax.all_to_all(
        wrench.reshape(ndevices, 1, LANES), ("sector", "bin"), split_axis=0, concat_axis=0, tiled=True
    )
    new_block = pl.pallas_call(
        pair_kernel,
        out_shape=jax.ShapeDtypeStruct((7, slots), jnp.float32),
        in_specs=[whole_vmem()] * 3,
        out_specs=pl.BlockSpec(memory_space=pltpu.HBM),
        scratch_shapes=[
            pltpu.VMEM((48, slots), jnp.bfloat16),
            pltpu.VMEM((32, slots), jnp.bfloat16),
            pltpu.VMEM((7, slots), jnp.float32),
            pltpu.SemaphoreType.DMA((slots // PAIR_BLOCK,)),
        ],
        name="pair",
    )(near(arrived), near(force), near(left))
    kick = jnp.sum(shared[:, 0, :6], 0, keepdims=True)
    return new_block, kick


def contact(spheres, facets):
    centre = spheres[0:3]
    radius = spheres[3]
    corner = facets[0:3]
    edge_one = facets[3:6] - corner
    edge_two = facets[6:9] - corner
    square_one = jnp.sum(edge_one * edge_one, 0)
    square_two = jnp.sum(edge_two * edge_two, 0)
    cross_term = jnp.sum(edge_one * edge_two, 0)
    inverse = 1.0 / (square_one * square_two - cross_term * cross_term)
    relative = centre[:, :, None] - corner[:, None, :]
    along_one = jnp.sum(relative * edge_one[:, None, :], 0)
    along_two = jnp.sum(relative * edge_two[:, None, :], 0)
    weight_b = (square_two * along_one - cross_term * along_two) * inverse
    weight_c = (square_one * along_two - cross_term * along_one) * inverse
    weight_a = jnp.maximum(1.0 - weight_b - weight_c, 0.0)
    weight_b = jnp.maximum(weight_b, 0.0)
    weight_c = jnp.maximum(weight_c, 0.0)
    totals = weight_a + weight_b + weight_c
    weight_b = weight_b / totals
    weight_c = weight_c / totals
    nearest = (
        corner[:, None, :]
        + weight_b[None] * edge_one[:, None, :]
        + weight_c[None] * edge_two[:, None, :]
    )
    offset = centre[:, :, None] - nearest
    squared = jnp.sum(offset * offset, 0)
    strength = stiff_wall * jnp.maximum(radius[:, None] * radius[:, None] - squared, 0.0)
    forces = strength[None] * offset
    on_spheres = jnp.sum(forces, 2)
    on_body = -jnp.sum(forces, (1, 2))
    torque = -jnp.sum(jnp.cross(nearest, forces, axis=0), (1, 2))
    return (on_spheres, jnp.concatenate([on_body, torque]))


def tile_forces(spheres, facets, tile_list):
    tiles_tri = facets.shape[1] // 128

    def advance_tile(carried, tile_code):
        forces, wrench = carried
        sphere_tile = tile_code // tiles_tri
        facet_tile = tile_code % tiles_tri
        sphere_part = lax.dynamic_slice_in_dim(spheres, sphere_tile * 128, 128, 1)
        facet_part = lax.dynamic_slice_in_dim(facets, facet_tile * 128, 128, 1)
        on_spheres, on_body = contact(sphere_part, facet_part)
        current = lax.dynamic_slice_in_dim(forces, sphere_tile * 128, 128, 1)
        forces = lax.dynamic_update_slice_in_dim(forces, current + on_spheres, sphere_tile * 128, 1)
        return ((forces, wrench + on_body), None)

    initial = (jnp.zeros((3, spheres.shape[1]), jnp.float32), jnp.zeros((6,), jnp.float32))
    (forces, wrench), unused = lax.scan(advance_tile, initial, tile_list)
    return (forces, wrench)


def sphere_forces(sphere_block):
    position = sphere_block[0:3]
    velocity = sphere_block[3:6]
    radius = sphere_block[6]
    width_all = sphere_block.shape[1]
    occupied = (radius > 0).astype(jnp.float32)
    coords = jnp.concatenate([position, radius[None]], 0)
    baseline = radius * radius - jnp.sum(position * position, 0)
    stacked = jnp.concatenate([position, velocity, jnp.ones((1, width_all), jnp.float32)], 0)
    row_block = 512

    def row_group(row_start):
        coords_rows = lax.dynamic_slice_in_dim(coords, row_start, row_block, 1)
        base_rows = lax.dynamic_slice_in_dim(baseline, row_start, row_block, 0)
        live_rows = lax.dynamic_slice_in_dim(occupied, row_start, row_block, 0)
        inner_products = lax.dot_general(
            coords_rows, coords, (((0,), (0,)), ((), ())), precision=lax.Precision.HIGHEST
        )
        intersection = jnp.maximum(
            base_rows[:, None] + baseline[None, :] + 2.0 * inner_products, 0.0
        )
        intersection = intersection * live_rows[:, None] * occupied[None, :]
        return lax.dot_general(
            stacked, intersection, (((1,), (1,)), ((), ())), precision=lax.Precision.HIGHEST
        )

    starts = jnp.arange(width_all // row_block, dtype=jnp.int32) * row_block
    grouped = lax.map(row_group, starts)
    weighted = jnp.transpose(grouped, (1, 0, 2)).reshape(7, width_all)
    totals = weighted[6]
    return stiff_pair * (totals * position - weighted[0:3]) - damp_pair * (
        totals * velocity - weighted[3:6]
    )


def advance(sphere_block, forces):
    position = sphere_block[0:3]
    velocity = sphere_block[3:6]
    radius = sphere_block[6]
    occupied = radius > 0
    masses = jnp.where(occupied, radius * radius * radius, 1.0)
    falling = jnp.array([0.0, 0.0, gravity], jnp.float32)
    acceleration = forces / masses[None] - falling[:, None]
    velocity_new = velocity + time_step * acceleration
    position_new = position + time_step * velocity_new
    result = jnp.concatenate([position_new, velocity_new, radius[None]], 0)
    return jnp.where(occupied[None], result, 0.0)


def bin_total(partial_row):
    return lax.psum(partial_row, "bin")


def general(sph_state, sph_dest, body_list, tile_codes, triangles):
    sectors = lax.axis_size("sector")
    bins = lax.axis_size("bin")
    ndevices = sectors * bins
    leaving = sph_state.shape[1]
    capacity = 2 * leaving // ndevices
    targets = sph_dest[:, 0]
    onehot = (targets[:, None] == jnp.arange(ndevices, dtype=jnp.int32)[None, :]).astype(jnp.int32)
    ranks = jnp.sum((jnp.cumsum(onehot, 0) - 1) * onehot, 1)
    columns = targets * capacity + ranks
    outgoing = jnp.zeros((7, ndevices * capacity), jnp.float32).at[:, columns].set(sph_state)
    outgoing = outgoing.reshape(7, sectors, bins, capacity)
    arrived = lax.all_to_all(
        lax.all_to_all(outgoing, "sector", split_axis=1, concat_axis=1, tiled=True),
        "bin",
        split_axis=2,
        concat_axis=2,
        tiled=True,
    )
    sphere_block = arrived.reshape(7, ndevices * capacity)
    width_all = sphere_block.shape[1]
    coords = jnp.concatenate([sphere_block[0:3], sphere_block[6:7]], 0)
    pair_total = sphere_forces(sphere_block)
    everyone = lax.all_gather(triangles, "sector", axis=1, tiled=True)
    wall_total = jnp.zeros((3, width_all), jnp.float32)
    partial_value = jnp.zeros((sectors, 6), jnp.float32)
    for slot_index in range(body_list.shape[1]):
        owner_body = body_list[0, slot_index]
        facets = lax.dynamic_index_in_dim(everyone, owner_body, 1, keepdims=False)
        on_spheres, on_body = tile_forces(coords, facets, tile_codes[0, slot_index])
        wall_total = wall_total + on_spheres
        selector = (jnp.arange(sectors, dtype=jnp.int32) == owner_body).astype(jnp.float32)
        partial_value = partial_value + selector[:, None] * on_body[None, :]
    own_row = lax.psum_scatter(partial_value, "sector", scatter_dimension=0, tiled=True)
    own_row = bin_total(own_row)
    new_block = advance(sphere_block, pair_total + wall_total)
    scaling = jnp.array([time_step / body_mass] * 3 + [time_step / body_inertia] * 3, jnp.float32)
    return (new_block, own_row * scaling[None, :])


def local(sph_state, sph_dest, body_list, tile_codes, triangles):
    sectors = lax.axis_size("sector")
    ndevices = sectors * lax.axis_size("bin")
    leaving = sph_state.shape[1]
    fits = 2 * leaving == 64 * ndevices and 16 * leaving == LANES * LANES and sectors & (sectors - 1) == 0
    chosen = fast if fits else general
    return chosen(sph_state, sph_dest, body_list, tile_codes, triangles)


def solution(mesh):
    return jax.shard_map(
        local,
        mesh=mesh,
        in_specs=(
            P(None, ("sector", "bin")),
            P(("sector", "bin"), None),
            P(("sector", "bin"), None),
            P(("sector", "bin"), None, None),
            P(None, "sector", "bin"),
        ),
        out_specs=(P(None, ("sector", "bin")), P("sector", None)),
        check_vma=False,
    )
```

```python
import functools

import jax
import jax.numpy as jnp
from jax import lax
from jax.experimental import pallas as pl
from jax.experimental.pallas import tpu as pltpu
from jax.sharding import PartitionSpec as P

stiff_pair = 50.0
damp_pair = 2.0
stiff_wall = 50.0
time_step = 0.01
gravity = 9.81
body_mass = 4.0
body_inertia = 40.0

LANES = 128
PAYLOAD = ((0, 3), (1, 4), (2, 5), (6, None))
PAIR_BLOCK = 512
SPREAD = 4


def iota(shape, dim):
    return lax.broadcasted_iota(jnp.int32, shape, dim)


def split3(x):
    hi = x.astype(jnp.bfloat16).astype(jnp.float32)
    rest = x - hi
    mid = rest.astype(jnp.bfloat16).astype(jnp.float32)
    return hi, mid, rest - mid


def dot(a, b, contract=((1,), (0,))):
    return lax.dot_general(a, b, (contract, ((), ())), preferred_element_type=jnp.float32)


def pack_kernel(dest_ref, state_ref, out_ref):
    blocks = dest_ref.shape[0]
    ndevices = out_ref.shape[0] * LANES // (8 * 64)
    capacity = 64
    dest = dest_ref[...]
    wide = blocks * ndevices
    expand = (iota((blocks, wide), 1) // ndevices == iota((blocks, wide), 0)).astype(jnp.bfloat16)
    dest_cols = jnp.transpose(dest.astype(jnp.float32)).astype(jnp.bfloat16)
    named = dot(dest_cols, expand)
    onehot = (named == (iota((LANES, wide), 1) % ndevices).astype(jnp.float32)).astype(jnp.float32)
    lower = (iota((LANES, LANES), 0) >= iota((LANES, LANES), 1)).astype(jnp.bfloat16)
    counted = dot(lower, onehot.astype(jnp.bfloat16))
    total = jnp.broadcast_to(counted[LANES - 1 :], (8, wide))
    before = jnp.zeros((8, wide), jnp.float32)
    for step in range(1, blocks):
        moved = pltpu.roll(total, step * ndevices, 1)
        before = before + jnp.where(iota((8, wide), 1) >= step * ndevices, moved, 0.0)
    place = (onehot * (counted - 1.0 + before[0:1])).astype(jnp.bfloat16)
    ranks = dot(expand, place, ((1,), (1,)))
    rank_row = jnp.concatenate([ranks[b : b + 1] for b in range(blocks)], 1)
    dest_row = jnp.concatenate([dest[b : b + 1] for b in range(blocks)], 1)
    leaving = blocks * LANES
    chosen = dest_row == iota((ndevices, leaving), 0)
    slot = (iota((LANES, leaving), 0) % capacity).astype(jnp.float32)
    at_rank = (rank_row == slot).astype(jnp.float32).astype(jnp.bfloat16)
    groups = len(PAYLOAD)
    sources = [pair[half] for half in range(2) for pair in PAYLOAD if pair[half] is not None]
    rows = [
        jnp.where(chosen, part[source : source + 1], 0.0).astype(jnp.bfloat16)
        for part in split3(state_ref[...])
        for source in sources
    ]
    pieces = dot(jnp.concatenate(rows, 0), at_rank, ((1,), (1,)))
    height = len(sources) * ndevices
    out = (pieces[:height] + pieces[height : 2 * height]) + pieces[2 * height :]
    low = iota((ndevices, LANES), 1) < capacity
    for k, pair in enumerate(PAYLOAD):
        halves = []
        for source in pair:
            if source is None:
                halves.append(jnp.zeros((ndevices, LANES), jnp.float32))
            else:
                place = sources.index(source) * ndevices
                halves.append(out[place : place + ndevices])
        out_ref[pl.ds(k, ndevices, stride=groups), :] = jnp.where(low, halves[0], halves[1])


def quotient(code, size):
    power = size & (size - 1) == 0
    return lax.shift_right_logical(code, size.bit_length() - 1) if power else lax.div(code, size)


def remainder(code, size):
    return code & (size - 1) if size & (size - 1) == 0 else lax.rem(code, size)


def total_of(x):
    return jnp.sum(jnp.sum(x, 0, keepdims=True), 1, keepdims=True)


def state_tile(arrived_ref, tile):
    words = arrived_ref[8 * tile : 8 * tile + 8, :]
    swapped = pltpu.roll(pltpu.roll(words, 64, 1), 4, 0)
    same = (iota((8, LANES), 0) < 4) == (iota((8, LANES), 1) < 64)
    return jnp.where(same, words, swapped)


def facet_kernel(sectors, *refs):
    bodies_ref = refs[0]
    tri_refs = refs[1 : 1 + sectors]
    facet, raw, tri_sem = refs[1 + sectors :]
    entries = bodies_ref.shape[1]
    me = lax.axis_index("sector")

    def fetch(entry, source):
        return pltpu.make_async_copy(tri_refs[source], raw.at[entry], tri_sem.at[entry])

    for entry in range(entries):
        relative = bodies_ref[0, entry] ^ me
        for source in range(sectors):

            @pl.when(relative == source)
            def _():
                fetch(entry, source).start()

    for entry in range(entries):
        fetch(entry, 0).wait()
        corner = [raw[entry, i] for i in range(3)]
        one = [raw[entry, 3 + i] - corner[i] for i in range(3)]
        two = [raw[entry, 6 + i] - corner[i] for i in range(3)]
        d11 = one[0] * one[0] + one[1] * one[1] + one[2] * one[2]
        d12 = one[0] * two[0] + one[1] * two[1] + one[2] * two[2]
        d22 = two[0] * two[0] + two[1] * two[1] + two[2] * two[2]
        inverse = 1.0 / (d11 * d22 - d12 * d12)
        for i in range(3):
            facet[entry, i] = corner[i]
            facet[entry, 3 + i] = one[i]
            facet[entry, 6 + i] = two[i]
            facet[entry, 9 + i] = (d22 * one[i] - d12 * two[i]) * inverse
            facet[entry, 12 + i] = (d11 * two[i] - d12 * one[i]) * inverse


def sphere_side(state, row8):
    square = state * state
    level = square[3:4] - (square[0:1] + square[1:2] + square[2:3])
    other = jnp.where(state[3:4] > 0.0, level, -3.0e38)
    return level, jnp.where(
        row8 < 4, state, jnp.where(row8 == 4, 1.0, jnp.where(row8 == 5, other, jnp.where(row8 == 6, square[3:4], 0.0)))
    )


def wall_kernel(sectors, bins, *refs):
    bodies_ref, codes_ref, facet, arrived_ref, wrench_ref, force_ref, left = refs[:7]
    spread, place, gathered = refs[7:10]
    accs = refs[10:]
    entries = bodies_ref.shape[1]
    codes = codes_ref.shape[2]
    tiles_tri = facet.shape[2]
    tiles = arrived_ref.shape[0] // 8
    row8 = iota((8, LANES), 0)

    wanted = iota((48, 4 * LANES), 1) // LANES
    wanted = jnp.where(wanted == 3, 6, wanted)
    row = iota((48, 4 * LANES), 0)
    select = (row % 8 == wanted) & ((row // 8 == 0) | (row // 8 == 1) | (row // 8 == 3))
    select = select.astype(jnp.float32).astype(jnp.bfloat16)
    for tile in range(tiles):
        at = slice(tile * LANES, (tile + 1) * LANES)
        state = state_tile(arrived_ref, tile)
        jh, jm, jl = split3(sphere_side(state, row8)[1])
        left[at, 0:48] = jnp.transpose(jnp.concatenate([jh, jm, jh, jl, jh, jm], 0)).astype(jnp.bfloat16)
        for i in range(3):
            place[i, tile : tile + 1, :] = state[i : i + 1]
    for group in range(tiles // SPREAD):
        at = slice(group * SPREAD * LANES, (group + 1) * SPREAD * LANES)
        wide = dot(left[at, 0:48], select)
        for i in range(4):
            spread[i, at, :] = wide[:, i * LANES : (i + 1) * LANES]
    for acc in accs:
        acc[...] = jnp.zeros_like(acc)

    def one_tile(entry, number):
        code = codes_ref[0, entry, number]
        first = pl.multiple_of(quotient(code, tiles_tri) * LANES, LANES)
        facet_tile = remainder(code, tiles_tri)
        f = [facet[entry, i, pl.ds(facet_tile, 1), :] for i in range(15)]
        at = pl.ds(first, LANES)
        dx, dy, dz = spread[0, at, :] - f[0], spread[1, at, :] - f[1], spread[2, at, :] - f[2]
        beta = dx * f[9] + dy * f[10] + dz * f[11]
        gamma = dx * f[12] + dy * f[13] + dz * f[14]
        alpha = jnp.maximum(1.0 - beta - gamma, 0.0)
        beta = jnp.maximum(beta, 0.0)
        gamma = jnp.maximum(gamma, 0.0)
        scale = 1.0 / (alpha + beta + gamma)
        beta = beta * scale
        gamma = gamma * scale
        ox = dx - beta * f[3] - gamma * f[6]
        oy = dy - beta * f[4] - gamma * f[7]
        oz = dz - beta * f[5] - gamma * f[8]
        deep = jnp.maximum(spread[3, at, :] - (ox * ox + oy * oy + oz * oz), 0.0)
        accs[3 * entry][at, :] += deep * ox
        accs[3 * entry + 1][at, :] += deep * oy
        accs[3 * entry + 2][at, :] += deep * oz

    def step(number, carry):
        for entry in range(entries):
            one_tile(entry, number)
        return carry

    lax.fori_loop(0, codes, step, 0)

    ones = jnp.ones((16, 2 * LANES), jnp.bfloat16)

    def gather(tile, carry):
        at = pl.ds(pl.multiple_of(tile * LANES, LANES), LANES)
        for which in range(3 * entries):
            value = accs[which][at, :]
            if which % 2:
                row = jnp.sum(jnp.transpose(value), 0, keepdims=True)
            else:
                high = value.astype(jnp.bfloat16)
                low = (value - high.astype(jnp.float32)).astype(jnp.bfloat16)
                row = dot(ones, jnp.concatenate([high, low], 1), ((1,), (1,)))
            gathered[which, pl.ds(tile, 1), :] = row[0:1]
        return carry

    lax.fori_loop(0, tiles, gather, 0, unroll=8)
    x, y, z = place[0], place[1], place[2]
    owner = iota((sectors * bins, LANES), 0) // bins
    lane = iota((1, LANES), 1)
    out = jnp.zeros((sectors * bins, LANES), jnp.float32)
    whole = [0.0, 0.0, 0.0]
    for entry in range(entries):
        fx, fy, fz = (gathered[3 * entry + i] for i in range(3))
        parts = (fx, fy, fz, y * fz - z * fy, z * fx - x * fz, x * fy - y * fx)
        mine = jnp.zeros((1, LANES), jnp.float32)
        for i, part in enumerate(parts):
            scale = time_step / (body_mass if i < 3 else body_inertia)
            mine = jnp.where(lane == i, total_of(part) * scale, mine)
        out = out + jnp.where(owner == bodies_ref[0, entry], mine * (-stiff_wall), 0.0)
        whole = [whole[0] + fx, whole[1] + fy, whole[2] + fz]
    wrench_ref[...] = out
    for i in range(3):
        force_ref[i] = stiff_wall * whole[i]


def pair_kernel(arrived_ref, force_ref, left, out_hbm, right, moved, out_ref, out_sem):
    tiles = arrived_ref.shape[0] // 8
    blocks = tiles * LANES // PAIR_BLOCK
    row8 = iota((8, LANES), 0)
    for tile in range(tiles):
        at = slice(tile * LANES, (tile + 1) * LANES)
        state = state_tile(arrived_ref, tile)
        level = sphere_side(state, row8)[0]
        i_side = jnp.where(row8 < 4, 2.0 * state, jnp.where(row8 == 4, level, jnp.where(row8 == 5, 1.0, 0.0)))
        ih, im, il = split3(i_side)
        right[:, at] = jnp.concatenate([ih, ih, im, ih, il, im], 0).astype(jnp.bfloat16)
        value = jnp.where(row8 == 3, 1.0, state)
        moved[:, at] = jnp.concatenate(list(split3(value)) + [jnp.zeros((8, LANES), jnp.float32)], 0).astype(
            jnp.bfloat16
        )

    def block_of(ib, carry):
        columns = pl.ds(pl.multiple_of(ib * PAIR_BLOCK, PAIR_BLOCK), PAIR_BLOCK)
        mine = right[:, columns]
        total = jnp.zeros((32, PAIR_BLOCK), jnp.float32)
        for jb in range(blocks):
            rows = slice(jb * PAIR_BLOCK, (jb + 1) * PAIR_BLOCK)
            weight = jnp.maximum(dot(left[rows, 0:48], mine), 0.0)
            high = weight.astype(jnp.bfloat16)
            low = (weight - high.astype(jnp.float32)).astype(jnp.bfloat16)
            values = moved[:, rows]
            total = total + (dot(values, high) + dot(values, low))
        total = total[0:8] + total[8:16] + total[16:24]
        for part in range(PAIR_BLOCK // LANES):
            tile = ib * (PAIR_BLOCK // LANES) + part
            words = arrived_ref[pl.ds(pl.multiple_of(8 * tile, 8), 8), :]
            swapped = pltpu.roll(pltpu.roll(words, 64, 1), 4, 0)
            state = jnp.where((row8 < 4) == (iota((8, LANES), 1) < 64), words, swapped)
            moment = total[:, part * LANES : (part + 1) * LANES]
            differ = moment[3:4] * state - moment
            force = stiff_pair * differ - damp_pair * pltpu.roll(differ, 4, 0)
            for i in range(3):
                force = force + jnp.where(row8 == i, force_ref[i, pl.ds(tile, 1), :], 0.0)
            radius = jnp.broadcast_to(state[3:4], (8, LANES))
            live = radius > 0.0
            mass = jnp.where(live, radius * radius * radius, 1.0)
            falling = jnp.where(row8 == 6, gravity, 0.0)
            speed = state + time_step * (pltpu.roll(force, 4, 0) / mass - falling)
            place = state + time_step * pltpu.roll(speed, 4, 0)
            result = jnp.where(
                row8 < 3, place, jnp.where(row8 < 6, pltpu.roll(speed, 7, 0), pltpu.roll(state, 3, 0))
            )
            result = jnp.where(live, result, 0.0)
            out_ref[:, pl.ds(pl.multiple_of(tile * LANES, LANES), LANES)] = result[0:7]
        leave(ib).start()
        return carry

    def leave(ib):
        columns = pl.ds(pl.multiple_of(ib * PAIR_BLOCK, PAIR_BLOCK), PAIR_BLOCK)
        return pltpu.make_async_copy(out_ref.at[:, columns], out_hbm.at[:, columns], out_sem.at[ib])

    lax.fori_loop(0, blocks, block_of, 0, unroll=2)
    for ib in range(blocks):
        leave(ib).wait()


def whole_vmem():
    return pl.BlockSpec(memory_space=pltpu.VMEM)


def whole_smem():
    return pl.BlockSpec(memory_space=pltpu.SMEM)


def near(x):
    return pltpu.with_memory_space_constraint(x, pltpu.VMEM)


def fast(sph_state, sph_dest, body_list, tile_codes, triangles):
    sectors = lax.axis_size("sector")
    bins = lax.axis_size("bin")
    ndevices = sectors * bins
    leaving = sph_state.shape[1]
    slots = 2 * leaving
    words = 8 * slots // LANES
    block = triangles.reshape(triangles.shape[0], -1, LANES)
    outgoing = pl.pallas_call(
        pack_kernel,
        out_shape=pltpu.VMEM((words, LANES), jnp.float32),
        in_specs=[whole_vmem(), whole_vmem()],
        out_specs=whole_vmem(),
        name="pack",
    )(sph_dest.reshape(-1, LANES), sph_state)
    blocks = [block] + [
        lax.ppermute(block, "sector", [(i, i ^ step) for i in range(sectors)]) for step in range(1, sectors)
    ]
    outgoing = outgoing.reshape(ndevices, 1, words * LANES // ndevices)
    arrived = lax.all_to_all(outgoing, ("sector", "bin"), split_axis=0, concat_axis=0, tiled=True)
    arrived = arrived.reshape(words, LANES)
    entries = body_list.shape[1]
    column = pltpu.VMEM((slots, LANES), jnp.float32)
    tiles = slots // LANES
    facets = pl.pallas_call(
        functools.partial(facet_kernel, sectors),
        out_shape=pltpu.VMEM((entries, 15) + block.shape[1:], jnp.float32),
        in_specs=[whole_smem(), pl.BlockSpec(memory_space=pltpu.HBM)] + [whole_vmem()] * (sectors - 1),
        out_specs=whole_vmem(),
        scratch_shapes=[pltpu.VMEM((entries,) + block.shape, jnp.float32), pltpu.SemaphoreType.DMA((entries,))],
        name="facet",
    )(body_list, blocks[0], *[near(other) for other in blocks[1:]])
    wrench, force, left = pl.pallas_call(
        functools.partial(wall_kernel, sectors, bins),
        out_shape=[
            pltpu.VMEM((ndevices, LANES), jnp.float32),
            pltpu.VMEM((3, tiles, LANES), jnp.float32),
            pltpu.VMEM((slots, LANES), jnp.bfloat16),
        ],
        in_specs=[whole_smem(), whole_smem()] + [whole_vmem()] * 2,
        out_specs=[whole_vmem()] * 3,
        scratch_shapes=[
            pltpu.VMEM((4, slots, LANES), jnp.float32),
            pltpu.VMEM((3, tiles, LANES), jnp.float32),
            pltpu.VMEM((3 * entries, tiles, LANES), jnp.float32),
        ]
        + [column] * (3 * entries),
        name="wall",
    )(body_list, tile_codes, near(facets), near(arrived))
    shared = lax.all_to_all(
        wrench.reshape(ndevices, 1, LANES), ("sector", "bin"), split_axis=0, concat_axis=0, tiled=True
    )
    new_block = pl.pallas_call(
        pair_kernel,
        out_shape=jax.ShapeDtypeStruct((7, slots), jnp.float32),
        in_specs=[whole_vmem()] * 3,
        out_specs=pl.BlockSpec(memory_space=pltpu.HBM),
        scratch_shapes=[
            pltpu.VMEM((48, slots), jnp.bfloat16),
            pltpu.VMEM((32, slots), jnp.bfloat16),
            pltpu.VMEM((7, slots), jnp.float32),
            pltpu.SemaphoreType.DMA((slots // PAIR_BLOCK,)),
        ],
        name="pair",
    )(near(arrived), near(force), near(left))
    kick = jnp.sum(shared[:, 0, :6], 0, keepdims=True)
    return new_block, kick


def contact(spheres, facets):
    centre = spheres[0:3]
    radius = spheres[3]
    corner = facets[0:3]
    edge_one = facets[3:6] - corner
    edge_two = facets[6:9] - corner
    square_one = jnp.sum(edge_one * edge_one, 0)
    square_two = jnp.sum(edge_two * edge_two, 0)
    cross_term = jnp.sum(edge_one * edge_two, 0)
    inverse = 1.0 / (square_one * square_two - cross_term * cross_term)
    relative = centre[:, :, None] - corner[:, None, :]
    along_one = jnp.sum(relative * edge_one[:, None, :], 0)
    along_two = jnp.sum(relative * edge_two[:, None, :], 0)
    weight_b = (square_two * along_one - cross_term * along_two) * inverse
    weight_c = (square_one * along_two - cross_term * along_one) * inverse
    weight_a = jnp.maximum(1.0 - weight_b - weight_c, 0.0)
    weight_b = jnp.maximum(weight_b, 0.0)
    weight_c = jnp.maximum(weight_c, 0.0)
    totals = weight_a + weight_b + weight_c
    weight_b = weight_b / totals
    weight_c = weight_c / totals
    nearest = (
        corner[:, None, :]
        + weight_b[None] * edge_one[:, None, :]
        + weight_c[None] * edge_two[:, None, :]
    )
    offset = centre[:, :, None] - nearest
    squared = jnp.sum(offset * offset, 0)
    strength = stiff_wall * jnp.maximum(radius[:, None] * radius[:, None] - squared, 0.0)
    forces = strength[None] * offset
    on_spheres = jnp.sum(forces, 2)
    on_body = -jnp.sum(forces, (1, 2))
    torque = -jnp.sum(jnp.cross(nearest, forces, axis=0), (1, 2))
    return (on_spheres, jnp.concatenate([on_body, torque]))


def tile_forces(spheres, facets, tile_list):
    tiles_tri = facets.shape[1] // 128

    def advance_tile(carried, tile_code):
        forces, wrench = carried
        sphere_tile = tile_code // tiles_tri
        facet_tile = tile_code % tiles_tri
        sphere_part = lax.dynamic_slice_in_dim(spheres, sphere_tile * 128, 128, 1)
        facet_part = lax.dynamic_slice_in_dim(facets, facet_tile * 128, 128, 1)
        on_spheres, on_body = contact(sphere_part, facet_part)
        current = lax.dynamic_slice_in_dim(forces, sphere_tile * 128, 128, 1)
        forces = lax.dynamic_update_slice_in_dim(forces, current + on_spheres, sphere_tile * 128, 1)
        return ((forces, wrench + on_body), None)

    initial = (jnp.zeros((3, spheres.shape[1]), jnp.float32), jnp.zeros((6,), jnp.float32))
    (forces, wrench), unused = lax.scan(advance_tile, initial, tile_list)
    return (forces, wrench)


def sphere_forces(sphere_block):
    position = sphere_block[0:3]
    velocity = sphere_block[3:6]
    radius = sphere_block[6]
    width_all = sphere_block.shape[1]
    occupied = (radius > 0).astype(jnp.float32)
    coords = jnp.concatenate([position, radius[None]], 0)
    baseline = radius * radius - jnp.sum(position * position, 0)
    stacked = jnp.concatenate([position, velocity, jnp.ones((1, width_all), jnp.float32)], 0)
    row_block = 512

    def row_group(row_start):
        coords_rows = lax.dynamic_slice_in_dim(coords, row_start, row_block, 1)
        base_rows = lax.dynamic_slice_in_dim(baseline, row_start, row_block, 0)
        live_rows = lax.dynamic_slice_in_dim(occupied, row_start, row_block, 0)
        inner_products = lax.dot_general(
            coords_rows, coords, (((0,), (0,)), ((), ())), precision=lax.Precision.HIGHEST
        )
        intersection = jnp.maximum(
            base_rows[:, None] + baseline[None, :] + 2.0 * inner_products, 0.0
        )
        intersection = intersection * live_rows[:, None] * occupied[None, :]
        return lax.dot_general(
            stacked, intersection, (((1,), (1,)), ((), ())), precision=lax.Precision.HIGHEST
        )

    starts = jnp.arange(width_all // row_block, dtype=jnp.int32) * row_block
    grouped = lax.map(row_group, starts)
    weighted = jnp.transpose(grouped, (1, 0, 2)).reshape(7, width_all)
    totals = weighted[6]
    return stiff_pair * (totals * position - weighted[0:3]) - damp_pair * (
        totals * velocity - weighted[3:6]
    )


def advance(sphere_block, forces):
    position = sphere_block[0:3]
    velocity = sphere_block[3:6]
    radius = sphere_block[6]
    occupied = radius > 0
    masses = jnp.where(occupied, radius * radius * radius, 1.0)
    falling = jnp.array([0.0, 0.0, gravity], jnp.float32)
    acceleration = forces / masses[None] - falling[:, None]
    velocity_new = velocity + time_step * acceleration
    position_new = position + time_step * velocity_new
    result = jnp.concatenate([position_new, velocity_new, radius[None]], 0)
    return jnp.where(occupied[None], result, 0.0)


def bin_total(partial_row):
    return lax.psum(partial_row, "bin")


def general(sph_state, sph_dest, body_list, tile_codes, triangles):
    sectors = lax.axis_size("sector")
    bins = lax.axis_size("bin")
    ndevices = sectors * bins
    leaving = sph_state.shape[1]
    capacity = 2 * leaving // ndevices
    targets = sph_dest[:, 0]
    onehot = (targets[:, None] == jnp.arange(ndevices, dtype=jnp.int32)[None, :]).astype(jnp.int32)
    ranks = jnp.sum((jnp.cumsum(onehot, 0) - 1) * onehot, 1)
    columns = targets * capacity + ranks
    outgoing = jnp.zeros((7, ndevices * capacity), jnp.float32).at[:, columns].set(sph_state)
    outgoing = outgoing.reshape(7, sectors, bins, capacity)
    arrived = lax.all_to_all(
        lax.all_to_all(outgoing, "sector", split_axis=1, concat_axis=1, tiled=True),
        "bin",
        split_axis=2,
        concat_axis=2,
        tiled=True,
    )
    sphere_block = arrived.reshape(7, ndevices * capacity)
    width_all = sphere_block.shape[1]
    coords = jnp.concatenate([sphere_block[0:3], sphere_block[6:7]], 0)
    pair_total = sphere_forces(sphere_block)
    everyone = lax.all_gather(triangles, "sector", axis=1, tiled=True)
    wall_total = jnp.zeros((3, width_all), jnp.float32)
    partial_value = jnp.zeros((sectors, 6), jnp.float32)
    for slot_index in range(body_list.shape[1]):
        owner_body = body_list[0, slot_index]
        facets = lax.dynamic_index_in_dim(everyone, owner_body, 1, keepdims=False)
        on_spheres, on_body = tile_forces(coords, facets, tile_codes[0, slot_index])
        wall_total = wall_total + on_spheres
        selector = (jnp.arange(sectors, dtype=jnp.int32) == owner_body).astype(jnp.float32)
        partial_value = partial_value + selector[:, None] * on_body[None, :]
    own_row = lax.psum_scatter(partial_value, "sector", scatter_dimension=0, tiled=True)
    own_row = bin_total(own_row)
    new_block = advance(sphere_block, pair_total + wall_total)
    scaling = jnp.array([time_step / body_mass] * 3 + [time_step / body_inertia] * 3, jnp.float32)
    return (new_block, own_row * scaling[None, :])


def local(sph_state, sph_dest, body_list, tile_codes, triangles):
    sectors = lax.axis_size("sector")
    ndevices = sectors * lax.axis_size("bin")
    leaving = sph_state.shape[1]
    fits = 2 * leaving == 64 * ndevices and 16 * leaving == LANES * LANES and sectors & (sectors - 1) == 0
    chosen = fast if fits else general
    return chosen(sph_state, sph_dest, body_list, tile_codes, triangles)


def solution(mesh):
    return jax.shard_map(
        local,
        mesh=mesh,
        in_specs=(
            P(None, ("sector", "bin")),
            P(("sector", "bin"), None),
            P(("sector", "bin"), None),
            P(("sector", "bin"), None, None),
            P(None, "sector", "bin"),
        ),
        out_specs=(P(None, ("sector", "bin")), P("sector", None)),
        check_vma=False,
    )
```

```python
import functools

import jax
import jax.numpy as jnp
from jax import lax
from jax.experimental import pallas as pl
from jax.experimental.pallas import tpu as pltpu
from jax.sharding import PartitionSpec as P

stiff_pair = 50.0
damp_pair = 2.0
stiff_wall = 50.0
time_step = 0.01
gravity = 9.81
body_mass = 4.0
body_inertia = 40.0

LANES = 128
PAYLOAD = ((0, 3), (1, 4), (2, 5), (6, None))
PAIR_BLOCK = 1024
SPREAD = 4


def iota(shape, dim):
    return lax.broadcasted_iota(jnp.int32, shape, dim)


def split3(x):
    hi = x.astype(jnp.bfloat16).astype(jnp.float32)
    rest = x - hi
    mid = rest.astype(jnp.bfloat16).astype(jnp.float32)
    return hi, mid, rest - mid


def dot(a, b, contract=((1,), (0,))):
    return lax.dot_general(a, b, (contract, ((), ())), preferred_element_type=jnp.float32)


def pack_kernel(dest_ref, state_ref, out_ref):
    blocks = dest_ref.shape[0]
    ndevices = out_ref.shape[0] * LANES // (8 * 64)
    capacity = 64
    dest = dest_ref[...]
    upper = (iota((LANES, LANES), 0) <= iota((LANES, LANES), 1)).astype(jnp.bfloat16)
    named = [
        (dest[b : b + 1] == iota((ndevices, LANES), 0)).astype(jnp.float32) for b in range(blocks)
    ]
    counted = dot(jnp.concatenate(named, 0).astype(jnp.bfloat16), upper)
    before = jnp.full((ndevices, LANES), -1.0, jnp.float32)
    ranks = []
    for b in range(blocks):
        mine = counted[b * ndevices : (b + 1) * ndevices]
        ranks.append(jnp.sum(named[b] * (mine + before), 0, keepdims=True))
        before = before + jnp.broadcast_to(mine[:, LANES - 1 :], (ndevices, LANES))
    rank_row = jnp.concatenate(ranks, 1)
    dest_row = jnp.concatenate([dest[b : b + 1] for b in range(blocks)], 1)
    leaving = blocks * LANES
    chosen = dest_row == iota((ndevices, leaving), 0)
    slot = (iota((LANES, leaving), 0) % capacity).astype(jnp.float32)
    at_rank = (rank_row == slot).astype(jnp.float32).astype(jnp.bfloat16)
    groups = len(PAYLOAD)
    sources = [pair[half] for half in range(2) for pair in PAYLOAD if pair[half] is not None]
    rows = [
        jnp.where(chosen, part[source : source + 1], 0.0).astype(jnp.bfloat16)
        for part in split3(state_ref[...])
        for source in sources
    ]
    pieces = dot(jnp.concatenate(rows, 0), at_rank, ((1,), (1,)))
    height = len(sources) * ndevices
    out = (pieces[:height] + pieces[height : 2 * height]) + pieces[2 * height :]
    low = iota((ndevices, LANES), 1) < capacity
    for k, pair in enumerate(PAYLOAD):
        halves = []
        for source in pair:
            if source is None:
                halves.append(jnp.zeros((ndevices, LANES), jnp.float32))
            else:
                place = sources.index(source) * ndevices
                halves.append(out[place : place + ndevices])
        out_ref[pl.ds(k, ndevices, stride=groups), :] = jnp.where(low, halves[0], halves[1])


def quotient(code, size):
    power = size & (size - 1) == 0
    return lax.shift_right_logical(code, size.bit_length() - 1) if power else lax.div(code, size)


def remainder(code, size):
    return code & (size - 1) if size & (size - 1) == 0 else lax.rem(code, size)


def total_of(x):
    return jnp.sum(jnp.sum(x, 0, keepdims=True), 1, keepdims=True)


def state_tile(arrived_ref, tile):
    words = arrived_ref[8 * tile : 8 * tile + 8, :]
    swapped = pltpu.roll(pltpu.roll(words, 64, 1), 4, 0)
    same = (iota((8, LANES), 0) < 4) == (iota((8, LANES), 1) < 64)
    return jnp.where(same, words, swapped)


def facet_kernel(sectors, *refs):
    bodies_ref = refs[0]
    tri_refs = refs[1 : 1 + sectors]
    facet, raw, tri_sem = refs[1 + sectors :]
    entries = bodies_ref.shape[1]
    me = lax.axis_index("sector")

    def fetch(entry, source):
        return pltpu.make_async_copy(tri_refs[source], raw.at[entry], tri_sem.at[entry])

    for entry in range(entries):
        relative = bodies_ref[0, entry] ^ me
        for source in range(sectors):

            @pl.when(relative == source)
            def _():
                fetch(entry, source).start()

    for entry in range(entries):
        fetch(entry, 0).wait()
        corner = [raw[entry, i] for i in range(3)]
        one = [raw[entry, 3 + i] - corner[i] for i in range(3)]
        two = [raw[entry, 6 + i] - corner[i] for i in range(3)]
        d11 = one[0] * one[0] + one[1] * one[1] + one[2] * one[2]
        d12 = one[0] * two[0] + one[1] * two[1] + one[2] * two[2]
        d22 = two[0] * two[0] + two[1] * two[1] + two[2] * two[2]
        inverse = 1.0 / (d11 * d22 - d12 * d12)
        for i in range(3):
            facet[entry, i] = corner[i]
            facet[entry, 3 + i] = one[i]
            facet[entry, 6 + i] = two[i]
            facet[entry, 9 + i] = (d22 * one[i] - d12 * two[i]) * inverse
            facet[entry, 12 + i] = (d11 * two[i] - d12 * one[i]) * inverse


def sphere_side(state, row8):
    square = state * state
    level = square[3:4] - (square[0:1] + square[1:2] + square[2:3])
    other = jnp.where(state[3:4] > 0.0, level, -3.0e38)
    return level, jnp.where(
        row8 < 4, state, jnp.where(row8 == 4, 1.0, jnp.where(row8 == 5, other, jnp.where(row8 == 6, square[3:4], 0.0)))
    )


def wall_kernel(sectors, bins, *refs):
    bodies_ref, codes_ref, facet, arrived_ref, wrench_ref, force_ref, left = refs[:7]
    spread, place, gathered = refs[7:10]
    accs = refs[10:]
    entries = bodies_ref.shape[1]
    codes = codes_ref.shape[2]
    tiles_tri = facet.shape[2]
    tiles = arrived_ref.shape[0] // 8
    row8 = iota((8, LANES), 0)

    wanted = iota((48, 4 * LANES), 1) // LANES
    wanted = jnp.where(wanted == 3, 6, wanted)
    row = iota((48, 4 * LANES), 0)
    select = (row % 8 == wanted) & ((row // 8 == 0) | (row // 8 == 1) | (row // 8 == 3))
    select = select.astype(jnp.float32).astype(jnp.bfloat16)
    for tile in range(tiles):
        at = slice(tile * LANES, (tile + 1) * LANES)
        state = state_tile(arrived_ref, tile)
        jh, jm, jl = split3(sphere_side(state, row8)[1])
        left[at, 0:48] = jnp.transpose(jnp.concatenate([jh, jm, jh, jl, jh, jm], 0)).astype(jnp.bfloat16)
        for i in range(3):
            place[i, tile : tile + 1, :] = state[i : i + 1]
    for group in range(tiles // SPREAD):
        at = slice(group * SPREAD * LANES, (group + 1) * SPREAD * LANES)
        wide = dot(left[at, 0:48], select)
        for i in range(4):
            spread[i, at, :] = wide[:, i * LANES : (i + 1) * LANES]
    for acc in accs:
        acc[...] = jnp.zeros_like(acc)

    def one_tile(entry, number):
        code = codes_ref[0, entry, number]
        first = pl.multiple_of(quotient(code, tiles_tri) * LANES, LANES)
        facet_tile = remainder(code, tiles_tri)
        f = [facet[entry, i, pl.ds(facet_tile, 1), :] for i in range(15)]
        at = pl.ds(first, LANES)
        dx, dy, dz = spread[0, at, :] - f[0], spread[1, at, :] - f[1], spread[2, at, :] - f[2]
        beta = dx * f[9] + dy * f[10] + dz * f[11]
        gamma = dx * f[12] + dy * f[13] + dz * f[14]
        alpha = jnp.maximum(1.0 - beta - gamma, 0.0)
        beta = jnp.maximum(beta, 0.0)
        gamma = jnp.maximum(gamma, 0.0)
        scale = 1.0 / (alpha + beta + gamma)
        beta = beta * scale
        gamma = gamma * scale
        ox = dx - beta * f[3] - gamma * f[6]
        oy = dy - beta * f[4] - gamma * f[7]
        oz = dz - beta * f[5] - gamma * f[8]
        deep = jnp.maximum(spread[3, at, :] - (ox * ox + oy * oy + oz * oz), 0.0)
        accs[3 * entry][at, :] += deep * ox
        accs[3 * entry + 1][at, :] += deep * oy
        accs[3 * entry + 2][at, :] += deep * oz

    def step(number, carry):
        for entry in range(entries):
            one_tile(entry, number)
        return carry

    lax.fori_loop(0, codes, step, 0)

    ones = jnp.ones((16, 2 * LANES), jnp.bfloat16)

    def gather(tile, carry):
        at = pl.ds(pl.multiple_of(tile * LANES, LANES), LANES)
        for which in range(3 * entries):
            value = accs[which][at, :]
            if which % 2:
                row = jnp.sum(jnp.transpose(value), 0, keepdims=True)
            else:
                high = value.astype(jnp.bfloat16)
                low = (value - high.astype(jnp.float32)).astype(jnp.bfloat16)
                row = dot(ones, jnp.concatenate([high, low], 1), ((1,), (1,)))
            gathered[which, pl.ds(tile, 1), :] = row[0:1]
        return carry

    lax.fori_loop(0, tiles, gather, 0, unroll=8)
    x, y, z = place[0], place[1], place[2]
    owner = iota((sectors * bins, LANES), 0) // bins
    lane = iota((1, LANES), 1)
    out = jnp.zeros((sectors * bins, LANES), jnp.float32)
    whole = [0.0, 0.0, 0.0]
    for entry in range(entries):
        fx, fy, fz = (gathered[3 * entry + i] for i in range(3))
        parts = (fx, fy, fz, y * fz - z * fy, z * fx - x * fz, x * fy - y * fx)
        mine = jnp.zeros((1, LANES), jnp.float32)
        for i, part in enumerate(parts):
            scale = time_step / (body_mass if i < 3 else body_inertia)
            mine = jnp.where(lane == i, total_of(part) * scale, mine)
        out = out + jnp.where(owner == bodies_ref[0, entry], mine * (-stiff_wall), 0.0)
        whole = [whole[0] + fx, whole[1] + fy, whole[2] + fz]
    wrench_ref[...] = out
    for i in range(3):
        force_ref[i] = stiff_wall * whole[i]


def pair_kernel(arrived_ref, force_ref, left, out_hbm, right, moved, out_ref, out_sem):
    tiles = arrived_ref.shape[0] // 8
    blocks = tiles * LANES // PAIR_BLOCK
    row8 = iota((8, LANES), 0)
    for tile in range(tiles):
        at = slice(tile * LANES, (tile + 1) * LANES)
        state = state_tile(arrived_ref, tile)
        level = sphere_side(state, row8)[0]
        i_side = jnp.where(row8 < 4, 2.0 * state, jnp.where(row8 == 4, level, jnp.where(row8 == 5, 1.0, 0.0)))
        ih, im, il = split3(i_side)
        right[:, at] = jnp.concatenate([ih, ih, im, ih, il, im], 0).astype(jnp.bfloat16)
        value = jnp.where(row8 == 3, 1.0, state)
        moved[:, at] = jnp.concatenate(list(split3(value)) + [jnp.zeros((8, LANES), jnp.float32)], 0).astype(
            jnp.bfloat16
        )

    def block_of(ib, carry):
        columns = pl.ds(pl.multiple_of(ib * PAIR_BLOCK, PAIR_BLOCK), PAIR_BLOCK)
        mine = right[:, columns]
        total = jnp.zeros((32, PAIR_BLOCK), jnp.float32)
        for jb in range(blocks):
            rows = slice(jb * PAIR_BLOCK, (jb + 1) * PAIR_BLOCK)
            weight = jnp.maximum(dot(left[rows, 0:48], mine), 0.0)
            high = weight.astype(jnp.bfloat16)
            low = (weight - high.astype(jnp.float32)).astype(jnp.bfloat16)
            values = moved[:, rows]
            total = total + (dot(values, high) + dot(values, low))
        total = total[0:8] + total[8:16] + total[16:24]
        for part in range(PAIR_BLOCK // LANES):
            tile = ib * (PAIR_BLOCK // LANES) + part
            words = arrived_ref[pl.ds(pl.multiple_of(8 * tile, 8), 8), :]
            swapped = pltpu.roll(pltpu.roll(words, 64, 1), 4, 0)
            state = jnp.where((row8 < 4) == (iota((8, LANES), 1) < 64), words, swapped)
            moment = total[:, part * LANES : (part + 1) * LANES]
            differ = moment[3:4] * state - moment
            force = stiff_pair * differ - damp_pair * pltpu.roll(differ, 4, 0)
            for i in range(3):
                force = force + jnp.where(row8 == i, force_ref[i, pl.ds(tile, 1), :], 0.0)
            radius = jnp.broadcast_to(state[3:4], (8, LANES))
            live = radius > 0.0
            mass = jnp.where(live, radius * radius * radius, 1.0)
            falling = jnp.where(row8 == 6, gravity, 0.0)
            speed = state + time_step * (pltpu.roll(force, 4, 0) / mass - falling)
            place = state + time_step * pltpu.roll(speed, 4, 0)
            result = jnp.where(
                row8 < 3, place, jnp.where(row8 < 6, pltpu.roll(speed, 7, 0), pltpu.roll(state, 3, 0))
            )
            result = jnp.where(live, result, 0.0)
            out_ref[:, pl.ds(pl.multiple_of(tile * LANES, LANES), LANES)] = result[0:7]
        leave(ib).start()
        return carry

    def leave(ib):
        columns = pl.ds(pl.multiple_of(ib * PAIR_BLOCK, PAIR_BLOCK), PAIR_BLOCK)
        return pltpu.make_async_copy(out_ref.at[:, columns], out_hbm.at[:, columns], out_sem.at[ib])

    lax.fori_loop(0, blocks, block_of, 0)
    for ib in range(blocks):
        leave(ib).wait()


def whole_vmem():
    return pl.BlockSpec(memory_space=pltpu.VMEM)


def whole_smem():
    return pl.BlockSpec(memory_space=pltpu.SMEM)


def near(x):
    return pltpu.with_memory_space_constraint(x, pltpu.VMEM)


def fast(sph_state, sph_dest, body_list, tile_codes, triangles):
    sectors = lax.axis_size("sector")
    bins = lax.axis_size("bin")
    ndevices = sectors * bins
    leaving = sph_state.shape[1]
    slots = 2 * leaving
    words = 8 * slots // LANES
    block = triangles.reshape(triangles.shape[0], -1, LANES)
    outgoing = pl.pallas_call(
        pack_kernel,
        out_shape=pltpu.VMEM((words, LANES), jnp.float32),
        in_specs=[whole_vmem(), whole_vmem()],
        out_specs=whole_vmem(),
        name="pack",
    )(sph_dest.reshape(-1, LANES), sph_state)
    blocks = [block] + [
        lax.ppermute(block, "sector", [(i, i ^ step) for i in range(sectors)]) for step in range(1, sectors)
    ]
    outgoing = outgoing.reshape(ndevices, 1, words * LANES // ndevices)
    arrived = lax.all_to_all(outgoing, ("sector", "bin"), split_axis=0, concat_axis=0, tiled=True)
    arrived = arrived.reshape(words, LANES)
    entries = body_list.shape[1]
    column = pltpu.VMEM((slots, LANES), jnp.float32)
    tiles = slots // LANES
    facets = pl.pallas_call(
        functools.partial(facet_kernel, sectors),
        out_shape=pltpu.VMEM((entries, 15) + block.shape[1:], jnp.float32),
        in_specs=[whole_smem(), pl.BlockSpec(memory_space=pltpu.HBM)] + [whole_vmem()] * (sectors - 1),
        out_specs=whole_vmem(),
        scratch_shapes=[pltpu.VMEM((entries,) + block.shape, jnp.float32), pltpu.SemaphoreType.DMA((entries,))],
        name="facet",
    )(body_list, blocks[0], *[near(other) for other in blocks[1:]])
    wrench, force, left = pl.pallas_call(
        functools.partial(wall_kernel, sectors, bins),
        out_shape=[
            pltpu.VMEM((ndevices, LANES), jnp.float32),
            pltpu.VMEM((3, tiles, LANES), jnp.float32),
            pltpu.VMEM((slots, LANES), jnp.bfloat16),
        ],
        in_specs=[whole_smem(), whole_smem()] + [whole_vmem()] * 2,
        out_specs=[whole_vmem()] * 3,
        scratch_shapes=[
            pltpu.VMEM((4, slots, LANES), jnp.float32),
            pltpu.VMEM((3, tiles, LANES), jnp.float32),
            pltpu.VMEM((3 * entries, tiles, LANES), jnp.float32),
        ]
        + [column] * (3 * entries),
        name="wall",
    )(body_list, tile_codes, near(facets), near(arrived))
    shared = lax.all_to_all(
        wrench.reshape(ndevices, 1, LANES), ("sector", "bin"), split_axis=0, concat_axis=0, tiled=True
    )
    new_block = pl.pallas_call(
        pair_kernel,
        out_shape=jax.ShapeDtypeStruct((7, slots), jnp.float32),
        in_specs=[whole_vmem()] * 3,
        out_specs=pl.BlockSpec(memory_space=pltpu.HBM),
        scratch_shapes=[
            pltpu.VMEM((48, slots), jnp.bfloat16),
            pltpu.VMEM((32, slots), jnp.bfloat16),
            pltpu.VMEM((7, slots), jnp.float32),
            pltpu.SemaphoreType.DMA((slots // PAIR_BLOCK,)),
        ],
        name="pair",
    )(near(arrived), near(force), near(left))
    kick = jnp.sum(shared[:, 0, :6], 0, keepdims=True)
    return new_block, kick


def contact(spheres, facets):
    centre = spheres[0:3]
    radius = spheres[3]
    corner = facets[0:3]
    edge_one = facets[3:6] - corner
    edge_two = facets[6:9] - corner
    square_one = jnp.sum(edge_one * edge_one, 0)
    square_two = jnp.sum(edge_two * edge_two, 0)
    cross_term = jnp.sum(edge_one * edge_two, 0)
    inverse = 1.0 / (square_one * square_two - cross_term * cross_term)
    relative = centre[:, :, None] - corner[:, None, :]
    along_one = jnp.sum(relative * edge_one[:, None, :], 0)
    along_two = jnp.sum(relative * edge_two[:, None, :], 0)
    weight_b = (square_two * along_one - cross_term * along_two) * inverse
    weight_c = (square_one * along_two - cross_term * along_one) * inverse
    weight_a = jnp.maximum(1.0 - weight_b - weight_c, 0.0)
    weight_b = jnp.maximum(weight_b, 0.0)
    weight_c = jnp.maximum(weight_c, 0.0)
    totals = weight_a + weight_b + weight_c
    weight_b = weight_b / totals
    weight_c = weight_c / totals
    nearest = (
        corner[:, None, :]
        + weight_b[None] * edge_one[:, None, :]
        + weight_c[None] * edge_two[:, None, :]
    )
    offset = centre[:, :, None] - nearest
    squared = jnp.sum(offset * offset, 0)
    strength = stiff_wall * jnp.maximum(radius[:, None] * radius[:, None] - squared, 0.0)
    forces = strength[None] * offset
    on_spheres = jnp.sum(forces, 2)
    on_body = -jnp.sum(forces, (1, 2))
    torque = -jnp.sum(jnp.cross(nearest, forces, axis=0), (1, 2))
    return (on_spheres, jnp.concatenate([on_body, torque]))


def tile_forces(spheres, facets, tile_list):
    tiles_tri = facets.shape[1] // 128

    def advance_tile(carried, tile_code):
        forces, wrench = carried
        sphere_tile = tile_code // tiles_tri
        facet_tile = tile_code % tiles_tri
        sphere_part = lax.dynamic_slice_in_dim(spheres, sphere_tile * 128, 128, 1)
        facet_part = lax.dynamic_slice_in_dim(facets, facet_tile * 128, 128, 1)
        on_spheres, on_body = contact(sphere_part, facet_part)
        current = lax.dynamic_slice_in_dim(forces, sphere_tile * 128, 128, 1)
        forces = lax.dynamic_update_slice_in_dim(forces, current + on_spheres, sphere_tile * 128, 1)
        return ((forces, wrench + on_body), None)

    initial = (jnp.zeros((3, spheres.shape[1]), jnp.float32), jnp.zeros((6,), jnp.float32))
    (forces, wrench), unused = lax.scan(advance_tile, initial, tile_list)
    return (forces, wrench)


def sphere_forces(sphere_block):
    position = sphere_block[0:3]
    velocity = sphere_block[3:6]
    radius = sphere_block[6]
    width_all = sphere_block.shape[1]
    occupied = (radius > 0).astype(jnp.float32)
    coords = jnp.concatenate([position, radius[None]], 0)
    baseline = radius * radius - jnp.sum(position * position, 0)
    stacked = jnp.concatenate([position, velocity, jnp.ones((1, width_all), jnp.float32)], 0)
    row_block = 512

    def row_group(row_start):
        coords_rows = lax.dynamic_slice_in_dim(coords, row_start, row_block, 1)
        base_rows = lax.dynamic_slice_in_dim(baseline, row_start, row_block, 0)
        live_rows = lax.dynamic_slice_in_dim(occupied, row_start, row_block, 0)
        inner_products = lax.dot_general(
            coords_rows, coords, (((0,), (0,)), ((), ())), precision=lax.Precision.HIGHEST
        )
        intersection = jnp.maximum(
            base_rows[:, None] + baseline[None, :] + 2.0 * inner_products, 0.0
        )
        intersection = intersection * live_rows[:, None] * occupied[None, :]
        return lax.dot_general(
            stacked, intersection, (((1,), (1,)), ((), ())), precision=lax.Precision.HIGHEST
        )

    starts = jnp.arange(width_all // row_block, dtype=jnp.int32) * row_block
    grouped = lax.map(row_group, starts)
    weighted = jnp.transpose(grouped, (1, 0, 2)).reshape(7, width_all)
    totals = weighted[6]
    return stiff_pair * (totals * position - weighted[0:3]) - damp_pair * (
        totals * velocity - weighted[3:6]
    )


def advance(sphere_block, forces):
    position = sphere_block[0:3]
    velocity = sphere_block[3:6]
    radius = sphere_block[6]
    occupied = radius > 0
    masses = jnp.where(occupied, radius * radius * radius, 1.0)
    falling = jnp.array([0.0, 0.0, gravity], jnp.float32)
    acceleration = forces / masses[None] - falling[:, None]
    velocity_new = velocity + time_step * acceleration
    position_new = position + time_step * velocity_new
    result = jnp.concatenate([position_new, velocity_new, radius[None]], 0)
    return jnp.where(occupied[None], result, 0.0)


def bin_total(partial_row):
    return lax.psum(partial_row, "bin")


def general(sph_state, sph_dest, body_list, tile_codes, triangles):
    sectors = lax.axis_size("sector")
    bins = lax.axis_size("bin")
    ndevices = sectors * bins
    leaving = sph_state.shape[1]
    capacity = 2 * leaving // ndevices
    targets = sph_dest[:, 0]
    onehot = (targets[:, None] == jnp.arange(ndevices, dtype=jnp.int32)[None, :]).astype(jnp.int32)
    ranks = jnp.sum((jnp.cumsum(onehot, 0) - 1) * onehot, 1)
    columns = targets * capacity + ranks
    outgoing = jnp.zeros((7, ndevices * capacity), jnp.float32).at[:, columns].set(sph_state)
    outgoing = outgoing.reshape(7, sectors, bins, capacity)
    arrived = lax.all_to_all(
        lax.all_to_all(outgoing, "sector", split_axis=1, concat_axis=1, tiled=True),
        "bin",
        split_axis=2,
        concat_axis=2,
        tiled=True,
    )
    sphere_block = arrived.reshape(7, ndevices * capacity)
    width_all = sphere_block.shape[1]
    coords = jnp.concatenate([sphere_block[0:3], sphere_block[6:7]], 0)
    pair_total = sphere_forces(sphere_block)
    everyone = lax.all_gather(triangles, "sector", axis=1, tiled=True)
    wall_total = jnp.zeros((3, width_all), jnp.float32)
    partial_value = jnp.zeros((sectors, 6), jnp.float32)
    for slot_index in range(body_list.shape[1]):
        owner_body = body_list[0, slot_index]
        facets = lax.dynamic_index_in_dim(everyone, owner_body, 1, keepdims=False)
        on_spheres, on_body = tile_forces(coords, facets, tile_codes[0, slot_index])
        wall_total = wall_total + on_spheres
        selector = (jnp.arange(sectors, dtype=jnp.int32) == owner_body).astype(jnp.float32)
        partial_value = partial_value + selector[:, None] * on_body[None, :]
    own_row = lax.psum_scatter(partial_value, "sector", scatter_dimension=0, tiled=True)
    own_row = bin_total(own_row)
    new_block = advance(sphere_block, pair_total + wall_total)
    scaling = jnp.array([time_step / body_mass] * 3 + [time_step / body_inertia] * 3, jnp.float32)
    return (new_block, own_row * scaling[None, :])


def local(sph_state, sph_dest, body_list, tile_codes, triangles):
    sectors = lax.axis_size("sector")
    ndevices = sectors * lax.axis_size("bin")
    leaving = sph_state.shape[1]
    fits = 2 * leaving == 64 * ndevices and 16 * leaving == LANES * LANES and sectors & (sectors - 1) == 0
    chosen = fast if fits else general
    return chosen(sph_state, sph_dest, body_list, tile_codes, triangles)


def solution(mesh):
    return jax.shard_map(
        local,
        mesh=mesh,
        in_specs=(
            P(None, ("sector", "bin")),
            P(("sector", "bin"), None),
            P(("sector", "bin"), None),
            P(("sector", "bin"), None, None),
            P(None, "sector", "bin"),
        ),
        out_specs=(P(None, ("sector", "bin")), P("sector", None)),
        check_vma=False,
    )
```

```python
import functools

import jax
import jax.numpy as jnp
from jax import lax
from jax.experimental import pallas as pl
from jax.experimental.pallas import tpu as pltpu
from jax.sharding import PartitionSpec as P

stiff_pair = 50.0
damp_pair = 2.0
stiff_wall = 50.0
time_step = 0.01
gravity = 9.81
body_mass = 4.0
body_inertia = 40.0

LANES = 128
PAYLOAD = ((0, 3), (1, 4), (2, 5), (6, None))
PAIR_BLOCK = 1024
SPREAD = 4
WALL_ROWS = 64


def iota(shape, dim):
    return lax.broadcasted_iota(jnp.int32, shape, dim)


def split3(x):
    hi = x.astype(jnp.bfloat16).astype(jnp.float32)
    rest = x - hi
    mid = rest.astype(jnp.bfloat16).astype(jnp.float32)
    return hi, mid, rest - mid


def dot(a, b, contract=((1,), (0,))):
    return lax.dot_general(a, b, (contract, ((), ())), preferred_element_type=jnp.float32)


def pack_kernel(dest_ref, state_ref, out_ref):
    blocks = dest_ref.shape[0]
    ndevices = out_ref.shape[0] * LANES // (8 * 64)
    capacity = 64
    dest = dest_ref[...]
    upper = (iota((LANES, LANES), 0) <= iota((LANES, LANES), 1)).astype(jnp.bfloat16)
    named = [
        (dest[b : b + 1] == iota((ndevices, LANES), 0)).astype(jnp.float32) for b in range(blocks)
    ]
    counted = dot(jnp.concatenate(named, 0).astype(jnp.bfloat16), upper)
    before = jnp.full((ndevices, LANES), -1.0, jnp.float32)
    ranks = []
    for b in range(blocks):
        mine = counted[b * ndevices : (b + 1) * ndevices]
        ranks.append(jnp.sum(named[b] * (mine + before), 0, keepdims=True))
        before = before + jnp.broadcast_to(mine[:, LANES - 1 :], (ndevices, LANES))
    rank_row = jnp.concatenate(ranks, 1)
    dest_row = jnp.concatenate([dest[b : b + 1] for b in range(blocks)], 1)
    leaving = blocks * LANES
    chosen = dest_row == iota((ndevices, leaving), 0)
    slot = (iota((LANES, leaving), 0) % capacity).astype(jnp.float32)
    at_rank = (rank_row == slot).astype(jnp.float32).astype(jnp.bfloat16)
    groups = len(PAYLOAD)
    sources = [pair[half] for half in range(2) for pair in PAYLOAD if pair[half] is not None]
    rows = [
        jnp.where(chosen, part[source : source + 1], 0.0).astype(jnp.bfloat16)
        for part in split3(state_ref[...])
        for source in sources
    ]
    pieces = dot(jnp.concatenate(rows, 0), at_rank, ((1,), (1,)))
    height = len(sources) * ndevices
    out = (pieces[:height] + pieces[height : 2 * height]) + pieces[2 * height :]
    low = iota((ndevices, LANES), 1) < capacity
    for k, pair in enumerate(PAYLOAD):
        halves = []
        for source in pair:
            if source is None:
                halves.append(jnp.zeros((ndevices, LANES), jnp.float32))
            else:
                place = sources.index(source) * ndevices
                halves.append(out[place : place + ndevices])
        out_ref[pl.ds(k, ndevices, stride=groups), :] = jnp.where(low, halves[0], halves[1])


def quotient(code, size):
    power = size & (size - 1) == 0
    return lax.shift_right_logical(code, size.bit_length() - 1) if power else lax.div(code, size)


def remainder(code, size):
    return code & (size - 1) if size & (size - 1) == 0 else lax.rem(code, size)


def total_of(x):
    return jnp.sum(jnp.sum(x, 0, keepdims=True), 1, keepdims=True)


def state_tile(arrived_ref, tile):
    words = arrived_ref[8 * tile : 8 * tile + 8, :]
    swapped = pltpu.roll(pltpu.roll(words, 64, 1), 4, 0)
    same = (iota((8, LANES), 0) < 4) == (iota((8, LANES), 1) < 64)
    return jnp.where(same, words, swapped)


def facet_kernel(sectors, *refs):
    bodies_ref = refs[0]
    tri_refs = refs[1 : 1 + sectors]
    facet, raw, tri_sem = refs[1 + sectors :]
    entries = bodies_ref.shape[1]
    me = lax.axis_index("sector")

    def fetch(entry, source):
        return pltpu.make_async_copy(tri_refs[source], raw.at[entry], tri_sem.at[entry])

    for entry in range(entries):
        relative = bodies_ref[0, entry] ^ me
        for source in range(sectors):

            @pl.when(relative == source)
            def _():
                fetch(entry, source).start()

    for entry in range(entries):
        fetch(entry, 0).wait()
        corner = [raw[entry, i] for i in range(3)]
        one = [raw[entry, 3 + i] - corner[i] for i in range(3)]
        two = [raw[entry, 6 + i] - corner[i] for i in range(3)]
        d11 = one[0] * one[0] + one[1] * one[1] + one[2] * one[2]
        d12 = one[0] * two[0] + one[1] * two[1] + one[2] * two[2]
        d22 = two[0] * two[0] + two[1] * two[1] + two[2] * two[2]
        inverse = 1.0 / (d11 * d22 - d12 * d12)
        for i in range(3):
            facet[entry, i] = corner[i]
            facet[entry, 3 + i] = one[i]
            facet[entry, 6 + i] = two[i]
            facet[entry, 9 + i] = (d22 * one[i] - d12 * two[i]) * inverse
            facet[entry, 12 + i] = (d11 * two[i] - d12 * one[i]) * inverse


def sphere_side(state, row8):
    square = state * state
    level = square[3:4] - (square[0:1] + square[1:2] + square[2:3])
    other = jnp.where(state[3:4] > 0.0, level, -3.0e38)
    return level, jnp.where(
        row8 < 4, state, jnp.where(row8 == 4, 1.0, jnp.where(row8 == 5, other, jnp.where(row8 == 6, square[3:4], 0.0)))
    )


def wall_kernel(sectors, bins, *refs):
    bodies_ref, codes_ref, facet, arrived_ref, wrench_ref, force_ref, left = refs[:7]
    spread, place, gathered = refs[7:10]
    accs = refs[10:]
    entries = bodies_ref.shape[1]
    codes = codes_ref.shape[2]
    tiles_tri = facet.shape[2]
    tiles = arrived_ref.shape[0] // 8
    row8 = iota((8, LANES), 0)

    wanted = iota((48, 4 * LANES), 1) // LANES
    wanted = jnp.where(wanted == 3, 6, wanted)
    row = iota((48, 4 * LANES), 0)
    select = (row % 8 == wanted) & ((row // 8 == 0) | (row // 8 == 1) | (row // 8 == 3))
    select = select.astype(jnp.float32).astype(jnp.bfloat16)
    for tile in range(tiles):
        at = slice(tile * LANES, (tile + 1) * LANES)
        state = state_tile(arrived_ref, tile)
        jh, jm, jl = split3(sphere_side(state, row8)[1])
        left[at, 0:48] = jnp.transpose(jnp.concatenate([jh, jm, jh, jl, jh, jm], 0)).astype(jnp.bfloat16)
        for i in range(3):
            place[i, tile : tile + 1, :] = state[i : i + 1]
    for group in range(tiles // SPREAD):
        at = slice(group * SPREAD * LANES, (group + 1) * SPREAD * LANES)
        wide = dot(left[at, 0:48], select)
        for i in range(4):
            spread[i, at, :] = wide[:, i * LANES : (i + 1) * LANES]
    for acc in accs:
        acc[...] = jnp.zeros_like(acc)

    def one_tile(entry, number):
        code = codes_ref[0, entry, number]
        first = pl.multiple_of(quotient(code, tiles_tri) * LANES, LANES)
        facet_tile = remainder(code, tiles_tri)
        f = [facet[entry, i, pl.ds(facet_tile, 1), :] for i in range(15)]
        for part in range(LANES // WALL_ROWS):
            at = pl.ds(pl.multiple_of(first + part * WALL_ROWS, WALL_ROWS), WALL_ROWS)
            dx, dy, dz = spread[0, at, :] - f[0], spread[1, at, :] - f[1], spread[2, at, :] - f[2]
            beta = dx * f[9] + dy * f[10] + dz * f[11]
            gamma = dx * f[12] + dy * f[13] + dz * f[14]
            alpha = jnp.maximum(1.0 - beta - gamma, 0.0)
            beta = jnp.maximum(beta, 0.0)
            gamma = jnp.maximum(gamma, 0.0)
            scale = 1.0 / (alpha + beta + gamma)
            beta = beta * scale
            gamma = gamma * scale
            ox = dx - beta * f[3] - gamma * f[6]
            oy = dy - beta * f[4] - gamma * f[7]
            oz = dz - beta * f[5] - gamma * f[8]
            deep = jnp.maximum(spread[3, at, :] - (ox * ox + oy * oy + oz * oz), 0.0)
            accs[3 * entry][at, :] += deep * ox
            accs[3 * entry + 1][at, :] += deep * oy
            accs[3 * entry + 2][at, :] += deep * oz

    def step(number, carry):
        for entry in range(entries):
            one_tile(entry, number)
        return carry

    lax.fori_loop(0, codes, step, 0)

    ones = jnp.ones((16, 2 * LANES), jnp.bfloat16)

    def gather(tile, carry):
        at = pl.ds(pl.multiple_of(tile * LANES, LANES), LANES)
        for which in range(3 * entries):
            value = accs[which][at, :]
            if which % 2:
                row = jnp.sum(jnp.transpose(value), 0, keepdims=True)
            else:
                high = value.astype(jnp.bfloat16)
                low = (value - high.astype(jnp.float32)).astype(jnp.bfloat16)
                row = dot(ones, jnp.concatenate([high, low], 1), ((1,), (1,)))
            gathered[which, pl.ds(tile, 1), :] = row[0:1]
        return carry

    lax.fori_loop(0, tiles, gather, 0, unroll=8)
    x, y, z = place[0], place[1], place[2]
    owner = iota((sectors * bins, LANES), 0) // bins
    lane = iota((1, LANES), 1)
    out = jnp.zeros((sectors * bins, LANES), jnp.float32)
    whole = [0.0, 0.0, 0.0]
    for entry in range(entries):
        fx, fy, fz = (gathered[3 * entry + i] for i in range(3))
        parts = (fx, fy, fz, y * fz - z * fy, z * fx - x * fz, x * fy - y * fx)
        mine = jnp.zeros((1, LANES), jnp.float32)
        for i, part in enumerate(parts):
            scale = time_step / (body_mass if i < 3 else body_inertia)
            mine = jnp.where(lane == i, total_of(part) * scale, mine)
        out = out + jnp.where(owner == bodies_ref[0, entry], mine * (-stiff_wall), 0.0)
        whole = [whole[0] + fx, whole[1] + fy, whole[2] + fz]
    wrench_ref[...] = out
    for i in range(3):
        force_ref[i] = stiff_wall * whole[i]


def pair_kernel(arrived_ref, force_ref, left, out_hbm, right, moved, out_ref, out_sem):
    tiles = arrived_ref.shape[0] // 8
    blocks = tiles * LANES // PAIR_BLOCK
    row8 = iota((8, LANES), 0)
    for tile in range(tiles):
        at = slice(tile * LANES, (tile + 1) * LANES)
        state = state_tile(arrived_ref, tile)
        level = sphere_side(state, row8)[0]
        i_side = jnp.where(row8 < 4, 2.0 * state, jnp.where(row8 == 4, level, jnp.where(row8 == 5, 1.0, 0.0)))
        ih, im, il = split3(i_side)
        right[:, at] = jnp.concatenate([ih, ih, im, ih, il, im], 0).astype(jnp.bfloat16)
        value = jnp.where(row8 == 3, 1.0, state)
        moved[:, at] = jnp.concatenate(list(split3(value)) + [jnp.zeros((8, LANES), jnp.float32)], 0).astype(
            jnp.bfloat16
        )

    def block_of(ib, carry):
        columns = pl.ds(pl.multiple_of(ib * PAIR_BLOCK, PAIR_BLOCK), PAIR_BLOCK)
        mine = right[:, columns]
        total = jnp.zeros((32, PAIR_BLOCK), jnp.float32)
        for jb in range(blocks):
            rows = slice(jb * PAIR_BLOCK, (jb + 1) * PAIR_BLOCK)
            weight = jnp.maximum(dot(left[rows, 0:48], mine), 0.0)
            high = weight.astype(jnp.bfloat16)
            low = (weight - high.astype(jnp.float32)).astype(jnp.bfloat16)
            values = moved[:, rows]
            total = total + (dot(values, high) + dot(values, low))
        total = total[0:8] + total[8:16] + total[16:24]
        for part in range(PAIR_BLOCK // LANES):
            tile = ib * (PAIR_BLOCK // LANES) + part
            words = arrived_ref[pl.ds(pl.multiple_of(8 * tile, 8), 8), :]
            swapped = pltpu.roll(pltpu.roll(words, 64, 1), 4, 0)
            state = jnp.where((row8 < 4) == (iota((8, LANES), 1) < 64), words, swapped)
            moment = total[:, part * LANES : (part + 1) * LANES]
            differ = moment[3:4] * state - moment
            force = stiff_pair * differ - damp_pair * pltpu.roll(differ, 4, 0)
            for i in range(3):
                force = force + jnp.where(row8 == i, force_ref[i, pl.ds(tile, 1), :], 0.0)
            radius = jnp.broadcast_to(state[3:4], (8, LANES))
            live = radius > 0.0
            mass = jnp.where(live, radius * radius * radius, 1.0)
            falling = jnp.where(row8 == 6, gravity, 0.0)
            speed = state + time_step * (pltpu.roll(force, 4, 0) / mass - falling)
            place = state + time_step * pltpu.roll(speed, 4, 0)
            result = jnp.where(
                row8 < 3, place, jnp.where(row8 < 6, pltpu.roll(speed, 7, 0), pltpu.roll(state, 3, 0))
            )
            result = jnp.where(live, result, 0.0)
            out_ref[:, pl.ds(pl.multiple_of(tile * LANES, LANES), LANES)] = result[0:7]
        leave(ib).start()
        return carry

    def leave(ib):
        columns = pl.ds(pl.multiple_of(ib * PAIR_BLOCK, PAIR_BLOCK), PAIR_BLOCK)
        return pltpu.make_async_copy(out_ref.at[:, columns], out_hbm.at[:, columns], out_sem.at[ib])

    lax.fori_loop(0, blocks, block_of, 0)
    for ib in range(blocks):
        leave(ib).wait()


def whole_vmem():
    return pl.BlockSpec(memory_space=pltpu.VMEM)


def whole_smem():
    return pl.BlockSpec(memory_space=pltpu.SMEM)


def near(x):
    return pltpu.with_memory_space_constraint(x, pltpu.VMEM)


def fast(sph_state, sph_dest, body_list, tile_codes, triangles):
    sectors = lax.axis_size("sector")
    bins = lax.axis_size("bin")
    ndevices = sectors * bins
    leaving = sph_state.shape[1]
    slots = 2 * leaving
    words = 8 * slots // LANES
    block = triangles.reshape(triangles.shape[0], -1, LANES)
    outgoing = pl.pallas_call(
        pack_kernel,
        out_shape=pltpu.VMEM((words, LANES), jnp.float32),
        in_specs=[whole_vmem(), whole_vmem()],
        out_specs=whole_vmem(),
        name="pack",
    )(sph_dest.reshape(-1, LANES), sph_state)
    blocks = [block] + [
        lax.ppermute(block, "sector", [(i, i ^ step) for i in range(sectors)]) for step in range(1, sectors)
    ]
    outgoing = outgoing.reshape(ndevices, 1, words * LANES // ndevices)
    arrived = lax.all_to_all(outgoing, ("sector", "bin"), split_axis=0, concat_axis=0, tiled=True)
    arrived = arrived.reshape(words, LANES)
    entries = body_list.shape[1]
    column = pltpu.VMEM((slots, LANES), jnp.float32)
    tiles = slots // LANES
    facets = pl.pallas_call(
        functools.partial(facet_kernel, sectors),
        out_shape=pltpu.VMEM((entries, 15) + block.shape[1:], jnp.float32),
        in_specs=[whole_smem(), pl.BlockSpec(memory_space=pltpu.HBM)] + [whole_vmem()] * (sectors - 1),
        out_specs=whole_vmem(),
        scratch_shapes=[pltpu.VMEM((entries,) + block.shape, jnp.float32), pltpu.SemaphoreType.DMA((entries,))],
        name="facet",
    )(body_list, blocks[0], *[near(other) for other in blocks[1:]])
    wrench, force, left = pl.pallas_call(
        functools.partial(wall_kernel, sectors, bins),
        out_shape=[
            pltpu.VMEM((ndevices, LANES), jnp.float32),
            pltpu.VMEM((3, tiles, LANES), jnp.float32),
            pltpu.VMEM((slots, LANES), jnp.bfloat16),
        ],
        in_specs=[whole_smem(), whole_smem()] + [whole_vmem()] * 2,
        out_specs=[whole_vmem()] * 3,
        scratch_shapes=[
            pltpu.VMEM((4, slots, LANES), jnp.float32),
            pltpu.VMEM((3, tiles, LANES), jnp.float32),
            pltpu.VMEM((3 * entries, tiles, LANES), jnp.float32),
        ]
        + [column] * (3 * entries),
        name="wall",
    )(body_list, tile_codes, near(facets), near(arrived))
    shared = lax.all_to_all(
        wrench.reshape(ndevices, 1, LANES), ("sector", "bin"), split_axis=0, concat_axis=0, tiled=True
    )
    new_block = pl.pallas_call(
        pair_kernel,
        out_shape=jax.ShapeDtypeStruct((7, slots), jnp.float32),
        in_specs=[whole_vmem()] * 3,
        out_specs=pl.BlockSpec(memory_space=pltpu.HBM),
        scratch_shapes=[
            pltpu.VMEM((48, slots), jnp.bfloat16),
            pltpu.VMEM((32, slots), jnp.bfloat16),
            pltpu.VMEM((7, slots), jnp.float32),
            pltpu.SemaphoreType.DMA((slots // PAIR_BLOCK,)),
        ],
        name="pair",
    )(near(arrived), near(force), near(left))
    kick = jnp.sum(shared[:, 0, :6], 0, keepdims=True)
    return new_block, kick


def contact(spheres, facets):
    centre = spheres[0:3]
    radius = spheres[3]
    corner = facets[0:3]
    edge_one = facets[3:6] - corner
    edge_two = facets[6:9] - corner
    square_one = jnp.sum(edge_one * edge_one, 0)
    square_two = jnp.sum(edge_two * edge_two, 0)
    cross_term = jnp.sum(edge_one * edge_two, 0)
    inverse = 1.0 / (square_one * square_two - cross_term * cross_term)
    relative = centre[:, :, None] - corner[:, None, :]
    along_one = jnp.sum(relative * edge_one[:, None, :], 0)
    along_two = jnp.sum(relative * edge_two[:, None, :], 0)
    weight_b = (square_two * along_one - cross_term * along_two) * inverse
    weight_c = (square_one * along_two - cross_term * along_one) * inverse
    weight_a = jnp.maximum(1.0 - weight_b - weight_c, 0.0)
    weight_b = jnp.maximum(weight_b, 0.0)
    weight_c = jnp.maximum(weight_c, 0.0)
    totals = weight_a + weight_b + weight_c
    weight_b = weight_b / totals
    weight_c = weight_c / totals
    nearest = (
        corner[:, None, :]
        + weight_b[None] * edge_one[:, None, :]
        + weight_c[None] * edge_two[:, None, :]
    )
    offset = centre[:, :, None] - nearest
    squared = jnp.sum(offset * offset, 0)
    strength = stiff_wall * jnp.maximum(radius[:, None] * radius[:, None] - squared, 0.0)
    forces = strength[None] * offset
    on_spheres = jnp.sum(forces, 2)
    on_body = -jnp.sum(forces, (1, 2))
    torque = -jnp.sum(jnp.cross(nearest, forces, axis=0), (1, 2))
    return (on_spheres, jnp.concatenate([on_body, torque]))


def tile_forces(spheres, facets, tile_list):
    tiles_tri = facets.shape[1] // 128

    def advance_tile(carried, tile_code):
        forces, wrench = carried
        sphere_tile = tile_code // tiles_tri
        facet_tile = tile_code % tiles_tri
        sphere_part = lax.dynamic_slice_in_dim(spheres, sphere_tile * 128, 128, 1)
        facet_part = lax.dynamic_slice_in_dim(facets, facet_tile * 128, 128, 1)
        on_spheres, on_body = contact(sphere_part, facet_part)
        current = lax.dynamic_slice_in_dim(forces, sphere_tile * 128, 128, 1)
        forces = lax.dynamic_update_slice_in_dim(forces, current + on_spheres, sphere_tile * 128, 1)
        return ((forces, wrench + on_body), None)

    initial = (jnp.zeros((3, spheres.shape[1]), jnp.float32), jnp.zeros((6,), jnp.float32))
    (forces, wrench), unused = lax.scan(advance_tile, initial, tile_list)
    return (forces, wrench)


def sphere_forces(sphere_block):
    position = sphere_block[0:3]
    velocity = sphere_block[3:6]
    radius = sphere_block[6]
    width_all = sphere_block.shape[1]
    occupied = (radius > 0).astype(jnp.float32)
    coords = jnp.concatenate([position, radius[None]], 0)
    baseline = radius * radius - jnp.sum(position * position, 0)
    stacked = jnp.concatenate([position, velocity, jnp.ones((1, width_all), jnp.float32)], 0)
    row_block = 512

    def row_group(row_start):
        coords_rows = lax.dynamic_slice_in_dim(coords, row_start, row_block, 1)
        base_rows = lax.dynamic_slice_in_dim(baseline, row_start, row_block, 0)
        live_rows = lax.dynamic_slice_in_dim(occupied, row_start, row_block, 0)
        inner_products = lax.dot_general(
            coords_rows, coords, (((0,), (0,)), ((), ())), precision=lax.Precision.HIGHEST
        )
        intersection = jnp.maximum(
            base_rows[:, None] + baseline[None, :] + 2.0 * inner_products, 0.0
        )
        intersection = intersection * live_rows[:, None] * occupied[None, :]
        return lax.dot_general(
            stacked, intersection, (((1,), (1,)), ((), ())), precision=lax.Precision.HIGHEST
        )

    starts = jnp.arange(width_all // row_block, dtype=jnp.int32) * row_block
    grouped = lax.map(row_group, starts)
    weighted = jnp.transpose(grouped, (1, 0, 2)).reshape(7, width_all)
    totals = weighted[6]
    return stiff_pair * (totals * position - weighted[0:3]) - damp_pair * (
        totals * velocity - weighted[3:6]
    )


def advance(sphere_block, forces):
    position = sphere_block[0:3]
    velocity = sphere_block[3:6]
    radius = sphere_block[6]
    occupied = radius > 0
    masses = jnp.where(occupied, radius * radius * radius, 1.0)
    falling = jnp.array([0.0, 0.0, gravity], jnp.float32)
    acceleration = forces / masses[None] - falling[:, None]
    velocity_new = velocity + time_step * acceleration
    position_new = position + time_step * velocity_new
    result = jnp.concatenate([position_new, velocity_new, radius[None]], 0)
    return jnp.where(occupied[None], result, 0.0)


def bin_total(partial_row):
    return lax.psum(partial_row, "bin")


def general(sph_state, sph_dest, body_list, tile_codes, triangles):
    sectors = lax.axis_size("sector")
    bins = lax.axis_size("bin")
    ndevices = sectors * bins
    leaving = sph_state.shape[1]
    capacity = 2 * leaving // ndevices
    targets = sph_dest[:, 0]
    onehot = (targets[:, None] == jnp.arange(ndevices, dtype=jnp.int32)[None, :]).astype(jnp.int32)
    ranks = jnp.sum((jnp.cumsum(onehot, 0) - 1) * onehot, 1)
    columns = targets * capacity + ranks
    outgoing = jnp.zeros((7, ndevices * capacity), jnp.float32).at[:, columns].set(sph_state)
    outgoing = outgoing.reshape(7, sectors, bins, capacity)
    arrived = lax.all_to_all(
        lax.all_to_all(outgoing, "sector", split_axis=1, concat_axis=1, tiled=True),
        "bin",
        split_axis=2,
        concat_axis=2,
        tiled=True,
    )
    sphere_block = arrived.reshape(7, ndevices * capacity)
    width_all = sphere_block.shape[1]
    coords = jnp.concatenate([sphere_block[0:3], sphere_block[6:7]], 0)
    pair_total = sphere_forces(sphere_block)
    everyone = lax.all_gather(triangles, "sector", axis=1, tiled=True)
    wall_total = jnp.zeros((3, width_all), jnp.float32)
    partial_value = jnp.zeros((sectors, 6), jnp.float32)
    for slot_index in range(body_list.shape[1]):
        owner_body = body_list[0, slot_index]
        facets = lax.dynamic_index_in_dim(everyone, owner_body, 1, keepdims=False)
        on_spheres, on_body = tile_forces(coords, facets, tile_codes[0, slot_index])
        wall_total = wall_total + on_spheres
        selector = (jnp.arange(sectors, dtype=jnp.int32) == owner_body).astype(jnp.float32)
        partial_value = partial_value + selector[:, None] * on_body[None, :]
    own_row = lax.psum_scatter(partial_value, "sector", scatter_dimension=0, tiled=True)
    own_row = bin_total(own_row)
    new_block = advance(sphere_block, pair_total + wall_total)
    scaling = jnp.array([time_step / body_mass] * 3 + [time_step / body_inertia] * 3, jnp.float32)
    return (new_block, own_row * scaling[None, :])


def local(sph_state, sph_dest, body_list, tile_codes, triangles):
    sectors = lax.axis_size("sector")
    ndevices = sectors * lax.axis_size("bin")
    leaving = sph_state.shape[1]
    fits = 2 * leaving == 64 * ndevices and 16 * leaving == LANES * LANES and sectors & (sectors - 1) == 0
    chosen = fast if fits else general
    return chosen(sph_state, sph_dest, body_list, tile_codes, triangles)


def solution(mesh):
    return jax.shard_map(
        local,
        mesh=mesh,
        in_specs=(
            P(None, ("sector", "bin")),
            P(("sector", "bin"), None),
            P(("sector", "bin"), None),
            P(("sector", "bin"), None, None),
            P(None, "sector", "bin"),
        ),
        out_specs=(P(None, ("sector", "bin")), P("sector", None)),
        check_vma=False,
    )
```

```python
import functools

import jax
import jax.numpy as jnp
from jax import lax
from jax.experimental import pallas as pl
from jax.experimental.pallas import tpu as pltpu
from jax.sharding import PartitionSpec as P

stiff_pair = 50.0
damp_pair = 2.0
stiff_wall = 50.0
time_step = 0.01
gravity = 9.81
body_mass = 4.0
body_inertia = 40.0

LANES = 128
PAYLOAD = ((0, 3), (1, 4), (2, 5), (6, None))
PAIR_BLOCK = 1024
SPREAD = 2
WALL_ROWS = 64


def iota(shape, dim):
    return lax.broadcasted_iota(jnp.int32, shape, dim)


def split3(x):
    hi = x.astype(jnp.bfloat16).astype(jnp.float32)
    rest = x - hi
    mid = rest.astype(jnp.bfloat16).astype(jnp.float32)
    return hi, mid, rest - mid


def dot(a, b, contract=((1,), (0,))):
    return lax.dot_general(a, b, (contract, ((), ())), preferred_element_type=jnp.float32)


def pack_kernel(dest_ref, state_ref, out_ref):
    blocks = dest_ref.shape[0]
    ndevices = out_ref.shape[0] * LANES // (8 * 64)
    capacity = 64
    dest = dest_ref[...]
    upper = (iota((LANES, LANES), 0) <= iota((LANES, LANES), 1)).astype(jnp.bfloat16)
    named = [
        (dest[b : b + 1] == iota((ndevices, LANES), 0)).astype(jnp.float32) for b in range(blocks)
    ]
    counted = dot(jnp.concatenate(named, 0).astype(jnp.bfloat16), upper)
    before = jnp.full((ndevices, LANES), -1.0, jnp.float32)
    ranks = []
    for b in range(blocks):
        mine = counted[b * ndevices : (b + 1) * ndevices]
        ranks.append(jnp.sum(named[b] * (mine + before), 0, keepdims=True))
        before = before + jnp.broadcast_to(mine[:, LANES - 1 :], (ndevices, LANES))
    rank_row = jnp.concatenate(ranks, 1)
    dest_row = jnp.concatenate([dest[b : b + 1] for b in range(blocks)], 1)
    leaving = blocks * LANES
    chosen = dest_row == iota((ndevices, leaving), 0)
    slot = (iota((LANES, leaving), 0) % capacity).astype(jnp.float32)
    at_rank = (rank_row == slot).astype(jnp.float32).astype(jnp.bfloat16)
    groups = len(PAYLOAD)
    sources = [pair[half] for half in range(2) for pair in PAYLOAD if pair[half] is not None]
    rows = [
        jnp.where(chosen, part[source : source + 1], 0.0).astype(jnp.bfloat16)
        for part in split3(state_ref[...])
        for source in sources
    ]
    pieces = dot(jnp.concatenate(rows, 0), at_rank, ((1,), (1,)))
    height = len(sources) * ndevices
    out = (pieces[:height] + pieces[height : 2 * height]) + pieces[2 * height :]
    low = iota((ndevices, LANES), 1) < capacity
    for k, pair in enumerate(PAYLOAD):
        halves = []
        for source in pair:
            if source is None:
                halves.append(jnp.zeros((ndevices, LANES), jnp.float32))
            else:
                place = sources.index(source) * ndevices
                halves.append(out[place : place + ndevices])
        out_ref[pl.ds(k, ndevices, stride=groups), :] = jnp.where(low, halves[0], halves[1])


def quotient(code, size):
    power = size & (size - 1) == 0
    return lax.shift_right_logical(code, size.bit_length() - 1) if power else lax.div(code, size)


def remainder(code, size):
    return code & (size - 1) if size & (size - 1) == 0 else lax.rem(code, size)


def total_of(x):
    return jnp.sum(jnp.sum(x, 0, keepdims=True), 1, keepdims=True)


def state_tile(arrived_ref, tile):
    words = arrived_ref[8 * tile : 8 * tile + 8, :]
    swapped = pltpu.roll(pltpu.roll(words, 64, 1), 4, 0)
    same = (iota((8, LANES), 0) < 4) == (iota((8, LANES), 1) < 64)
    return jnp.where(same, words, swapped)


def facet_kernel(sectors, *refs):
    bodies_ref = refs[0]
    tri_refs = refs[1 : 1 + sectors]
    facet, raw, tri_sem = refs[1 + sectors :]
    entries = bodies_ref.shape[1]
    me = lax.axis_index("sector")

    def fetch(entry, source):
        return pltpu.make_async_copy(tri_refs[source], raw.at[entry], tri_sem.at[entry])

    for entry in range(entries):
        relative = bodies_ref[0, entry] ^ me
        for source in range(sectors):

            @pl.when(relative == source)
            def _():
                fetch(entry, source).start()

    for entry in range(entries):
        fetch(entry, 0).wait()
        corner = [raw[entry, i] for i in range(3)]
        one = [raw[entry, 3 + i] - corner[i] for i in range(3)]
        two = [raw[entry, 6 + i] - corner[i] for i in range(3)]
        d11 = one[0] * one[0] + one[1] * one[1] + one[2] * one[2]
        d12 = one[0] * two[0] + one[1] * two[1] + one[2] * two[2]
        d22 = two[0] * two[0] + two[1] * two[1] + two[2] * two[2]
        inverse = 1.0 / (d11 * d22 - d12 * d12)
        for i in range(3):
            facet[entry, i] = corner[i]
            facet[entry, 3 + i] = one[i]
            facet[entry, 6 + i] = two[i]
            facet[entry, 9 + i] = (d22 * one[i] - d12 * two[i]) * inverse
            facet[entry, 12 + i] = (d11 * two[i] - d12 * one[i]) * inverse


def sphere_side(state, row8):
    square = state * state
    level = square[3:4] - (square[0:1] + square[1:2] + square[2:3])
    other = jnp.where(state[3:4] > 0.0, level, -3.0e38)
    return level, jnp.where(
        row8 < 4, state, jnp.where(row8 == 4, 1.0, jnp.where(row8 == 5, other, jnp.where(row8 == 6, square[3:4], 0.0)))
    )


def wall_kernel(sectors, bins, *refs):
    bodies_ref, codes_ref, facet, arrived_ref, wrench_ref, force_ref, left = refs[:7]
    spread, place, gathered = refs[7:10]
    accs = refs[10:]
    entries = bodies_ref.shape[1]
    codes = codes_ref.shape[2]
    tiles_tri = facet.shape[2]
    tiles = arrived_ref.shape[0] // 8
    row8 = iota((8, LANES), 0)

    wanted = iota((48, 4 * LANES), 1) // LANES
    wanted = jnp.where(wanted == 3, 6, wanted)
    row = iota((48, 4 * LANES), 0)
    select = (row % 8 == wanted) & ((row // 8 == 0) | (row // 8 == 1) | (row // 8 == 3))
    select = select.astype(jnp.float32).astype(jnp.bfloat16)
    for tile in range(tiles):
        at = slice(tile * LANES, (tile + 1) * LANES)
        state = state_tile(arrived_ref, tile)
        jh, jm, jl = split3(sphere_side(state, row8)[1])
        left[at, 0:48] = jnp.transpose(jnp.concatenate([jh, jm, jh, jl, jh, jm], 0)).astype(jnp.bfloat16)
        for i in range(3):
            place[i, tile : tile + 1, :] = state[i : i + 1]
    for group in range(tiles // SPREAD):
        at = slice(group * SPREAD * LANES, (group + 1) * SPREAD * LANES)
        wide = dot(left[at, 0:48], select)
        for i in range(4):
            spread[i, at, :] = wide[:, i * LANES : (i + 1) * LANES]
    for acc in accs:
        acc[...] = jnp.zeros_like(acc)

    def one_tile(entry, number):
        code = codes_ref[0, entry, number]
        first = pl.multiple_of(quotient(code, tiles_tri) * LANES, LANES)
        facet_tile = remainder(code, tiles_tri)
        f = [facet[entry, i, pl.ds(facet_tile, 1), :] for i in range(15)]
        for part in range(LANES // WALL_ROWS):
            at = pl.ds(pl.multiple_of(first + part * WALL_ROWS, WALL_ROWS), WALL_ROWS)
            dx, dy, dz = spread[0, at, :] - f[0], spread[1, at, :] - f[1], spread[2, at, :] - f[2]
            beta = dx * f[9] + dy * f[10] + dz * f[11]
            gamma = dx * f[12] + dy * f[13] + dz * f[14]
            alpha = jnp.maximum(1.0 - beta - gamma, 0.0)
            beta = jnp.maximum(beta, 0.0)
            gamma = jnp.maximum(gamma, 0.0)
            scale = 1.0 / (alpha + beta + gamma)
            beta = beta * scale
            gamma = gamma * scale
            ox = dx - beta * f[3] - gamma * f[6]
            oy = dy - beta * f[4] - gamma * f[7]
            oz = dz - beta * f[5] - gamma * f[8]
            deep = jnp.maximum(spread[3, at, :] - (ox * ox + oy * oy + oz * oz), 0.0)
            accs[3 * entry][at, :] += deep * ox
            accs[3 * entry + 1][at, :] += deep * oy
            accs[3 * entry + 2][at, :] += deep * oz

    def step(number, carry):
        for entry in range(entries):
            one_tile(entry, number)
        return carry

    lax.fori_loop(0, codes, step, 0)

    ones = jnp.ones((16, 2 * LANES), jnp.bfloat16)

    def gather(tile, carry):
        at = pl.ds(pl.multiple_of(tile * LANES, LANES), LANES)
        for which in range(3 * entries):
            value = accs[which][at, :]
            if which % 2:
                row = jnp.sum(jnp.transpose(value), 0, keepdims=True)
            else:
                high = value.astype(jnp.bfloat16)
                low = (value - high.astype(jnp.float32)).astype(jnp.bfloat16)
                row = dot(ones, jnp.concatenate([high, low], 1), ((1,), (1,)))
            gathered[which, pl.ds(tile, 1), :] = row[0:1]
        return carry

    lax.fori_loop(0, tiles, gather, 0, unroll=16)
    x, y, z = place[0], place[1], place[2]
    owner = iota((sectors * bins, LANES), 0) // bins
    lane = iota((1, LANES), 1)
    out = jnp.zeros((sectors * bins, LANES), jnp.float32)
    whole = [0.0, 0.0, 0.0]
    for entry in range(entries):
        fx, fy, fz = (gathered[3 * entry + i] for i in range(3))
        parts = (fx, fy, fz, y * fz - z * fy, z * fx - x * fz, x * fy - y * fx)
        mine = jnp.zeros((1, LANES), jnp.float32)
        for i, part in enumerate(parts):
            scale = time_step / (body_mass if i < 3 else body_inertia)
            mine = jnp.where(lane == i, total_of(part) * scale, mine)
        out = out + jnp.where(owner == bodies_ref[0, entry], mine * (-stiff_wall), 0.0)
        whole = [whole[0] + fx, whole[1] + fy, whole[2] + fz]
    wrench_ref[...] = out
    for i in range(3):
        force_ref[i] = stiff_wall * whole[i]


def pair_kernel(arrived_ref, force_ref, left, out_hbm, right, moved, out_ref, out_sem):
    tiles = arrived_ref.shape[0] // 8
    blocks = tiles * LANES // PAIR_BLOCK
    row8 = iota((8, LANES), 0)
    for tile in range(tiles):
        at = slice(tile * LANES, (tile + 1) * LANES)
        state = state_tile(arrived_ref, tile)
        level = sphere_side(state, row8)[0]
        i_side = jnp.where(row8 < 4, 2.0 * state, jnp.where(row8 == 4, level, jnp.where(row8 == 5, 1.0, 0.0)))
        ih, im, il = split3(i_side)
        right[:, at] = jnp.concatenate([ih, ih, im, ih, il, im], 0).astype(jnp.bfloat16)
        value = jnp.where(row8 == 3, 1.0, state)
        moved[:, at] = jnp.concatenate(list(split3(value)) + [jnp.zeros((8, LANES), jnp.float32)], 0).astype(
            jnp.bfloat16
        )

    def block_of(ib, carry):
        columns = pl.ds(pl.multiple_of(ib * PAIR_BLOCK, PAIR_BLOCK), PAIR_BLOCK)
        mine = right[:, columns]
        total = jnp.zeros((32, PAIR_BLOCK), jnp.float32)
        for jb in range(blocks):
            rows = slice(jb * PAIR_BLOCK, (jb + 1) * PAIR_BLOCK)
            weight = jnp.maximum(dot(left[rows, 0:48], mine), 0.0)
            high = weight.astype(jnp.bfloat16)
            low = (weight - high.astype(jnp.float32)).astype(jnp.bfloat16)
            values = moved[:, rows]
            total = total + (dot(values, high) + dot(values, low))
        total = total[0:8] + total[8:16] + total[16:24]
        for part in range(PAIR_BLOCK // LANES):
            tile = ib * (PAIR_BLOCK // LANES) + part
            words = arrived_ref[pl.ds(pl.multiple_of(8 * tile, 8), 8), :]
            swapped = pltpu.roll(pltpu.roll(words, 64, 1), 4, 0)
            state = jnp.where((row8 < 4) == (iota((8, LANES), 1) < 64), words, swapped)
            moment = total[:, part * LANES : (part + 1) * LANES]
            differ = moment[3:4] * state - moment
            force = stiff_pair * differ - damp_pair * pltpu.roll(differ, 4, 0)
            for i in range(3):
                force = force + jnp.where(row8 == i, force_ref[i, pl.ds(tile, 1), :], 0.0)
            radius = jnp.broadcast_to(state[3:4], (8, LANES))
            live = radius > 0.0
            mass = jnp.where(live, radius * radius * radius, 1.0)
            falling = jnp.where(row8 == 6, gravity, 0.0)
            speed = state + time_step * (pltpu.roll(force, 4, 0) / mass - falling)
            place = state + time_step * pltpu.roll(speed, 4, 0)
            result = jnp.where(
                row8 < 3, place, jnp.where(row8 < 6, pltpu.roll(speed, 7, 0), pltpu.roll(state, 3, 0))
            )
            result = jnp.where(live, result, 0.0)
            out_ref[:, pl.ds(pl.multiple_of(tile * LANES, LANES), LANES)] = result[0:7]
        leave(ib).start()
        return carry

    def leave(ib):
        columns = pl.ds(pl.multiple_of(ib * PAIR_BLOCK, PAIR_BLOCK), PAIR_BLOCK)
        return pltpu.make_async_copy(out_ref.at[:, columns], out_hbm.at[:, columns], out_sem.at[ib])

    lax.fori_loop(0, blocks, block_of, 0)
    for ib in range(blocks):
        leave(ib).wait()


def whole_vmem():
    return pl.BlockSpec(memory_space=pltpu.VMEM)


def whole_smem():
    return pl.BlockSpec(memory_space=pltpu.SMEM)


def near(x):
    return pltpu.with_memory_space_constraint(x, pltpu.VMEM)


def fast(sph_state, sph_dest, body_list, tile_codes, triangles):
    sectors = lax.axis_size("sector")
    bins = lax.axis_size("bin")
    ndevices = sectors * bins
    leaving = sph_state.shape[1]
    slots = 2 * leaving
    words = 8 * slots // LANES
    block = triangles.reshape(triangles.shape[0], -1, LANES)
    outgoing = pl.pallas_call(
        pack_kernel,
        out_shape=pltpu.VMEM((words, LANES), jnp.float32),
        in_specs=[whole_vmem(), whole_vmem()],
        out_specs=whole_vmem(),
        name="pack",
    )(sph_dest.reshape(-1, LANES), sph_state)
    blocks = [block] + [
        lax.ppermute(block, "sector", [(i, i ^ step) for i in range(sectors)]) for step in range(1, sectors)
    ]
    outgoing = outgoing.reshape(ndevices, 1, words * LANES // ndevices)
    arrived = lax.all_to_all(outgoing, ("sector", "bin"), split_axis=0, concat_axis=0, tiled=True)
    arrived = arrived.reshape(words, LANES)
    entries = body_list.shape[1]
    column = pltpu.VMEM((slots, LANES), jnp.float32)
    tiles = slots // LANES
    facets = pl.pallas_call(
        functools.partial(facet_kernel, sectors),
        out_shape=pltpu.VMEM((entries, 15) + block.shape[1:], jnp.float32),
        in_specs=[whole_smem(), pl.BlockSpec(memory_space=pltpu.HBM)] + [whole_vmem()] * (sectors - 1),
        out_specs=whole_vmem(),
        scratch_shapes=[pltpu.VMEM((entries,) + block.shape, jnp.float32), pltpu.SemaphoreType.DMA((entries,))],
        name="facet",
    )(body_list, blocks[0], *[near(other) for other in blocks[1:]])
    wrench, force, left = pl.pallas_call(
        functools.partial(wall_kernel, sectors, bins),
        out_shape=[
            pltpu.VMEM((ndevices, LANES), jnp.float32),
            pltpu.VMEM((3, tiles, LANES), jnp.float32),
            pltpu.VMEM((slots, LANES), jnp.bfloat16),
        ],
        in_specs=[whole_smem(), whole_smem()] + [whole_vmem()] * 2,
        out_specs=[whole_vmem()] * 3,
        scratch_shapes=[
            pltpu.VMEM((4, slots, LANES), jnp.float32),
            pltpu.VMEM((3, tiles, LANES), jnp.float32),
            pltpu.VMEM((3 * entries, tiles, LANES), jnp.float32),
        ]
        + [column] * (3 * entries),
        name="wall",
    )(body_list, tile_codes, near(facets), near(arrived))
    shared = lax.all_to_all(
        wrench.reshape(ndevices, 1, LANES), ("sector", "bin"), split_axis=0, concat_axis=0, tiled=True
    )
    new_block = pl.pallas_call(
        pair_kernel,
        out_shape=jax.ShapeDtypeStruct((7, slots), jnp.float32),
        in_specs=[whole_vmem()] * 3,
        out_specs=pl.BlockSpec(memory_space=pltpu.HBM),
        scratch_shapes=[
            pltpu.VMEM((48, slots), jnp.bfloat16),
            pltpu.VMEM((32, slots), jnp.bfloat16),
            pltpu.VMEM((7, slots), jnp.float32),
            pltpu.SemaphoreType.DMA((slots // PAIR_BLOCK,)),
        ],
        name="pair",
    )(near(arrived), near(force), near(left))
    kick = jnp.sum(shared[:, 0, :6], 0, keepdims=True)
    return new_block, kick


def contact(spheres, facets):
    centre = spheres[0:3]
    radius = spheres[3]
    corner = facets[0:3]
    edge_one = facets[3:6] - corner
    edge_two = facets[6:9] - corner
    square_one = jnp.sum(edge_one * edge_one, 0)
    square_two = jnp.sum(edge_two * edge_two, 0)
    cross_term = jnp.sum(edge_one * edge_two, 0)
    inverse = 1.0 / (square_one * square_two - cross_term * cross_term)
    relative = centre[:, :, None] - corner[:, None, :]
    along_one = jnp.sum(relative * edge_one[:, None, :], 0)
    along_two = jnp.sum(relative * edge_two[:, None, :], 0)
    weight_b = (square_two * along_one - cross_term * along_two) * inverse
    weight_c = (square_one * along_two - cross_term * along_one) * inverse
    weight_a = jnp.maximum(1.0 - weight_b - weight_c, 0.0)
    weight_b = jnp.maximum(weight_b, 0.0)
    weight_c = jnp.maximum(weight_c, 0.0)
    totals = weight_a + weight_b + weight_c
    weight_b = weight_b / totals
    weight_c = weight_c / totals
    nearest = (
        corner[:, None, :]
        + weight_b[None] * edge_one[:, None, :]
        + weight_c[None] * edge_two[:, None, :]
    )
    offset = centre[:, :, None] - nearest
    squared = jnp.sum(offset * offset, 0)
    strength = stiff_wall * jnp.maximum(radius[:, None] * radius[:, None] - squared, 0.0)
    forces = strength[None] * offset
    on_spheres = jnp.sum(forces, 2)
    on_body = -jnp.sum(forces, (1, 2))
    torque = -jnp.sum(jnp.cross(nearest, forces, axis=0), (1, 2))
    return (on_spheres, jnp.concatenate([on_body, torque]))


def tile_forces(spheres, facets, tile_list):
    tiles_tri = facets.shape[1] // 128

    def advance_tile(carried, tile_code):
        forces, wrench = carried
        sphere_tile = tile_code // tiles_tri
        facet_tile = tile_code % tiles_tri
        sphere_part = lax.dynamic_slice_in_dim(spheres, sphere_tile * 128, 128, 1)
        facet_part = lax.dynamic_slice_in_dim(facets, facet_tile * 128, 128, 1)
        on_spheres, on_body = contact(sphere_part, facet_part)
        current = lax.dynamic_slice_in_dim(forces, sphere_tile * 128, 128, 1)
        forces = lax.dynamic_update_slice_in_dim(forces, current + on_spheres, sphere_tile * 128, 1)
        return ((forces, wrench + on_body), None)

    initial = (jnp.zeros((3, spheres.shape[1]), jnp.float32), jnp.zeros((6,), jnp.float32))
    (forces, wrench), unused = lax.scan(advance_tile, initial, tile_list)
    return (forces, wrench)


def sphere_forces(sphere_block):
    position = sphere_block[0:3]
    velocity = sphere_block[3:6]
    radius = sphere_block[6]
    width_all = sphere_block.shape[1]
    occupied = (radius > 0).astype(jnp.float32)
    coords = jnp.concatenate([position, radius[None]], 0)
    baseline = radius * radius - jnp.sum(position * position, 0)
    stacked = jnp.concatenate([position, velocity, jnp.ones((1, width_all), jnp.float32)], 0)
    row_block = 512

    def row_group(row_start):
        coords_rows = lax.dynamic_slice_in_dim(coords, row_start, row_block, 1)
        base_rows = lax.dynamic_slice_in_dim(baseline, row_start, row_block, 0)
        live_rows = lax.dynamic_slice_in_dim(occupied, row_start, row_block, 0)
        inner_products = lax.dot_general(
            coords_rows, coords, (((0,), (0,)), ((), ())), precision=lax.Precision.HIGHEST
        )
        intersection = jnp.maximum(
            base_rows[:, None] + baseline[None, :] + 2.0 * inner_products, 0.0
        )
        intersection = intersection * live_rows[:, None] * occupied[None, :]
        return lax.dot_general(
            stacked, intersection, (((1,), (1,)), ((), ())), precision=lax.Precision.HIGHEST
        )

    starts = jnp.arange(width_all // row_block, dtype=jnp.int32) * row_block
    grouped = lax.map(row_group, starts)
    weighted = jnp.transpose(grouped, (1, 0, 2)).reshape(7, width_all)
    totals = weighted[6]
    return stiff_pair * (totals * position - weighted[0:3]) - damp_pair * (
        totals * velocity - weighted[3:6]
    )


def advance(sphere_block, forces):
    position = sphere_block[0:3]
    velocity = sphere_block[3:6]
    radius = sphere_block[6]
    occupied = radius > 0
    masses = jnp.where(occupied, radius * radius * radius, 1.0)
    falling = jnp.array([0.0, 0.0, gravity], jnp.float32)
    acceleration = forces / masses[None] - falling[:, None]
    velocity_new = velocity + time_step * acceleration
    position_new = position + time_step * velocity_new
    result = jnp.concatenate([position_new, velocity_new, radius[None]], 0)
    return jnp.where(occupied[None], result, 0.0)


def bin_total(partial_row):
    return lax.psum(partial_row, "bin")


def general(sph_state, sph_dest, body_list, tile_codes, triangles):
    sectors = lax.axis_size("sector")
    bins = lax.axis_size("bin")
    ndevices = sectors * bins
    leaving = sph_state.shape[1]
    capacity = 2 * leaving // ndevices
    targets = sph_dest[:, 0]
    onehot = (targets[:, None] == jnp.arange(ndevices, dtype=jnp.int32)[None, :]).astype(jnp.int32)
    ranks = jnp.sum((jnp.cumsum(onehot, 0) - 1) * onehot, 1)
    columns = targets * capacity + ranks
    outgoing = jnp.zeros((7, ndevices * capacity), jnp.float32).at[:, columns].set(sph_state)
    outgoing = outgoing.reshape(7, sectors, bins, capacity)
    arrived = lax.all_to_all(
        lax.all_to_all(outgoing, "sector", split_axis=1, concat_axis=1, tiled=True),
        "bin",
        split_axis=2,
        concat_axis=2,
        tiled=True,
    )
    sphere_block = arrived.reshape(7, ndevices * capacity)
    width_all = sphere_block.shape[1]
    coords = jnp.concatenate([sphere_block[0:3], sphere_block[6:7]], 0)
    pair_total = sphere_forces(sphere_block)
    everyone = lax.all_gather(triangles, "sector", axis=1, tiled=True)
    wall_total = jnp.zeros((3, width_all), jnp.float32)
    partial_value = jnp.zeros((sectors, 6), jnp.float32)
    for slot_index in range(body_list.shape[1]):
        owner_body = body_list[0, slot_index]
        facets = lax.dynamic_index_in_dim(everyone, owner_body, 1, keepdims=False)
        on_spheres, on_body = tile_forces(coords, facets, tile_codes[0, slot_index])
        wall_total = wall_total + on_spheres
        selector = (jnp.arange(sectors, dtype=jnp.int32) == owner_body).astype(jnp.float32)
        partial_value = partial_value + selector[:, None] * on_body[None, :]
    own_row = lax.psum_scatter(partial_value, "sector", scatter_dimension=0, tiled=True)
    own_row = bin_total(own_row)
    new_block = advance(sphere_block, pair_total + wall_total)
    scaling = jnp.array([time_step / body_mass] * 3 + [time_step / body_inertia] * 3, jnp.float32)
    return (new_block, own_row * scaling[None, :])


def local(sph_state, sph_dest, body_list, tile_codes, triangles):
    sectors = lax.axis_size("sector")
    ndevices = sectors * lax.axis_size("bin")
    leaving = sph_state.shape[1]
    fits = 2 * leaving == 64 * ndevices and 16 * leaving == LANES * LANES and sectors & (sectors - 1) == 0
    chosen = fast if fits else general
    return chosen(sph_state, sph_dest, body_list, tile_codes, triangles)


def solution(mesh):
    return jax.shard_map(
        local,
        mesh=mesh,
        in_specs=(
            P(None, ("sector", "bin")),
            P(("sector", "bin"), None),
            P(("sector", "bin"), None),
            P(("sector", "bin"), None, None),
            P(None, "sector", "bin"),
        ),
        out_specs=(P(None, ("sector", "bin")), P("sector", None)),
        check_vma=False,
    )
```
